512 devices in a mesh: atom: 64 (over y, z_lo, x), wave: 8 (over z_hi, core).
Axes of the slice: x: 4, y: 4, z: 16 (z_hi: 4, z_lo: 4; z = z_hi * 4 + z_lo), core: 2. Of those that a mesh axis runs over, the one named last changes fastest.
Arguments:
- features: bfloat16 [131072, 256], P('atom'), may hold values from -6 to 6
- coords: int32 [3, 131072], P(None, 'atom'), may hold values from 0 to 65535
- miller: int32 [3, 4096], P(None, 'wave'), may hold values from -8 to 8
- filter_weights: float32 [4096, 256], P('wave'), may hold values from -6 to 6
- norm_gain: float32 [256], replicated, may hold values from 0.1 to 1.9
- w_in: bfloat16 [256, 256], replicated, may hold values from -0.375 to 0.375
- w_out: bfloat16 [256, 256], replicated, may hold values from -0.375 to 0.375
Outputs:
- updated_features: bfloat16 [131072, 256], P(('atom', 'wave'))
The draws below stay inside these ranges and needn't reach their ends.
All inputs are finite; a program needn't handle non-finite values.
Results may differ from the reference program's by a relative error of at most 0.013.
Values may be sent and summed in bfloat16 or wider, within the bound.
No kernel may reach another device: no remote copies, remote signals or barrier semaphores. Data moves between devices by JAX's collectives and lax.ppermute only.
A program may use at most 64 MiB of HBM per device.

```python
import math
import jax
import jax.numpy as jnp
from jax import lax

F = 256
FH = 256
K = 4096
KMAX = 8
ATOMS = 131072


def set_ends(entries, stream_key, least, high):
    longest = entries.shape.index(max(entries.shape))
    spots = []
    for shift in (0, 1):
        where = [jax.random.randint(jax.random.fold_in(stream_key, axis), (), 0, length) for axis, length in enumerate(entries.shape)]
        where[longest] = (where[longest] + shift) % entries.shape[longest]
        spots.append(tuple(where))
    return entries.at[spots[0]].set(least).at[spots[1]].set(high)


def block_scale(rng, dims, split, least, top_value):
    factor_of = 1.0
    for position, shards_of in split:
        heights = jax.random.uniform(jax.random.fold_in(jax.random.fold_in(rng, 6), position), (shards_of,), jnp.float32, least / len(split), top_value / len(split))
        factor_of = factor_of * jnp.repeat(jnp.exp(heights), dims[position] // shards_of).reshape((-1,) + (1,) * (len(dims) - 1 - position))
    return factor_of


def noise(own_key, shape, scale, bound, pieces=(), held_as=jnp.bfloat16):
    level = block_scale(own_key, shape, pieces, -0.22, 0.18) if pieces else 1.0
    entries = jax.random.normal(own_key, shape, jnp.float32) * scale * level
    return jnp.minimum(jnp.maximum(entries, -bound), bound).astype(held_as)


def setup_inputs(seed: int = 0) -> dict:
    keys = jax.random.split(jax.random.key(seed), 8)
    features = noise(keys[0], (ATOMS, F), 1.0, 6.0, ((0, 64),))
    coords = set_ends(jax.random.randint(keys[1], (3, ATOMS), 0, 65536), jax.random.fold_in(keys[1], 1), 0, 65535).astype(jnp.int32)
    miller = set_ends(jax.random.randint(keys[2], (3, K), -KMAX, KMAX + 1), jax.random.fold_in(keys[2], 1), -KMAX, KMAX).astype(jnp.int32)
    filter_weights = noise(keys[3], (K, F), 1.0, 6.0, ((0, 8),), jnp.float32)
    norm_gain = jnp.clip(1.0 + 0.18 * jax.random.normal(keys[4], (F,), jnp.float32), 0.1, 1.9)
    w_in = noise(keys[5], (F, FH), F ** -0.5, 0.375)
    w_out = noise(keys[6], (FH, F), FH ** -0.5, 0.375)
    return dict(features=features, coords=coords, miller=miller, filter_weights=filter_weights, norm_gain=norm_gain, w_in=w_in, w_out=w_out)


def phase_tables(miller_block, coords):
    steps = miller_block[0][:, None] * coords[0][None, :]
    steps = steps + miller_block[1][:, None] * coords[1][None, :]
    steps = steps + miller_block[2][:, None] * coords[2][None, :]
    steps = jnp.mod(steps, 65536)
    angles = steps.astype(jnp.float32) * (2.0 * math.pi / 65536.0)
    tables = jnp.stack([jnp.cos(angles), jnp.sin(angles)], axis=1).astype(jnp.bfloat16)
    return tables.reshape(tables.shape[0] * 2, tables.shape[2])

def filter_factors(factors, weights):
    power = lax.optimization_barrier(jnp.mean(factors * factors, axis=(1, 2), keepdims=True))
    scaled = factors / jnp.sqrt(power + 1e-05)
    return (scaled * weights[:, None, :]).astype(jnp.bfloat16)

def reference(features, coords, miller, filter_weights, norm_gain, w_in, w_out):
    width = features.shape[1]
    block = math.gcd(K, 512)
    miller_blocks = miller.reshape(3, K // block, block).transpose(1, 0, 2)
    weight_blocks = filter_weights.reshape(K // block, block, width)

    def step_block(carry, inputs):
        miller_block, weight_block = inputs
        tables = phase_tables(miller_block, coords)
        factors = jnp.dot(tables, features, preferred_element_type=jnp.float32).reshape(block, 2, width)
        filtered = filter_factors(factors, weight_block)
        added = lax.dot_general(tables, filtered.reshape(block * 2, width), (((0,), (0,)), ((), ())), preferred_element_type=jnp.float32)
        return (carry + added, None)
    message, _ = lax.scan(step_block, jnp.zeros((features.shape[0], width), jnp.float32), (miller_blocks, weight_blocks))
    updated = features.astype(jnp.float32) + message / math.sqrt(K)
    normed = (updated / jnp.sqrt(lax.optimization_barrier(jnp.mean(updated * updated, axis=1, keepdims=True)) + 1e-06) * norm_gain).astype(jnp.bfloat16)
    hidden = jax.nn.silu(jnp.dot(normed, w_in, preferred_element_type=jnp.float32)).astype(jnp.bfloat16)
    return (updated + jnp.dot(hidden, w_out, preferred_element_type=jnp.float32)).astype(jnp.bfloat16)
```

```python
import itertools
import math

import jax
import jax.numpy as jnp
import numpy as np
from jax import lax
from jax.experimental import pallas as pl
from jax.experimental.pallas import tpu as pltpu
from jax.sharding import PartitionSpec as P

K = 4096
KMAX = 8
SIDE = 2 * KMAX + 1
PLANE = SIDE * SIDE
HALF = PLANE // 2
STRIP = 24
SHARDS = 8
POINTS = 320
PLANES = 16
LAYERS = 4
OWN = POINTS // (PLANES * LAYERS)
ROWS = 2 * POINTS
F = 256
TILE = 512
AXES = ("atom", "wave")
BOTH = (((1,), (0,)), ((), ()))
OUTER = (((0,), (0,)), ((), ()))


def device(y, z_lo, x, z_hi, core):
    return (((y * 4 + z_lo) * 4 + x) * 4 + z_hi) * 2 + core


FOUR = range(4)
TWO = range(2)
GROUPS_XY = [
    [device(y, l, x, h, c) for y in FOUR for x in FOUR] for l in FOUR for h in FOUR for c in TWO
]
GROUPS_LO = [
    [device(y, l, x, h, c) for l in FOUR] for y in FOUR for x in FOUR for h in FOUR for c in TWO
]
GROUPS_Z = [
    [device(y, l, x, h, c) for h in FOUR for l in FOUR] for y in FOUR for x in FOUR for c in TWO
]
SWAP = [
    (device(y, l, x, h, c), device(y, l, x, h, 1 - c))
    for y, l, x, h, c in itertools.product(FOUR, FOUR, FOUR, FOUR, TWO)
]


def wavevector(shard, point):
    if point < PLANE:
        return point // SIDE - KMAX, point % SIDE - KMAX, shard + 1
    strip = shard * STRIP + point - PLANE
    if point - PLANE >= STRIP or strip > HALF:
        return None
    return (strip + HALF) // SIDE - KMAX, (strip + HALF) % SIDE - KMAX, 0


def row_steps(shard):
    steps = np.zeros((8, ROWS), np.float32)
    for row in range(ROWS):
        chunk, part, own = row // (2 * OWN), row % (2 * OWN) // OWN, row % OWN
        vector = wavevector(shard, chunk * OWN + own)
        if vector is None:
            steps[6, row] = -0.25
            continue
        steps[0:3, row] = vector
        steps[3:6, row] = vector
        steps[6, row] = -0.25 * part
    return steps


def split_coords(coords):
    high = (coords >> 8).astype(jnp.float32) * (1.0 / 256.0)
    low = (coords & 255).astype(jnp.float32) * (1.0 / 65536.0)
    ones = jnp.ones((2, coords.shape[1]), jnp.float32)
    return jnp.concatenate([high, low, ones], axis=0).astype(jnp.bfloat16)


def cosine_coefficients():
    nodes = 0.125 + 0.125 * np.cos(np.pi * (np.arange(400) + 0.5) / 400)
    fit = np.polynomial.chebyshev.Chebyshev.fit(
        nodes, np.cos(2 * np.pi * np.sqrt(nodes)), 6, domain=[0, 0.25]
    )
    return [float(c) for c in fit.convert(kind=np.polynomial.Polynomial).coef]


COSINE = cosine_coefficients()


def cosine_of_turns(turns):
    left = turns - jnp.round(turns)
    square = left * left
    total = jnp.full_like(square, COSINE[-1])
    for c in COSINE[-2::-1]:
        total = total * square + c
    return total


def factors_kernel(place_ref, steps_ref, coords_ref, features_ref, out_ref, tables, total):
    tile = pl.program_id(0)
    parts = split_coords(coords_ref[...])
    steps = steps_ref[0].astype(jnp.bfloat16)
    block = 128
    for start in range(0, ROWS, block):
        turns = lax.dot_general(
            steps[:, start : start + block], parts, OUTER, preferred_element_type=jnp.float32
        )
        tables[start : start + block, :] = cosine_of_turns(turns).astype(jnp.bfloat16)
    added = jnp.dot(tables[...], features_ref[...], preferred_element_type=jnp.float32)

    @pl.when(tile == 0)
    def _():
        total[...] = added

    @pl.when(tile > 0)
    def _():
        total[...] += added

    @pl.when(tile == pl.num_programs(0) - 1)
    def _():
        out_ref[...] = total[...].astype(jnp.bfloat16)


def partial_factors(place, steps, coords, features):
    atoms = features.shape[0]
    return pl.pallas_call(
        factors_kernel,
        out_shape=jax.ShapeDtypeStruct((ROWS, F), jnp.bfloat16),
        grid_spec=pltpu.PrefetchScalarGridSpec(
            num_scalar_prefetch=1,
            grid=(atoms // TILE,),
            in_specs=[
                pl.BlockSpec((1, 8, ROWS), lambda t, place: (place[0], 0, 0)),
                pl.BlockSpec((3, TILE), lambda t, place: (0, t)),
                pl.BlockSpec((TILE, F), lambda t, place: (t, 0)),
            ],
            out_specs=pl.BlockSpec((ROWS, F), lambda t, place: (0, 0)),
            scratch_shapes=[
                pltpu.VMEM((ROWS, TILE), jnp.bfloat16),
                pltpu.VMEM((ROWS, F), jnp.float32),
            ],
        ),
        cost_estimate=pl.CostEstimate(
            flops=2 * ROWS * atoms * F, bytes_accessed=atoms * F * 2, transcendentals=0
        ),
        name="factors",
    )(place, steps, coords, features)


WROWS = 32


def weights_kernel(place_ref, miller_ref, weights_ref, own_ref, other_ref):
    core, plane, layer = place_ref[1], place_ref[2], place_ref[3]
    m0, m1, m2 = miller_ref[0:1, :], miller_ref[1:2, :], miller_ref[2:3, :]
    flat = (m0 + KMAX) * SIDE + (m1 + KMAX)
    flip = (m2 < 0) | ((m2 == 0) & (flat < HALF))
    flat = jnp.where(flip, 2 * HALF - flat, flat)
    strip = flat - HALF
    strip_shard = (
        (strip >= STRIP).astype(jnp.int32)
        + (strip >= 2 * STRIP).astype(jnp.int32)
        + (strip >= 3 * STRIP).astype(jnp.int32)
        + (strip >= 4 * STRIP).astype(jnp.int32)
        + (strip >= 5 * STRIP).astype(jnp.int32)
        + (strip >= 6 * STRIP).astype(jnp.int32)
    )
    shard = jnp.where(m2 == 0, strip_shard, jnp.abs(m2) - 1)
    point = jnp.where(m2 == 0, PLANE + strip - strip_shard * STRIP, flat)
    spot = shard * POINTS + point
    row = lax.broadcasted_iota(jnp.int32, (WROWS, miller_ref.shape[1]), 0)
    high = (
        (row >= OWN).astype(jnp.int32)
        + (row >= 2 * OWN).astype(jnp.int32)
        + (row >= 3 * OWN).astype(jnp.int32)
    )
    base = (plane * LAYERS + layer) * OWN + row - high * OWN
    weights = weights_ref[...]
    upper = weights.astype(jnp.bfloat16)
    lower = (weights - upper.astype(jnp.float32)).astype(jnp.bfloat16)
    for held, out_ref in ((core, own_ref), (1 - core, other_ref)):
        wanted = (high * 2 + held) * POINTS + base
        match = jnp.where((wanted == spot) & (row < 4 * OWN), 1.0, 0.0).astype(jnp.bfloat16)
        summed = jnp.dot(match, upper, preferred_element_type=jnp.float32)
        summed += jnp.dot(match, lower, preferred_element_type=jnp.float32)
        out_ref[...] = summed.astype(jnp.bfloat16)


def grid_weights(place, miller, weights):
    shape = jax.ShapeDtypeStruct((WROWS, F), jnp.bfloat16)
    return pl.pallas_call(
        weights_kernel,
        out_shape=(shape, shape),
        in_specs=[
            pl.BlockSpec(memory_space=pltpu.SMEM),
            pl.BlockSpec(memory_space=pltpu.VMEM),
            pl.BlockSpec(memory_space=pltpu.VMEM),
        ],
        out_specs=(pl.BlockSpec(memory_space=pltpu.VMEM),) * 2,
        cost_estimate=pl.CostEstimate(
            flops=8 * WROWS * 512 * F, bytes_accessed=512 * F * 4, transcendentals=0
        ),
        name="grid_weights",
    )(place, miller, weights)


def plane_sum_kernel(arrived_ref, out_ref, total):
    total[...] = jnp.sum(arrived_ref[...].astype(jnp.float32), axis=0)
    for layer in range(LAYERS):
        rows = total[layer * 2 * OWN : (layer + 1) * 2 * OWN, :]
        out_ref[layer] = rows.astype(jnp.bfloat16)


def plane_sum(arrived):
    rows = 2 * OWN * LAYERS
    return pl.pallas_call(
        plane_sum_kernel,
        out_shape=jax.ShapeDtypeStruct((LAYERS, 2 * OWN, F), jnp.bfloat16),
        in_specs=[pl.BlockSpec(memory_space=pltpu.VMEM)],
        out_specs=pl.BlockSpec(memory_space=pltpu.VMEM),
        scratch_shapes=[pltpu.VMEM((rows, F), jnp.float32)],
        name="plane_sum",
    )(arrived)


PACKED = 32


def scale_kernel(arrived_ref, own_ref, other_ref, out_ref, packed):
    total = jnp.sum(arrived_ref[...].astype(jnp.float32), axis=0)
    cosines, sines = total[:OWN], total[OWN:]
    power = jnp.sum(cosines * cosines + sines * sines, axis=1, keepdims=True) * (1.0 / (2 * F))
    scale = 1.0 / jnp.sqrt(power + 1e-05)
    packed[0:OWN, :] = cosines * scale
    packed[OWN : 2 * OWN, :] = sines * scale
    weights = own_ref[...].astype(jnp.float32) + other_ref[...].astype(jnp.float32)
    packed[2 * OWN : 6 * OWN, :] = weights[: 4 * OWN]
    packed[6 * OWN :, :] = jnp.zeros((PACKED - 6 * OWN, F), jnp.float32)
    sent = packed[...].astype(jnp.bfloat16)
    for peer in range(PLANES):
        out_ref[peer] = sent


def scale_factors(arrived, own, other):
    return pl.pallas_call(
        scale_kernel,
        out_shape=jax.ShapeDtypeStruct((PLANES, PACKED, F), jnp.bfloat16),
        in_specs=[pl.BlockSpec(memory_space=pltpu.VMEM)] * 3,
        out_specs=pl.BlockSpec(memory_space=pltpu.VMEM),
        scratch_shapes=[pltpu.VMEM((PACKED, F), jnp.float32)],
        name="scale_factors",
    )(arrived, own, other)


COLUMN = 2 * OWN * PLANES


def column_picks():
    factor = np.zeros((COLUMN, PLANES * PACKED), np.float32)
    weight = np.zeros((COLUMN, PLANES * PACKED), np.float32)
    for row in range(COLUMN):
        rank, spot = row // (2 * OWN), row % (2 * OWN)
        high, low = rank // LAYERS, rank % LAYERS
        factor[row, rank * PACKED + spot] = 1
        for source in range(4):
            at = (source * LAYERS + low) * PACKED + 2 * OWN + high * OWN + spot % OWN
            weight[row, at] = 1
    return factor, weight


def filter_kernel(arrived_ref, factor_ref, weight_ref, out_ref):
    arrived = arrived_ref[...]
    factors = jnp.dot(factor_ref[...], arrived, preferred_element_type=jnp.float32)
    weights = jnp.dot(weight_ref[...], arrived, preferred_element_type=jnp.float32)
    filtered = (factors * weights).astype(jnp.bfloat16)
    for peer in range(PLANES):
        out_ref[peer] = filtered


def filter_column(arrived, factor, weight):
    return pl.pallas_call(
        filter_kernel,
        out_shape=jax.ShapeDtypeStruct((PLANES, COLUMN, F), jnp.bfloat16),
        in_specs=[pl.BlockSpec(memory_space=pltpu.VMEM)] * 3,
        out_specs=pl.BlockSpec(memory_space=pltpu.VMEM),
        name="filter_column",
    )(arrived, factor, weight)


ALL_ROWS = COLUMN * PLANES


def tables_kernel(place_ref, steps_ref, coords_ref, out_ref):
    parts = split_coords(coords_ref[...])
    steps = steps_ref[0].astype(jnp.bfloat16)
    block = 128
    for start in range(0, TILE, block):
        turns = lax.dot_general(
            parts[:, start : start + block], steps, OUTER, preferred_element_type=jnp.float32
        )
        out_ref[start : start + block, :] = cosine_of_turns(turns).astype(jnp.bfloat16)


def message_tables(place, steps, coords):
    width = 512
    return pl.pallas_call(
        tables_kernel,
        out_shape=jax.ShapeDtypeStruct((TILE, ALL_ROWS), jnp.bfloat16),
        grid_spec=pltpu.PrefetchScalarGridSpec(
            num_scalar_prefetch=1,
            grid=(ALL_ROWS // width,),
            in_specs=[
                pl.BlockSpec((1, 8, width), lambda t, place: (place[1], 0, t)),
                pl.BlockSpec((3, TILE), lambda t, place: (0, place[4])),
            ],
            out_specs=pl.BlockSpec((TILE, width), lambda t, place: (0, t)),
        ),
        cost_estimate=pl.CostEstimate(
            flops=16 * TILE * ALL_ROWS, bytes_accessed=TILE * ALL_ROWS * 2, transcendentals=0
        ),
        name="message_tables",
    )(place, steps, coords)


def message_kernel(place_ref, tables_ref, filtered_ref, own_ref, other_ref, total):
    core = place_ref[1]
    total[...] = jnp.dot(tables_ref[...], filtered_ref[...], preferred_element_type=jnp.float32)
    half = TILE // 2
    own_ref[...] = total[pl.ds(pl.multiple_of(core * half, half), half), :]
    other = total[pl.ds(pl.multiple_of((1 - core) * half, half), half), :]
    other_ref[...] = other.astype(jnp.bfloat16)


def message_parts(place, tables, filtered):
    half = TILE // 2
    return pl.pallas_call(
        message_kernel,
        out_shape=(
            jax.ShapeDtypeStruct((half, F), jnp.float32),
            jax.ShapeDtypeStruct((half, F), jnp.bfloat16),
        ),
        in_specs=[
            pl.BlockSpec(memory_space=pltpu.SMEM),
            pl.BlockSpec(memory_space=pltpu.VMEM),
            pl.BlockSpec(memory_space=pltpu.VMEM),
        ],
        out_specs=(pl.BlockSpec(memory_space=pltpu.VMEM),) * 2,
        scratch_shapes=[pltpu.VMEM((TILE, F), jnp.float32)],
        name="message",
    )(place, tables, filtered)


def update_kernel(
    place_ref, features_ref, own_ref, other_ref, gain_ref, w_in_ref, w_out_ref, out_ref
):
    message = own_ref[...] + other_ref[...].astype(jnp.float32)
    updated = features_ref[...].astype(jnp.float32) + message * (1.0 / math.sqrt(K))
    power = jnp.mean(updated * updated, axis=1, keepdims=True)
    normed = (updated / jnp.sqrt(power + 1e-06) * gain_ref[...]).astype(jnp.bfloat16)
    hidden = jnp.dot(normed, w_in_ref[...], preferred_element_type=jnp.float32)
    hidden = (hidden / (1.0 + jnp.exp(-hidden))).astype(jnp.bfloat16)
    added = jnp.dot(hidden, w_out_ref[...], preferred_element_type=jnp.float32)
    out_ref[...] = (updated + added).astype(jnp.bfloat16)


def update(place, features, own, other, gain, w_in, w_out):
    half = TILE // 2
    return pl.pallas_call(
        update_kernel,
        out_shape=jax.ShapeDtypeStruct((half, F), jnp.bfloat16),
        grid_spec=pltpu.PrefetchScalarGridSpec(
            num_scalar_prefetch=1,
            grid=(1,),
            in_specs=[
                pl.BlockSpec((half, F), lambda t, place: (place[0], 0)),
                pl.BlockSpec((half, F), lambda t, place: (0, 0)),
                pl.BlockSpec((half, F), lambda t, place: (0, 0)),
                pl.BlockSpec((1, F), lambda t, place: (0, 0)),
                pl.BlockSpec((F, F), lambda t, place: (0, 0)),
                pl.BlockSpec((F, F), lambda t, place: (0, 0)),
            ],
            out_specs=pl.BlockSpec((half, F), lambda t, place: (0, 0)),
        ),
        name="update",
    )(place, features, own, other, gain, w_in, w_out)


def exchange(pieces, groups):
    return lax.all_to_all(
        pieces, AXES, split_axis=0, concat_axis=0, tiled=True, axis_index_groups=groups
    )


def shard_steps():
    return np.stack([row_steps(shard) for shard in range(SHARDS)])


def column_steps(steps):
    by_core = steps.reshape(4, 2, 8, PLANES, 2 * OWN * LAYERS)
    return by_core.transpose(1, 2, 3, 0, 4).reshape(2, 8, ALL_ROWS)


STEPS = shard_steps()
COLUMN_STEPS = column_steps(STEPS)
PICK_FACTOR, PICK_WEIGHT = column_picks()


def on_device(features, coords, miller, filter_weights, norm_gain, w_in, w_out):
    atom, wave = lax.axis_index("atom"), lax.axis_index("wave")
    core, high = wave % 2, wave // 2
    plane = atom // 16 * 4 + atom % 4
    layer = atom // 4 % 4
    place = jnp.stack([wave, core, plane, layer, high]).astype(jnp.int32)

    factors = partial_factors(place, jnp.asarray(STEPS), coords, features)
    factors, coords, miller = lax.optimization_barrier((factors, coords, miller))
    arrived = exchange(factors.reshape(PLANES, 2 * OWN * LAYERS, F), GROUPS_XY)
    own_weights, other_weights = grid_weights(place, miller, filter_weights)
    other_weights = lax.ppermute(other_weights, AXES, SWAP)
    tables = message_tables(place, jnp.asarray(COLUMN_STEPS), coords)
    shares = exchange(plane_sum(arrived), GROUPS_LO)
    packed = exchange(scale_factors(shares, own_weights, other_weights), GROUPS_Z)
    filtered = filter_column(
        packed.reshape(PLANES * PACKED, F),
        jnp.asarray(PICK_FACTOR, jnp.bfloat16),
        jnp.asarray(PICK_WEIGHT, jnp.bfloat16),
    )
    filtered = exchange(filtered, GROUPS_XY).reshape(ALL_ROWS, F)
    own, other = message_parts(place, tables, filtered)
    other = lax.ppermute(other, AXES, SWAP)
    return update(place, features, own, other, norm_gain.reshape(1, F), w_in, w_out)


def solution(mesh):
    in_specs = (P("atom", None), P(None, "atom"), P(None, "wave"), P("wave", None), P(), P(), P())
    out_specs = P(("atom", "wave"), None)
    return jax.shard_map(
        on_device, mesh=mesh, in_specs=in_specs, out_specs=out_specs, check_vma=False
    )
```

```python
import itertools
import math

import jax
import jax.numpy as jnp
import numpy as np
from jax import lax
from jax.experimental import pallas as pl
from jax.experimental.pallas import tpu as pltpu
from jax.sharding import PartitionSpec as P

K = 4096
KMAX = 8
SIDE = 2 * KMAX + 1
PLANE = SIDE * SIDE
HALF = PLANE // 2
STRIP = 24
SHARDS = 8
POINTS = 320
PLANES = 16
OWN = POINTS // PLANES
CHUNK = 2 * OWN
PADDED = 24
ROWS = 2 * POINTS
F = 256
TILE = 512
AXES = ("atom", "wave")
BOTH = (((1,), (0,)), ((), ()))
OUTER = (((0,), (0,)), ((), ()))


def device(y, z_lo, x, z_hi, core):
    return (((y * 4 + z_lo) * 4 + x) * 4 + z_hi) * 2 + core


FOUR = range(4)
TWO = range(2)
GROUPS_XY = [
    [device(y, l, x, h, c) for y in FOUR for x in FOUR] for l in FOUR for h in FOUR for c in TWO
]
GROUPS_LO = [
    [device(y, l, x, h, c) for l in FOUR] for y in FOUR for x in FOUR for h in FOUR for c in TWO
]
GROUPS_HI = [
    [device(y, l, x, h, c) for h in FOUR] for y in FOUR for x in FOUR for l in FOUR for c in TWO
]
SWAP = [
    (device(y, l, x, h, c), device(y, l, x, h, 1 - c))
    for y, l, x, h, c in itertools.product(FOUR, FOUR, FOUR, FOUR, TWO)
]


def wavevector(shard, point):
    if point < PLANE:
        return point // SIDE - KMAX, point % SIDE - KMAX, shard + 1
    strip = shard * STRIP + point - PLANE
    if point - PLANE >= STRIP or strip > HALF:
        return None
    return (strip + HALF) // SIDE - KMAX, (strip + HALF) % SIDE - KMAX, 0


def row_steps(shard):
    steps = np.zeros((8, ROWS), np.float32)
    for row in range(ROWS):
        chunk, part, own = row // CHUNK, row % CHUNK // OWN, row % OWN
        vector = wavevector(shard, chunk * OWN + own)
        if vector is None:
            steps[6, row] = -0.25
            continue
        steps[0:3, row] = vector
        steps[3:6, row] = vector
        steps[6, row] = -0.25 * part
    return steps


def split_coords(coords):
    high = (coords >> 8).astype(jnp.float32) * (1.0 / 256.0)
    low = (coords & 255).astype(jnp.float32) * (1.0 / 65536.0)
    ones = jnp.ones((2, coords.shape[1]), jnp.float32)
    return jnp.concatenate([high, low, ones], axis=0).astype(jnp.bfloat16)


def cosine_coefficients():
    nodes = 0.125 + 0.125 * np.cos(np.pi * (np.arange(400) + 0.5) / 400)
    fit = np.polynomial.chebyshev.Chebyshev.fit(
        nodes, np.cos(2 * np.pi * np.sqrt(nodes)), 6, domain=[0, 0.25]
    )
    return [float(c) for c in fit.convert(kind=np.polynomial.Polynomial).coef]


COSINE = cosine_coefficients()


def cosine_of_turns(turns):
    left = turns - jnp.round(turns)
    square = left * left
    total = jnp.full_like(square, COSINE[-1])
    for c in COSINE[-2::-1]:
        total = total * square + c
    return total


def factors_kernel(place_ref, steps_ref, coords_ref, features_ref, out_ref, tables, total):
    tile = pl.program_id(0)
    parts = split_coords(coords_ref[...])
    steps = steps_ref[0].astype(jnp.bfloat16)
    block = 128
    for start in range(0, ROWS, block):
        turns = lax.dot_general(
            steps[:, start : start + block], parts, OUTER, preferred_element_type=jnp.float32
        )
        tables[start : start + block, :] = cosine_of_turns(turns).astype(jnp.bfloat16)
    added = jnp.dot(tables[...], features_ref[...], preferred_element_type=jnp.float32)

    @pl.when(tile == 0)
    def _():
        total[...] = added

    @pl.when(tile > 0)
    def _():
        total[...] += added

    @pl.when(tile == pl.num_programs(0) - 1)
    def _():
        out_ref[...] = total[...].astype(jnp.bfloat16)


def partial_factors(place, steps, coords, features):
    atoms = features.shape[0]
    return pl.pallas_call(
        factors_kernel,
        out_shape=jax.ShapeDtypeStruct((ROWS, F), jnp.bfloat16),
        grid_spec=pltpu.PrefetchScalarGridSpec(
            num_scalar_prefetch=1,
            grid=(atoms // TILE,),
            in_specs=[
                pl.BlockSpec((1, 8, ROWS), lambda t, place: (place[0], 0, 0)),
                pl.BlockSpec((3, TILE), lambda t, place: (0, t)),
                pl.BlockSpec((TILE, F), lambda t, place: (t, 0)),
            ],
            out_specs=pl.BlockSpec((ROWS, F), lambda t, place: (0, 0)),
            scratch_shapes=[
                pltpu.VMEM((ROWS, TILE), jnp.bfloat16),
                pltpu.VMEM((ROWS, F), jnp.float32),
            ],
        ),
        compiler_params=pltpu.CompilerParams(vmem_limit_bytes=16 << 20),
        cost_estimate=pl.CostEstimate(
            flops=2 * ROWS * atoms * F, bytes_accessed=atoms * F * 2, transcendentals=0
        ),
        name="factors",
    )(place, steps, coords, features)


def weights_kernel(place_ref, miller_ref, weights_ref, out_ref):
    plane = place_ref[4] * 4 + place_ref[3]
    m0, m1, m2 = miller_ref[0:1, :], miller_ref[1:2, :], miller_ref[2:3, :]
    flat = (m0 + KMAX) * SIDE + (m1 + KMAX)
    flip = (m2 < 0) | ((m2 == 0) & (flat < HALF))
    flat = jnp.where(flip, 2 * HALF - flat, flat)
    strip = flat - HALF
    strip_shard = (strip >= STRIP).astype(jnp.int32)
    for bound in range(2, 7):
        strip_shard += (strip >= bound * STRIP).astype(jnp.int32)
    shard = jnp.where(m2 == 0, strip_shard, jnp.abs(m2) - 1)
    point = jnp.where(m2 == 0, PLANE + strip - strip_shard * STRIP, flat)
    spot = shard * POINTS + point
    row = lax.broadcasted_iota(jnp.int32, (SHARDS * PADDED, miller_ref.shape[1]), 0)
    owner = (row * 171) >> 12
    own = row - owner * PADDED
    wanted = owner * POINTS + plane * OWN + own
    match = jnp.where((wanted == spot) & (own < OWN), 1.0, 0.0).astype(jnp.bfloat16)
    weights = weights_ref[...]
    upper = weights.astype(jnp.bfloat16)
    lower = (weights - upper.astype(jnp.float32)).astype(jnp.bfloat16)
    summed = jnp.dot(match, upper, preferred_element_type=jnp.float32)
    summed += jnp.dot(match, lower, preferred_element_type=jnp.float32)
    out_ref[...] = summed.astype(jnp.bfloat16)


def grid_weights(place, miller, weights):
    return pl.pallas_call(
        weights_kernel,
        out_shape=jax.ShapeDtypeStruct((SHARDS * PADDED, F), jnp.bfloat16),
        in_specs=[
            pl.BlockSpec(memory_space=pltpu.SMEM),
            pl.BlockSpec(memory_space=pltpu.VMEM),
            pl.BlockSpec(memory_space=pltpu.VMEM),
        ],
        out_specs=pl.BlockSpec(memory_space=pltpu.VMEM),
        compiler_params=pltpu.CompilerParams(vmem_limit_bytes=8 << 20),
        cost_estimate=pl.CostEstimate(
            flops=4 * SHARDS * PADDED * 512 * F, bytes_accessed=512 * F * 4, transcendentals=0
        ),
        name="grid_weights",
    )(place, miller, weights)


def plane_sum_kernel(arrived_ref, out_ref):
    total = jnp.sum(arrived_ref[...].astype(jnp.float32), axis=0).astype(jnp.bfloat16)
    for peer in range(4):
        out_ref[peer] = total


def plane_sum(arrived):
    return pl.pallas_call(
        plane_sum_kernel,
        out_shape=jax.ShapeDtypeStruct((4, CHUNK, F), jnp.bfloat16),
        in_specs=[pl.BlockSpec(memory_space=pltpu.VMEM)],
        out_specs=pl.BlockSpec(memory_space=pltpu.VMEM),
        compiler_params=pltpu.CompilerParams(vmem_limit_bytes=8 << 20),
        name="plane_sum",
    )(arrived)


def filter_kernel(arrived_ref, weights_ref, out_ref, filtered):
    total = jnp.sum(arrived_ref[...].astype(jnp.float32), axis=0)
    cosines, sines = total[:OWN], total[OWN:]
    power = jnp.sum(cosines * cosines + sines * sines, axis=1, keepdims=True) * (1.0 / (2 * F))
    weights = jnp.sum(weights_ref[...].astype(jnp.float32), axis=0)[:OWN]
    scaled = weights * (1.0 / jnp.sqrt(power + 1e-05))
    filtered[:OWN, :] = cosines * scaled
    filtered[OWN:, :] = sines * scaled
    sent = filtered[...].astype(jnp.bfloat16)
    for peer in range(4):
        out_ref[peer] = sent


def filter_factors(arrived, weights):
    return pl.pallas_call(
        filter_kernel,
        out_shape=jax.ShapeDtypeStruct((4, CHUNK, F), jnp.bfloat16),
        in_specs=[pl.BlockSpec(memory_space=pltpu.VMEM)] * 2,
        out_specs=pl.BlockSpec(memory_space=pltpu.VMEM),
        scratch_shapes=[pltpu.VMEM((CHUNK, F), jnp.float32)],
        compiler_params=pltpu.CompilerParams(vmem_limit_bytes=8 << 20),
        name="filter_factors",
    )(arrived, weights)


COLUMN = 4 * CHUNK


def copies_kernel(column_ref, out_ref):
    column = column_ref[...]
    for peer in range(PLANES):
        out_ref[peer] = column


def copies(column):
    return pl.pallas_call(
        copies_kernel,
        out_shape=jax.ShapeDtypeStruct((PLANES, COLUMN, F), jnp.bfloat16),
        in_specs=[pl.BlockSpec(memory_space=pltpu.VMEM)],
        out_specs=pl.BlockSpec(memory_space=pltpu.VMEM),
        compiler_params=pltpu.CompilerParams(vmem_limit_bytes=8 << 20),
        name="copies",
    )(column)


ALL_ROWS = COLUMN * PLANES


def tables_kernel(place_ref, steps_ref, coords_ref, out_ref):
    parts = split_coords(coords_ref[...])
    steps = steps_ref[0].astype(jnp.bfloat16)
    block = 128
    for start in range(0, TILE, block):
        turns = lax.dot_general(
            parts[:, start : start + block], steps, OUTER, preferred_element_type=jnp.float32
        )
        out_ref[start : start + block, :] = cosine_of_turns(turns).astype(jnp.bfloat16)


def message_tables(place, steps, coords):
    width = 512
    return pl.pallas_call(
        tables_kernel,
        out_shape=jax.ShapeDtypeStruct((TILE, ALL_ROWS), jnp.bfloat16),
        grid_spec=pltpu.PrefetchScalarGridSpec(
            num_scalar_prefetch=1,
            grid=(ALL_ROWS // width,),
            in_specs=[
                pl.BlockSpec((1, 8, width), lambda t, place: (place[1], 0, t)),
                pl.BlockSpec((3, TILE), lambda t, place: (0, place[2])),
            ],
            out_specs=pl.BlockSpec((TILE, width), lambda t, place: (0, t)),
        ),
        compiler_params=pltpu.CompilerParams(vmem_limit_bytes=16 << 20),
        cost_estimate=pl.CostEstimate(
            flops=16 * TILE * ALL_ROWS, bytes_accessed=TILE * ALL_ROWS * 2, transcendentals=0
        ),
        name="message_tables",
    )(place, steps, coords)


def message_kernel(place_ref, tables_ref, filtered_ref, own_ref, other_ref, total):
    core = place_ref[1]
    total[...] = jnp.dot(tables_ref[...], filtered_ref[...], preferred_element_type=jnp.float32)
    half = TILE // 2
    own_ref[...] = total[pl.ds(pl.multiple_of(core * half, half), half), :]
    other = total[pl.ds(pl.multiple_of((1 - core) * half, half), half), :]
    other_ref[...] = other.astype(jnp.bfloat16)


def message_parts(place, tables, filtered):
    half = TILE // 2
    return pl.pallas_call(
        message_kernel,
        out_shape=(
            jax.ShapeDtypeStruct((half, F), jnp.float32),
            jax.ShapeDtypeStruct((half, F), jnp.bfloat16),
        ),
        in_specs=[
            pl.BlockSpec(memory_space=pltpu.SMEM),
            pl.BlockSpec(memory_space=pltpu.VMEM),
            pl.BlockSpec(memory_space=pltpu.VMEM),
        ],
        out_specs=(pl.BlockSpec(memory_space=pltpu.VMEM),) * 2,
        scratch_shapes=[pltpu.VMEM((TILE, F), jnp.float32)],
        compiler_params=pltpu.CompilerParams(vmem_limit_bytes=16 << 20),
        name="message",
    )(place, tables, filtered)


def update_kernel(
    place_ref, features_ref, own_ref, other_ref, gain_ref, w_in_ref, w_out_ref, out_ref
):
    message = own_ref[...] + other_ref[...].astype(jnp.float32)
    updated = features_ref[...].astype(jnp.float32) + message * (1.0 / math.sqrt(K))
    power = jnp.mean(updated * updated, axis=1, keepdims=True)
    normed = (updated / jnp.sqrt(power + 1e-06) * gain_ref[...]).astype(jnp.bfloat16)
    hidden = jnp.dot(normed, w_in_ref[...], preferred_element_type=jnp.float32)
    hidden = (hidden / (1.0 + jnp.exp(-hidden))).astype(jnp.bfloat16)
    added = jnp.dot(hidden, w_out_ref[...], preferred_element_type=jnp.float32)
    out_ref[...] = (updated + added).astype(jnp.bfloat16)


def update(place, features, own, other, gain, w_in, w_out):
    half = TILE // 2
    return pl.pallas_call(
        update_kernel,
        out_shape=jax.ShapeDtypeStruct((half, F), jnp.bfloat16),
        grid_spec=pltpu.PrefetchScalarGridSpec(
            num_scalar_prefetch=1,
            grid=(1,),
            in_specs=[
                pl.BlockSpec((half, F), lambda t, place: (place[0], 0)),
                pl.BlockSpec((half, F), lambda t, place: (0, 0)),
                pl.BlockSpec((half, F), lambda t, place: (0, 0)),
                pl.BlockSpec((1, F), lambda t, place: (0, 0)),
                pl.BlockSpec((F, F), lambda t, place: (0, 0)),
                pl.BlockSpec((F, F), lambda t, place: (0, 0)),
            ],
            out_specs=pl.BlockSpec((half, F), lambda t, place: (0, 0)),
        ),
        compiler_params=pltpu.CompilerParams(vmem_limit_bytes=8 << 20),
        name="update",
    )(place, features, own, other, gain, w_in, w_out)


def exchange(pieces, groups):
    return lax.all_to_all(
        pieces, AXES, split_axis=0, concat_axis=0, tiled=True, axis_index_groups=groups
    )


def shard_steps():
    return np.stack([row_steps(shard) for shard in range(SHARDS)])


def column_steps(steps):
    by_core = steps.reshape(4, 2, 8, PLANES, CHUNK)
    return by_core.transpose(1, 2, 3, 0, 4).reshape(2, 8, ALL_ROWS)


STEPS = shard_steps()
COLUMN_STEPS = column_steps(STEPS)


def on_device(features, coords, miller, filter_weights, norm_gain, w_in, w_out):
    number = lax.axis_index("atom") * 8 + lax.axis_index("wave")
    place = number // np.array([1, 1, 2, 8, 128], np.int32) % np.array([8, 2, 4, 4, 4], np.int32)

    factors = partial_factors(place, jnp.asarray(STEPS), coords, features)
    factors, coords, miller = lax.optimization_barrier((factors, coords, miller))
    arrived = exchange(factors.reshape(PLANES, CHUNK, F), GROUPS_XY)
    weights = grid_weights(place, miller, filter_weights).reshape(SHARDS, PADDED, F)
    weights = lax.all_to_all(weights, "wave", split_axis=0, concat_axis=0, tiled=True)
    tables = message_tables(place, jnp.asarray(COLUMN_STEPS), coords)
    shares = exchange(plane_sum(arrived), GROUPS_LO)
    filtered = exchange(filter_factors(shares, weights), GROUPS_HI)
    filtered = exchange(copies(filtered.reshape(COLUMN, F)), GROUPS_XY).reshape(ALL_ROWS, F)
    own, other = message_parts(place, tables, filtered)
    other = lax.ppermute(other, AXES, SWAP)
    return update(place, features, own, other, norm_gain.reshape(1, F), w_in, w_out)


def solution(mesh):
    in_specs = (P("atom", None), P(None, "atom"), P(None, "wave"), P("wave", None), P(), P(), P())
    out_specs = P(("atom", "wave"), None)
    return jax.shard_map(
        on_device, mesh=mesh, in_specs=in_specs, out_specs=out_specs, check_vma=False
    )
```

```python
import itertools
import math

import jax
import jax.numpy as jnp
import numpy as np
from jax import lax
from jax.experimental import pallas as pl
from jax.experimental.pallas import tpu as pltpu
from jax.sharding import PartitionSpec as P

K = 4096
KMAX = 8
SIDE = 2 * KMAX + 1
PLANE = SIDE * SIDE
HALF = PLANE // 2
STRIP = 24
SHARDS = 8
POINTS = 320
PLANES = 16
OWN = POINTS // PLANES
CHUNK = 2 * OWN
ROWS = 2 * POINTS
F = 256
TILE = 512
AXES = ("atom", "wave")
BOTH = (((1,), (0,)), ((), ()))
OUTER = (((0,), (0,)), ((), ()))


def device(y, z_lo, x, z_hi, core):
    return (((y * 4 + z_lo) * 4 + x) * 4 + z_hi) * 2 + core


FOUR = range(4)
TWO = range(2)
GROUPS_XY = [
    [device(y, l, x, h, c) for y in FOUR for x in FOUR] for l in FOUR for h in FOUR for c in TWO
]
GROUPS_LO = [
    [device(y, l, x, h, c) for l in FOUR] for y in FOUR for x in FOUR for h in FOUR for c in TWO
]
GROUPS_HI = [
    [device(y, l, x, h, c) for h in FOUR] for y in FOUR for x in FOUR for l in FOUR for c in TWO
]
SWAP = [
    (device(y, l, x, h, c), device(y, l, x, h, 1 - c))
    for y, l, x, h, c in itertools.product(FOUR, FOUR, FOUR, FOUR, TWO)
]


def wavevector(shard, point):
    if point < PLANE:
        return point // SIDE - KMAX, point % SIDE - KMAX, shard + 1
    strip = shard * STRIP + point - PLANE
    if point - PLANE >= STRIP or strip > HALF:
        return None
    return (strip + HALF) // SIDE - KMAX, (strip + HALF) % SIDE - KMAX, 0


def row_steps(shard):
    steps = np.zeros((8, ROWS), np.float32)
    for row in range(ROWS):
        chunk, part, own = row // CHUNK, row % CHUNK // OWN, row % OWN
        vector = wavevector(shard, chunk * OWN + own)
        if vector is None:
            steps[6, row] = -0.25
            continue
        steps[0:3, row] = vector
        steps[3:6, row] = vector
        steps[6, row] = -0.25 * part
    return steps


def split_coords(coords):
    high = (coords >> 8).astype(jnp.float32) * (1.0 / 256.0)
    low = (coords & 255).astype(jnp.float32) * (1.0 / 65536.0)
    ones = jnp.ones((2, coords.shape[1]), jnp.float32)
    return jnp.concatenate([high, low, ones], axis=0).astype(jnp.bfloat16)


def cosine_coefficients():
    nodes = 0.125 + 0.125 * np.cos(np.pi * (np.arange(400) + 0.5) / 400)
    fit = np.polynomial.chebyshev.Chebyshev.fit(
        nodes, np.cos(2 * np.pi * np.sqrt(nodes)), 6, domain=[0, 0.25]
    )
    return [float(c) for c in fit.convert(kind=np.polynomial.Polynomial).coef]


COSINE = cosine_coefficients()


def cosine_of_turns(turns):
    left = turns - jnp.round(turns)
    square = left * left
    total = jnp.full_like(square, COSINE[-1])
    for c in COSINE[-2::-1]:
        total = total * square + c
    return total


def factors_kernel(place_ref, steps_ref, coords_ref, features_ref, out_ref, tables, total):
    tile = pl.program_id(0)
    parts = split_coords(coords_ref[...])
    steps = steps_ref[0].astype(jnp.bfloat16)
    block = 128
    for start in range(0, ROWS, block):
        turns = lax.dot_general(
            steps[:, start : start + block], parts, OUTER, preferred_element_type=jnp.float32
        )
        tables[start : start + block, :] = cosine_of_turns(turns).astype(jnp.bfloat16)
    added = jnp.dot(tables[...], features_ref[...], preferred_element_type=jnp.float32)

    @pl.when(tile == 0)
    def _():
        total[...] = added

    @pl.when(tile > 0)
    def _():
        total[...] += added

    @pl.when(tile == pl.num_programs(0) - 1)
    def _():
        out_ref[...] = total[...].astype(jnp.bfloat16)


def partial_factors(place, steps, coords, features):
    atoms = features.shape[0]
    return pl.pallas_call(
        factors_kernel,
        out_shape=jax.ShapeDtypeStruct((ROWS, F), jnp.bfloat16),
        grid_spec=pltpu.PrefetchScalarGridSpec(
            num_scalar_prefetch=1,
            grid=(atoms // TILE,),
            in_specs=[
                pl.BlockSpec((1, 8, ROWS), lambda t, place: (place[0], 0, 0)),
                pl.BlockSpec((3, TILE), lambda t, place: (0, t)),
                pl.BlockSpec((TILE, F), lambda t, place: (t, 0)),
            ],
            out_specs=pl.BlockSpec((ROWS, F), lambda t, place: (0, 0)),
            scratch_shapes=[
                pltpu.VMEM((ROWS, TILE), jnp.bfloat16),
                pltpu.VMEM((ROWS, F), jnp.float32),
            ],
        ),
        cost_estimate=pl.CostEstimate(
            flops=2 * ROWS * atoms * F, bytes_accessed=atoms * F * 2, transcendentals=0
        ),
        name="factors",
    )(place, steps, coords, features)


SPOTS = 4 * OWN


def weights_kernel(place_ref, miller_ref, weights_ref, own_ref, other_ref):
    core, plane = place_ref[1], place_ref[4] * 4 + place_ref[3]
    m0, m1, m2 = miller_ref[0:1, :], miller_ref[1:2, :], miller_ref[2:3, :]
    flat = (m0 + KMAX) * SIDE + (m1 + KMAX)
    flip = (m2 < 0) | ((m2 == 0) & (flat < HALF))
    flat = jnp.where(flip, 2 * HALF - flat, flat)
    strip = flat - HALF
    strip_shard = (strip >= STRIP).astype(jnp.int32)
    for bound in range(2, 7):
        strip_shard += (strip >= bound * STRIP).astype(jnp.int32)
    shard = jnp.where(m2 == 0, strip_shard, jnp.abs(m2) - 1)
    point = jnp.where(m2 == 0, PLANE + strip - strip_shard * STRIP, flat)
    spot = shard * POINTS + point
    row = lax.broadcasted_iota(jnp.int32, (SPOTS, miller_ref.shape[1]), 0)
    high = (row >= OWN).astype(jnp.int32)
    for bound in range(2, 4):
        high += (row >= bound * OWN).astype(jnp.int32)
    base = plane * OWN + row - high * OWN
    weights = weights_ref[...]
    upper = weights.astype(jnp.bfloat16)
    lower = (weights - upper.astype(jnp.float32)).astype(jnp.bfloat16)
    for held, out_ref in ((core, own_ref), (1 - core, other_ref)):
        wanted = (high * 2 + held) * POINTS + base
        match = jnp.where(wanted == spot, 1.0, 0.0).astype(jnp.bfloat16)
        summed = jnp.dot(match, upper, preferred_element_type=jnp.float32)
        summed += jnp.dot(match, lower, preferred_element_type=jnp.float32)
        out_ref[...] = summed.astype(jnp.bfloat16)


def grid_weights(place, miller, weights):
    shape = jax.ShapeDtypeStruct((SPOTS, F), jnp.bfloat16)
    return pl.pallas_call(
        weights_kernel,
        out_shape=(shape, shape),
        in_specs=[
            pl.BlockSpec(memory_space=pltpu.SMEM),
            pl.BlockSpec(memory_space=pltpu.VMEM),
            pl.BlockSpec(memory_space=pltpu.VMEM),
        ],
        out_specs=(pl.BlockSpec(memory_space=pltpu.VMEM),) * 2,
        compiler_params=pltpu.CompilerParams(vmem_limit_bytes=8 << 20),
        cost_estimate=pl.CostEstimate(
            flops=8 * SPOTS * 512 * F, bytes_accessed=512 * F * 4, transcendentals=0
        ),
        name="grid_weights",
    )(place, miller, weights)


def plane_sum_kernel(arrived_ref, out_ref):
    total = jnp.sum(arrived_ref[...].astype(jnp.float32), axis=0).astype(jnp.bfloat16)
    for peer in range(4):
        out_ref[peer] = total


def plane_sum(arrived):
    return pl.pallas_call(
        plane_sum_kernel,
        out_shape=jax.ShapeDtypeStruct((4, CHUNK, F), jnp.bfloat16),
        in_specs=[pl.BlockSpec(memory_space=pltpu.VMEM)],
        out_specs=pl.BlockSpec(memory_space=pltpu.VMEM),
        compiler_params=pltpu.CompilerParams(vmem_limit_bytes=8 << 20),
        name="plane_sum",
    )(arrived)


PACKED = CHUNK + SPOTS


def scale_kernel(arrived_ref, own_ref, other_ref, out_ref, packed):
    total = jnp.sum(arrived_ref[...].astype(jnp.float32), axis=0)
    cosines, sines = total[:OWN], total[OWN:]
    power = jnp.sum(cosines * cosines + sines * sines, axis=1, keepdims=True) * (1.0 / (2 * F))
    scale = 1.0 / jnp.sqrt(power + 1e-05)
    packed[:OWN, :] = cosines * scale
    packed[OWN:CHUNK, :] = sines * scale
    packed[CHUNK:, :] = own_ref[...].astype(jnp.float32) + other_ref[...].astype(jnp.float32)
    sent = packed[...].astype(jnp.bfloat16)
    for peer in range(4):
        out_ref[peer] = sent


def scale_factors(arrived, own, other):
    return pl.pallas_call(
        scale_kernel,
        out_shape=jax.ShapeDtypeStruct((4, PACKED, F), jnp.bfloat16),
        in_specs=[pl.BlockSpec(memory_space=pltpu.VMEM)] * 3,
        out_specs=pl.BlockSpec(memory_space=pltpu.VMEM),
        scratch_shapes=[pltpu.VMEM((PACKED, F), jnp.float32)],
        compiler_params=pltpu.CompilerParams(vmem_limit_bytes=8 << 20),
        name="scale_factors",
    )(arrived, own, other)


COLUMN = 4 * CHUNK


def filter_kernel(arrived_ref, out_ref, filtered):
    weights = jnp.sum(arrived_ref[:, CHUNK:, :].astype(jnp.float32), axis=0)
    for high in range(4):
        weight = weights[high * OWN : (high + 1) * OWN]
        factors = arrived_ref[high, :CHUNK, :].astype(jnp.float32)
        filtered[high * CHUNK : high * CHUNK + OWN, :] = factors[:OWN] * weight
        filtered[high * CHUNK + OWN : (high + 1) * CHUNK, :] = factors[OWN:] * weight
    column = filtered[...].astype(jnp.bfloat16)
    for peer in range(PLANES):
        out_ref[peer] = column


def filter_column(arrived):
    return pl.pallas_call(
        filter_kernel,
        out_shape=jax.ShapeDtypeStruct((PLANES, COLUMN, F), jnp.bfloat16),
        in_specs=[pl.BlockSpec(memory_space=pltpu.VMEM)],
        out_specs=pl.BlockSpec(memory_space=pltpu.VMEM),
        scratch_shapes=[pltpu.VMEM((COLUMN, F), jnp.float32)],
        compiler_params=pltpu.CompilerParams(vmem_limit_bytes=8 << 20),
        name="filter_column",
    )(arrived)


ALL_ROWS = COLUMN * PLANES


def tables_kernel(place_ref, steps_ref, coords_ref, out_ref):
    parts = split_coords(coords_ref[...])
    steps = steps_ref[0].astype(jnp.bfloat16)
    block = 128
    for start in range(0, TILE, block):
        turns = lax.dot_general(
            parts[:, start : start + block], steps, OUTER, preferred_element_type=jnp.float32
        )
        out_ref[start : start + block, :] = cosine_of_turns(turns).astype(jnp.bfloat16)


def message_tables(place, steps, coords):
    width = 512
    return pl.pallas_call(
        tables_kernel,
        out_shape=jax.ShapeDtypeStruct((TILE, ALL_ROWS), jnp.bfloat16),
        grid_spec=pltpu.PrefetchScalarGridSpec(
            num_scalar_prefetch=1,
            grid=(ALL_ROWS // width,),
            in_specs=[
                pl.BlockSpec((1, 8, width), lambda t, place: (place[1], 0, t)),
                pl.BlockSpec((3, TILE), lambda t, place: (0, place[2])),
            ],
            out_specs=pl.BlockSpec((TILE, width), lambda t, place: (0, t)),
        ),
        compiler_params=pltpu.CompilerParams(vmem_limit_bytes=16 << 20),
        cost_estimate=pl.CostEstimate(
            flops=16 * TILE * ALL_ROWS, bytes_accessed=TILE * ALL_ROWS * 2, transcendentals=0
        ),
        name="message_tables",
    )(place, steps, coords)


def message_kernel(place_ref, tables_ref, filtered_ref, own_ref, other_ref, total):
    core = place_ref[1]
    total[...] = jnp.dot(tables_ref[...], filtered_ref[...], preferred_element_type=jnp.float32)
    half = TILE // 2
    own_ref[...] = total[pl.ds(pl.multiple_of(core * half, half), half), :]
    other = total[pl.ds(pl.multiple_of((1 - core) * half, half), half), :]
    other_ref[...] = other.astype(jnp.bfloat16)


def message_parts(place, tables, filtered):
    half = TILE // 2
    return pl.pallas_call(
        message_kernel,
        out_shape=(
            jax.ShapeDtypeStruct((half, F), jnp.float32),
            jax.ShapeDtypeStruct((half, F), jnp.bfloat16),
        ),
        in_specs=[
            pl.BlockSpec(memory_space=pltpu.SMEM),
            pl.BlockSpec(memory_space=pltpu.VMEM),
            pl.BlockSpec(memory_space=pltpu.VMEM),
        ],
        out_specs=(pl.BlockSpec(memory_space=pltpu.VMEM),) * 2,
        scratch_shapes=[pltpu.VMEM((TILE, F), jnp.float32)],
        compiler_params=pltpu.CompilerParams(vmem_limit_bytes=16 << 20),
        name="message",
    )(place, tables, filtered)


def update_kernel(
    place_ref, features_ref, own_ref, other_ref, gain_ref, w_in_ref, w_out_ref, out_ref
):
    message = own_ref[...] + other_ref[...].astype(jnp.float32)
    updated = features_ref[...].astype(jnp.float32) + message * (1.0 / math.sqrt(K))
    power = jnp.mean(updated * updated, axis=1, keepdims=True)
    normed = (updated / jnp.sqrt(power + 1e-06) * gain_ref[...]).astype(jnp.bfloat16)
    hidden = jnp.dot(normed, w_in_ref[...], preferred_element_type=jnp.float32)
    hidden = (hidden / (1.0 + jnp.exp(-hidden))).astype(jnp.bfloat16)
    added = jnp.dot(hidden, w_out_ref[...], preferred_element_type=jnp.float32)
    out_ref[...] = (updated + added).astype(jnp.bfloat16)


def update(place, features, own, other, gain, w_in, w_out):
    half = TILE // 2
    return pl.pallas_call(
        update_kernel,
        out_shape=jax.ShapeDtypeStruct((half, F), jnp.bfloat16),
        grid_spec=pltpu.PrefetchScalarGridSpec(
            num_scalar_prefetch=1,
            grid=(1,),
            in_specs=[
                pl.BlockSpec((half, F), lambda t, place: (place[0], 0)),
                pl.BlockSpec((half, F), lambda t, place: (0, 0)),
                pl.BlockSpec((half, F), lambda t, place: (0, 0)),
                pl.BlockSpec((1, F), lambda t, place: (0, 0)),
                pl.BlockSpec((F, F), lambda t, place: (0, 0)),
                pl.BlockSpec((F, F), lambda t, place: (0, 0)),
            ],
            out_specs=pl.BlockSpec((half, F), lambda t, place: (0, 0)),
        ),
        compiler_params=pltpu.CompilerParams(vmem_limit_bytes=8 << 20),
        name="update",
    )(place, features, own, other, gain, w_in, w_out)


def exchange(pieces, groups):
    return lax.all_to_all(
        pieces, AXES, split_axis=0, concat_axis=0, tiled=True, axis_index_groups=groups
    )


def shard_steps():
    return np.stack([row_steps(shard) for shard in range(SHARDS)])


def column_steps(steps):
    by_core = steps.reshape(4, 2, 8, PLANES, CHUNK)
    return by_core.transpose(1, 2, 3, 0, 4).reshape(2, 8, ALL_ROWS)


STEPS = shard_steps()
COLUMN_STEPS = column_steps(STEPS)


def on_device(features, coords, miller, filter_weights, norm_gain, w_in, w_out):
    number = lax.axis_index("atom") * 8 + lax.axis_index("wave")
    place = number // np.array([1, 1, 2, 8, 128], np.int32) % np.array([8, 2, 4, 4, 4], np.int32)

    factors = partial_factors(place, jnp.asarray(STEPS), coords, features)
    factors, coords, miller = lax.optimization_barrier((factors, coords, miller))
    arrived = exchange(factors.reshape(PLANES, CHUNK, F), GROUPS_XY)
    own_weights, other_weights = grid_weights(place, miller, filter_weights)
    other_weights = lax.ppermute(other_weights, AXES, SWAP)
    tables = message_tables(place, jnp.asarray(COLUMN_STEPS), coords)
    shares = exchange(plane_sum(arrived), GROUPS_LO)
    packed = exchange(scale_factors(shares, own_weights, other_weights), GROUPS_HI)
    filtered = exchange(filter_column(packed), GROUPS_XY).reshape(ALL_ROWS, F)
    own, other = message_parts(place, tables, filtered)
    other = lax.ppermute(other, AXES, SWAP)
    return update(place, features, own, other, norm_gain.reshape(1, F), w_in, w_out)


def solution(mesh):
    in_specs = (P("atom", None), P(None, "atom"), P(None, "wave"), P("wave", None), P(), P(), P())
    out_specs = P(("atom", "wave"), None)
    return jax.shard_map(
        on_device, mesh=mesh, in_specs=in_specs, out_specs=out_specs, check_vma=False
    )
```

```python
import itertools
import math

import jax
import jax.numpy as jnp
import numpy as np
from jax import lax
from jax.experimental import pallas as pl
from jax.experimental.pallas import tpu as pltpu
from jax.sharding import PartitionSpec as P

K = 4096
KMAX = 8
SIDE = 2 * KMAX + 1
PLANE = SIDE * SIDE
HALF = PLANE // 2
STRIP = 24
SHARDS = 8
POINTS = 320
PLANES = 16
PEERS = 64
OWN = POINTS // PEERS
CHUNK = 2 * OWN
ROWS = 2 * POINTS
F = 256
LANES = 128
TILE = 512
AXES = ("atom", "wave")
BOTH = (((1,), (0,)), ((), ()))
OUTER = (((0,), (0,)), ((), ()))


def device(y, z_lo, x, z_hi, core):
    return (((y * 4 + z_lo) * 4 + x) * 4 + z_hi) * 2 + core


FOUR = range(4)
TWO = range(2)
GROUPS_XY = [
    [device(y, l, x, h, c) for y in FOUR for x in FOUR] for l in FOUR for h in FOUR for c in TWO
]
GROUPS_LO = [
    [device(y, l, x, h, c) for l in FOUR] for y in FOUR for x in FOUR for h in FOUR for c in TWO
]
GROUPS_HI = [
    [device(y, l, x, h, c) for h in FOUR] for y in FOUR for x in FOUR for l in FOUR for c in TWO
]
SWAP = [
    (device(y, l, x, h, c), device(y, l, x, h, 1 - c))
    for y, l, x, h, c in itertools.product(FOUR, FOUR, FOUR, FOUR, TWO)
]


def wavevector(shard, point):
    if point < PLANE:
        return point // SIDE - KMAX, point % SIDE - KMAX, shard + 1
    strip = shard * STRIP + point - PLANE
    if point - PLANE >= STRIP or strip > HALF:
        return None
    return (strip + HALF) // SIDE - KMAX, (strip + HALF) % SIDE - KMAX, 0


def row_steps(shard):
    steps = np.zeros((8, ROWS), np.float32)
    for row in range(ROWS):
        chunk, part, own = row // CHUNK, row % CHUNK // OWN, row % OWN
        vector = wavevector(shard, chunk * OWN + own)
        if vector is None:
            steps[6, row] = -0.25
            continue
        steps[0:3, row] = vector
        steps[3:6, row] = vector
        steps[6, row] = -0.25 * part
    return steps


def split_coords(coords):
    high = (coords >> 8).astype(jnp.float32) * (1.0 / 256.0)
    low = (coords & 255).astype(jnp.float32) * (1.0 / 65536.0)
    ones = jnp.ones((2, coords.shape[1]), jnp.float32)
    return jnp.concatenate([high, low, ones], axis=0).astype(jnp.bfloat16)


def cosine_coefficients():
    nodes = 0.125 + 0.125 * np.cos(np.pi * (np.arange(400) + 0.5) / 400)
    fit = np.polynomial.chebyshev.Chebyshev.fit(
        nodes, np.cos(2 * np.pi * np.sqrt(nodes)), 6, domain=[0, 0.25]
    )
    return [float(c) for c in fit.convert(kind=np.polynomial.Polynomial).coef]


COSINE = cosine_coefficients()


def cosine_of_turns(turns):
    left = turns - jnp.round(turns)
    square = left * left
    total = jnp.full_like(square, COSINE[-1])
    for c in COSINE[-2::-1]:
        total = total * square + c
    return total


def factors_kernel(place_ref, steps_ref, coords_ref, features_ref, out_ref, tables, total):
    tile = pl.program_id(0)
    parts = split_coords(coords_ref[...])
    steps = steps_ref[0].astype(jnp.bfloat16)
    block = 128
    for start in range(0, ROWS, block):
        turns = lax.dot_general(
            steps[:, start : start + block], parts, OUTER, preferred_element_type=jnp.float32
        )
        tables[start : start + block, :] = cosine_of_turns(turns).astype(jnp.bfloat16)
    added = jnp.dot(tables[...], features_ref[...], preferred_element_type=jnp.float32)

    @pl.when(tile == 0)
    def _():
        total[...] = added

    @pl.when(tile > 0)
    def _():
        total[...] += added

    @pl.when(tile == pl.num_programs(0) - 1)
    def _():
        for peer in range(PEERS):
            for side in range(2):
                piece = total[peer * CHUNK : (peer + 1) * CHUNK, side * LANES : (side + 1) * LANES]
                out_ref[peer, side * CHUNK : (side + 1) * CHUNK, :] = piece.astype(jnp.bfloat16)


def partial_factors(place, steps, coords, features):
    atoms = features.shape[0]
    return pl.pallas_call(
        factors_kernel,
        out_shape=jax.ShapeDtypeStruct((PEERS, 2 * CHUNK, LANES), jnp.bfloat16),
        grid_spec=pltpu.PrefetchScalarGridSpec(
            num_scalar_prefetch=1,
            grid=(atoms // TILE,),
            in_specs=[
                pl.BlockSpec((1, 8, ROWS), lambda t, place: (place[0], 0, 0)),
                pl.BlockSpec((3, TILE), lambda t, place: (0, t)),
                pl.BlockSpec((TILE, F), lambda t, place: (t, 0)),
            ],
            out_specs=pl.BlockSpec((PEERS, 2 * CHUNK, LANES), lambda t, place: (0, 0, 0)),
            scratch_shapes=[
                pltpu.VMEM((ROWS, TILE), jnp.bfloat16),
                pltpu.VMEM((ROWS, F), jnp.float32),
            ],
        ),
        cost_estimate=pl.CostEstimate(
            flops=2 * ROWS * atoms * F, bytes_accessed=atoms * F * 2, transcendentals=0
        ),
        name="factors",
    )(place, steps, coords, features)


SPOTS = 32


def weights_kernel(place_ref, miller_ref, weights_ref, own_ref, other_ref):
    core, atom = place_ref[1], place_ref[3]
    m0, m1, m2 = miller_ref[0:1, :], miller_ref[1:2, :], miller_ref[2:3, :]
    flat = (m0 + KMAX) * SIDE + (m1 + KMAX)
    flip = (m2 < 0) | ((m2 == 0) & (flat < HALF))
    flat = jnp.where(flip, 2 * HALF - flat, flat)
    strip = flat - HALF
    strip_shard = (strip >= STRIP).astype(jnp.int32)
    for bound in range(2, 7):
        strip_shard += (strip >= bound * STRIP).astype(jnp.int32)
    shard = jnp.where(m2 == 0, strip_shard, jnp.abs(m2) - 1)
    point = jnp.where(m2 == 0, PLANE + strip - strip_shard * STRIP, flat)
    spot = shard * POINTS + point
    row = lax.broadcasted_iota(jnp.int32, (SPOTS, miller_ref.shape[1]), 0)
    high = (row >= OWN).astype(jnp.int32)
    for bound in range(2, 7):
        high += (row >= bound * OWN).astype(jnp.int32)
    base = atom * OWN + row - high * OWN
    weights = weights_ref[...]
    upper = weights.astype(jnp.bfloat16)
    lower = (weights - upper.astype(jnp.float32)).astype(jnp.bfloat16)
    for held, out_ref in ((core, own_ref), (1 - core, other_ref)):
        wanted = (high * 2 + held) * POINTS + base
        match = jnp.where(wanted == spot, 1.0, 0.0).astype(jnp.bfloat16)
        summed = jnp.dot(match, upper, preferred_element_type=jnp.float32)
        summed += jnp.dot(match, lower, preferred_element_type=jnp.float32)
        out_ref[...] = summed.astype(jnp.bfloat16)


def grid_weights(place, miller, weights):
    shape = jax.ShapeDtypeStruct((SPOTS, F), jnp.bfloat16)
    return pl.pallas_call(
        weights_kernel,
        out_shape=(shape, shape),
        in_specs=[
            pl.BlockSpec(memory_space=pltpu.SMEM),
            pl.BlockSpec(memory_space=pltpu.VMEM),
            pl.BlockSpec(memory_space=pltpu.VMEM),
        ],
        out_specs=(pl.BlockSpec(memory_space=pltpu.VMEM),) * 2,
        compiler_params=pltpu.CompilerParams(vmem_limit_bytes=8 << 20),
        cost_estimate=pl.CostEstimate(
            flops=8 * SPOTS * 512 * F, bytes_accessed=512 * F * 4, transcendentals=0
        ),
        name="grid_weights",
    )(place, miller, weights)


def scale_kernel(arrived_ref, own_ref, other_ref, out_ref, total, packed):
    total[...] = jnp.sum(arrived_ref[...].astype(jnp.float32), axis=0)
    halves = total[...] * total[...]
    squares = halves[:CHUNK] + halves[CHUNK:]
    power = jnp.sum(squares[:OWN] + squares[OWN:], axis=1, keepdims=True) * (1.0 / (2 * F))
    scale = 1.0 / jnp.sqrt(power + 1e-05)
    for part in range(2):
        for side in range(2):
            start = side * CHUNK + part * OWN
            packed[part * OWN : (part + 1) * OWN, side * LANES : (side + 1) * LANES] = (
                total[start : start + OWN, :] * scale
            )
    weights = own_ref[...].astype(jnp.float32) + other_ref[...].astype(jnp.float32)
    packed[CHUNK:, :] = weights[: PACKED - CHUNK]
    sent = packed[...].astype(jnp.bfloat16)
    for peer in range(4):
        out_ref[peer] = sent


PACKED = 32


def scale_factors(arrived, own, other):
    return pl.pallas_call(
        scale_kernel,
        out_shape=jax.ShapeDtypeStruct((4, PACKED, F), jnp.bfloat16),
        in_specs=[pl.BlockSpec(memory_space=pltpu.VMEM)] * 3,
        out_specs=pl.BlockSpec(memory_space=pltpu.VMEM),
        scratch_shapes=[
            pltpu.VMEM((2 * CHUNK, LANES), jnp.float32),
            pltpu.VMEM((PACKED, F), jnp.float32),
        ],
        compiler_params=pltpu.CompilerParams(vmem_limit_bytes=8 << 20),
        name="scale_factors",
    )(arrived, own, other)


LINE = 4 * CHUNK


def filter_kernel(arrived_ref, out_ref, filtered):
    weights = jnp.sum(arrived_ref[...].astype(jnp.float32), axis=0)
    for high in range(4):
        weight = weights[CHUNK + high * OWN : CHUNK + (high + 1) * OWN]
        factors = arrived_ref[high].astype(jnp.float32)
        for part in range(2):
            start = high * CHUNK + part * OWN
            filtered[start : start + OWN, :] = factors[part * OWN : (part + 1) * OWN] * weight
    line = filtered[...].astype(jnp.bfloat16)
    for peer in range(4):
        out_ref[peer] = line


def filter_line(arrived):
    return pl.pallas_call(
        filter_kernel,
        out_shape=jax.ShapeDtypeStruct((4, LINE, F), jnp.bfloat16),
        in_specs=[pl.BlockSpec(memory_space=pltpu.VMEM)],
        out_specs=pl.BlockSpec(memory_space=pltpu.VMEM),
        scratch_shapes=[pltpu.VMEM((LINE, F), jnp.float32)],
        compiler_params=pltpu.CompilerParams(vmem_limit_bytes=8 << 20),
        name="filter_line",
    )(arrived)


COLUMN = 4 * LINE


def copies_kernel(column_ref, out_ref):
    column = column_ref[...]
    for peer in range(PLANES):
        out_ref[peer] = column


def copies(column):
    return pl.pallas_call(
        copies_kernel,
        out_shape=jax.ShapeDtypeStruct((PLANES, COLUMN, F), jnp.bfloat16),
        in_specs=[pl.BlockSpec(memory_space=pltpu.VMEM)],
        out_specs=pl.BlockSpec(memory_space=pltpu.VMEM),
        compiler_params=pltpu.CompilerParams(vmem_limit_bytes=8 << 20),
        name="copies",
    )(column)


ALL_ROWS = COLUMN * PLANES


def tables_kernel(place_ref, steps_ref, coords_ref, out_ref):
    parts = split_coords(coords_ref[...])
    steps = steps_ref[0].astype(jnp.bfloat16)
    block = 128
    for start in range(0, TILE, block):
        turns = lax.dot_general(
            parts[:, start : start + block], steps, OUTER, preferred_element_type=jnp.float32
        )
        out_ref[start : start + block, :] = cosine_of_turns(turns).astype(jnp.bfloat16)


def message_tables(place, steps, coords):
    width = 512
    return pl.pallas_call(
        tables_kernel,
        out_shape=jax.ShapeDtypeStruct((TILE, ALL_ROWS), jnp.bfloat16),
        grid_spec=pltpu.PrefetchScalarGridSpec(
            num_scalar_prefetch=1,
            grid=(ALL_ROWS // width,),
            in_specs=[
                pl.BlockSpec((1, 8, width), lambda t, place: (place[1], 0, t)),
                pl.BlockSpec((3, TILE), lambda t, place: (0, place[2])),
            ],
            out_specs=pl.BlockSpec((TILE, width), lambda t, place: (0, t)),
        ),
        compiler_params=pltpu.CompilerParams(vmem_limit_bytes=16 << 20),
        cost_estimate=pl.CostEstimate(
            flops=16 * TILE * ALL_ROWS, bytes_accessed=TILE * ALL_ROWS * 2, transcendentals=0
        ),
        name="message_tables",
    )(place, steps, coords)


def message_kernel(place_ref, tables_ref, filtered_ref, own_ref, other_ref, total):
    core = place_ref[1]
    total[...] = jnp.dot(tables_ref[...], filtered_ref[...], preferred_element_type=jnp.float32)
    half = TILE // 2
    own_ref[...] = total[pl.ds(pl.multiple_of(core * half, half), half), :]
    other = total[pl.ds(pl.multiple_of((1 - core) * half, half), half), :]
    other_ref[...] = other.astype(jnp.bfloat16)


def message_parts(place, tables, filtered):
    half = TILE // 2
    return pl.pallas_call(
        message_kernel,
        out_shape=(
            jax.ShapeDtypeStruct((half, F), jnp.float32),
            jax.ShapeDtypeStruct((half, F), jnp.bfloat16),
        ),
        in_specs=[
            pl.BlockSpec(memory_space=pltpu.SMEM),
            pl.BlockSpec(memory_space=pltpu.VMEM),
            pl.BlockSpec(memory_space=pltpu.VMEM),
        ],
        out_specs=(pl.BlockSpec(memory_space=pltpu.VMEM),) * 2,
        scratch_shapes=[pltpu.VMEM((TILE, F), jnp.float32)],
        compiler_params=pltpu.CompilerParams(vmem_limit_bytes=16 << 20),
        name="message",
    )(place, tables, filtered)


def update_kernel(
    place_ref, features_ref, own_ref, other_ref, gain_ref, w_in_ref, w_out_ref, out_ref
):
    message = own_ref[...] + other_ref[...].astype(jnp.float32)
    updated = features_ref[...].astype(jnp.float32) + message * (1.0 / math.sqrt(K))
    power = jnp.mean(updated * updated, axis=1, keepdims=True)
    normed = (updated / jnp.sqrt(power + 1e-06) * gain_ref[...]).astype(jnp.bfloat16)
    hidden = jnp.dot(normed, w_in_ref[...], preferred_element_type=jnp.float32)
    hidden = (hidden / (1.0 + jnp.exp(-hidden))).astype(jnp.bfloat16)
    added = jnp.dot(hidden, w_out_ref[...], preferred_element_type=jnp.float32)
    out_ref[...] = (updated + added).astype(jnp.bfloat16)


def update(place, features, own, other, gain, w_in, w_out):
    half = TILE // 2
    return pl.pallas_call(
        update_kernel,
        out_shape=jax.ShapeDtypeStruct((half, F), jnp.bfloat16),
        grid_spec=pltpu.PrefetchScalarGridSpec(
            num_scalar_prefetch=1,
            grid=(1,),
            in_specs=[
                pl.BlockSpec((half, F), lambda t, place: (place[0], 0)),
                pl.BlockSpec((half, F), lambda t, place: (0, 0)),
                pl.BlockSpec((half, F), lambda t, place: (0, 0)),
                pl.BlockSpec((1, F), lambda t, place: (0, 0)),
                pl.BlockSpec((F, F), lambda t, place: (0, 0)),
                pl.BlockSpec((F, F), lambda t, place: (0, 0)),
            ],
            out_specs=pl.BlockSpec((half, F), lambda t, place: (0, 0)),
        ),
        compiler_params=pltpu.CompilerParams(vmem_limit_bytes=8 << 20),
        name="update",
    )(place, features, own, other, gain, w_in, w_out)


def exchange(pieces, groups):
    return lax.all_to_all(
        pieces, AXES, split_axis=0, concat_axis=0, tiled=True, axis_index_groups=groups
    )


def shard_steps():
    return np.stack([row_steps(shard) for shard in range(SHARDS)])


def column_steps(steps):
    by_core = steps.reshape(4, 2, 8, 4, 4, 4, CHUNK)
    return by_core.transpose(1, 2, 3, 5, 4, 0, 6).reshape(2, 8, ALL_ROWS)


STEPS = shard_steps()
COLUMN_STEPS = column_steps(STEPS)


def on_device(features, coords, miller, filter_weights, norm_gain, w_in, w_out):
    number = lax.axis_index("atom") * 8 + lax.axis_index("wave")
    place = number // np.array([1, 1, 2, 8], np.int32) % np.array([8, 2, 4, 64], np.int32)

    factors = partial_factors(place, jnp.asarray(STEPS), coords, features)
    factors, coords, miller = lax.optimization_barrier((factors, coords, miller))
    arrived = lax.all_to_all(factors, "atom", split_axis=0, concat_axis=0, tiled=True)
    own_weights, other_weights = grid_weights(place, miller, filter_weights)
    other_weights = lax.ppermute(other_weights, AXES, SWAP)
    tables = message_tables(place, jnp.asarray(COLUMN_STEPS), coords)
    packed = exchange(scale_factors(arrived, own_weights, other_weights), GROUPS_HI)
    line = exchange(filter_line(packed), GROUPS_LO)
    filtered = exchange(copies(line.reshape(COLUMN, F)), GROUPS_XY).reshape(ALL_ROWS, F)
    own, other = message_parts(place, tables, filtered)
    other = lax.ppermute(other, AXES, SWAP)
    return update(place, features, own, other, norm_gain.reshape(1, F), w_in, w_out)


def solution(mesh):
    in_specs = (P("atom", None), P(None, "atom"), P(None, "wave"), P("wave", None), P(), P(), P())
    out_specs = P(("atom", "wave"), None)
    return jax.shard_map(
        on_device, mesh=mesh, in_specs=in_specs, out_specs=out_specs, check_vma=False
    )
```

```python
import itertools
import math

import jax
import jax.numpy as jnp
import numpy as np
from jax import lax
from jax.experimental import pallas as pl
from jax.experimental.pallas import tpu as pltpu
from jax.sharding import PartitionSpec as P

K = 4096
KMAX = 8
SIDE = 2 * KMAX + 1
PLANES = 16
BLOCKS = 4
OWN = 20
BLOCK = 2 * OWN
COLUMN = BLOCKS * BLOCK
ALL_ROWS = PLANES * COLUMN
MIDDLE = 8
POINTS = BLOCKS * OWN
F = 256
HALVES = 256
TILE = 512
AXES = ("atom", "wave")
BOTH = (((1,), (0,)), ((), ()))
OUTER = (((0,), (0,)), ((), ()))


def device(y, z_lo, x, z_hi, core):
    return (((y * 4 + z_lo) * 4 + x) * 4 + z_hi) * 2 + core


FOUR = range(4)
TWO = range(2)
GROUPS_XY = [
    [device(y, l, x, h, c) for y in FOUR for x in FOUR] for l in FOUR for h in FOUR for c in TWO
]
GROUPS_LO = [
    [device(y, l, x, h, c) for l in FOUR] for y in FOUR for x in FOUR for h in FOUR for c in TWO
]
SWAP = [
    (device(y, l, x, h, c), device(y, l, x, h, 1 - c))
    for y, l, x, h, c in itertools.product(FOUR, FOUR, FOUR, FOUR, TWO)
]
OUTER_PAIRS = [
    (device(y, l, x, h, c), device(y, l, x, 3 - h, c))
    for y, l, x, h, c in itertools.product(FOUR, FOUR, FOUR, FOUR, TWO)
]
INNER_PAIRS = [
    (device(y, l, x, h, c), device(y, l, x, h ^ 1, c))
    for y, l, x, h, c in itertools.product(FOUR, FOUR, FOUR, FOUR, TWO)
]


def row_line(core, block, spot):
    third = 2 * block + core + 1
    if spot < SIDE:
        return (spot - KMAX, 0, third), 1
    if spot == SIDE:
        return (4 * core + block + 1, 0, 0), 1
    if spot == SIDE + 1:
        return (0, KMAX, third), 0
    if (core, block) == (0, 0):
        return (0, MIDDLE, 0), 1
    if (core, block) == (0, 1):
        return (MIDDLE + 1, KMAX, 0), 0
    if (core, block) == (0, 2):
        return (KMAX, KMAX, MIDDLE + 1), 2
    return None


def column_of(vector, part):
    steps = np.zeros(8, np.float32)
    steps[0:3] = vector
    steps[3:6] = vector
    steps[6] = -0.25 * part
    return steps


def row_steps(core, block, row, peer):
    line = row_line(core, block, row % OWN)
    if line is None:
        return column_of((0, 0, 0), 1)
    vector = list(line[0])
    vector[line[1]] += peer - MIDDLE
    return column_of(vector, row // OWN)


def stride_steps(core, block, row):
    line = row_line(core, block, row % OWN)
    vector = [0, 0, 0]
    vector[1 if line is None else line[1]] = 1
    return column_of(vector, 0)


MIXED = list(range(16, 24)) + list(range(32, 40))
FIRST = 2 * BLOCK + len(MIXED)


def first_steps():
    out = np.zeros((2, 8, BLOCKS * FIRST), np.float32)
    for core in range(2):
        columns = []
        for block in range(BLOCKS):
            columns += [row_steps(core, block, row, MIDDLE) for row in range(BLOCK)]
            columns += [row_steps(core, block, row, MIDDLE + 1) for row in range(BLOCK)]
            columns += [stride_steps(core, block, row) for row in MIXED]
        out[core] = np.stack(columns, axis=1)
    return out


def all_steps():
    rows = list(itertools.product(range(PLANES), range(BLOCKS), range(BLOCK)))
    return np.stack(
        [np.stack([row_steps(c, b, r, q) for q, b, r in rows], axis=1) for c in range(2)]
    )


def split_coords(coords):
    high = (coords >> 8).astype(jnp.float32) * (1.0 / 256.0)
    low = (coords & 255).astype(jnp.float32) * (1.0 / 65536.0)
    ones = jnp.ones((2, coords.shape[1]), jnp.float32)
    return jnp.concatenate([high, low, ones], axis=0).astype(jnp.bfloat16)


def cosine_coefficients():
    nodes = 0.125 + 0.125 * np.cos(np.pi * (np.arange(400) + 0.5) / 400)
    fit = np.polynomial.chebyshev.Chebyshev.fit(
        nodes, np.cos(2 * np.pi * np.sqrt(nodes)), 6, domain=[0, 0.25]
    )
    return [float(c) for c in fit.convert(kind=np.polynomial.Polynomial).coef]


COSINE = cosine_coefficients()


def cosine_of_turns(turns):
    left = turns - jnp.round(turns)
    square = left * left
    total = jnp.full_like(square, COSINE[-1])
    for c in COSINE[-2::-1]:
        total = total * square + c
    return total


def factors_kernel(steps_ref, coords_ref, features_ref, out_ref, first, tables, total):
    tile = pl.program_id(0)
    core = lax.axis_index("wave") % 2
    parts = split_coords(coords_ref[...])
    steps = steps_ref[core].astype(jnp.bfloat16)
    for block in range(BLOCKS):
        turns = lax.dot_general(
            steps[:, block * FIRST : (block + 1) * FIRST],
            parts,
            OUTER,
            preferred_element_type=jnp.float32,
        )
        first[block] = cosine_of_turns(turns)
    features = features_ref[...]
    for block in range(BLOCKS):
        for start in range(0, TILE, HALVES):
            lanes = pl.ds(start, HALVES)
            at = first[block, :BLOCK, lanes]
            after = first[block, BLOCK : 2 * BLOCK, lanes]
            mixed = 2.0 * first[block, 2 * BLOCK :, lanes]
            common = jnp.broadcast_to(mixed[0:1, :], (16, HALVES))
            stride = jnp.concatenate([common, mixed[:8], common[:8], mixed[8:]], axis=0)
            held = {MIDDLE: at, MIDDLE + 1: after}
            for peer in range(MIDDLE, PLANES, 2):
                for later in (peer, peer + 1):
                    if later not in held:
                        held[later] = stride * held[later - 1] - held[later - 2]
                pair = jnp.concatenate([held[peer], held[peer + 1]], axis=0)
                tables[block, peer * BLOCK : (peer + 2) * BLOCK, lanes] = pair.astype(jnp.bfloat16)
            for peer in range(MIDDLE - 2, -1, -2):
                for earlier in (peer + 1, peer):
                    held[earlier] = stride * held[earlier + 1] - held[earlier + 2]
                pair = jnp.concatenate([held[peer], held[peer + 1]], axis=0)
                tables[block, peer * BLOCK : (peer + 2) * BLOCK, lanes] = pair.astype(jnp.bfloat16)
        added = jnp.dot(tables[block], features, preferred_element_type=jnp.float32)

        @pl.when(tile == 0)
        def _():
            total[block] = added

        @pl.when(tile > 0)
        def _():
            total[block] += added

    @pl.when(tile == pl.num_programs(0) - 1)
    def _():
        for block in range(BLOCKS):
            for peer in range(PLANES):
                piece = total[block, peer * BLOCK : (peer + 1) * BLOCK, :]
                out_ref[peer, block * BLOCK : (block + 1) * BLOCK, :] = piece.astype(jnp.bfloat16)


def partial_factors(steps, coords, features):
    atoms = features.shape[0]
    return pl.pallas_call(
        factors_kernel,
        out_shape=jax.ShapeDtypeStruct((PLANES, COLUMN, F), jnp.bfloat16),
        grid=(atoms // TILE,),
        in_specs=[
            pl.BlockSpec((2, 8, BLOCKS * FIRST), lambda t: (0, 0, 0)),
            pl.BlockSpec((3, TILE), lambda t: (0, t)),
            pl.BlockSpec((TILE, F), lambda t: (t, 0)),
        ],
        out_specs=pl.BlockSpec((PLANES, COLUMN, F), lambda t: (0, 0, 0)),
        scratch_shapes=[
            pltpu.VMEM((BLOCKS, FIRST, TILE), jnp.float32),
            pltpu.VMEM((BLOCKS, PLANES * BLOCK, TILE), jnp.bfloat16),
            pltpu.VMEM((BLOCKS, PLANES * BLOCK, F), jnp.float32),
        ],
        cost_estimate=pl.CostEstimate(
            flops=2 * ALL_ROWS * atoms * F, bytes_accessed=atoms * F * 2, transcendentals=0
        ),
        name="factors",
    )(steps, coords, features)


def grid_spots(m0, m1, m2):
    flip = (m2 < 0) | ((m2 == 0) & ((m0 < 0) | ((m0 == 0) & (m1 < 0))))
    m0, m1, m2 = (jnp.where(flip, -m, m) for m in (m0, m1, m2))
    zero, last = m2 == 0, m1 == KMAX
    corner = last & (m0 == KMAX) & (m2 > 0)
    edge = zero & last & (m0 > 0)
    axis = zero & (m0 == 0)
    sheet = zero & (m0 > 0) & (m1 < KMAX)
    rim = last & (m0 < KMAX) & (m2 > 0)
    core = jnp.where(sheet, (m0 - 1) >> 2, (m2 - 1) & 1)
    block = jnp.where(sheet, (m0 - 1) & 3, (m2 - 1) >> 1)
    block = jnp.where(corner, 2, jnp.where(edge, 1, jnp.where(axis, 0, block)))
    core = jnp.where(corner | edge | axis, 0, core)
    peer = jnp.where(rim, m0 + KMAX, m1 + KMAX)
    peer = jnp.where(corner, m2 - 1, jnp.where(edge, m0 - 1, jnp.where(axis, m1, peer)))
    spot = jnp.where(sheet, SIDE, jnp.where(rim, SIDE + 1, m0 + KMAX))
    spot = jnp.where(corner | edge | axis, SIDE + 2, spot)
    return ((core * PLANES + peer) * BLOCKS + block) * OWN + spot


def weights_kernel(miller_ref, weights_ref, own_ref, other_ref):
    core, atom = lax.axis_index("wave") % 2, lax.axis_index("atom")
    plane = atom // 16 * 4 + atom % 4
    spots = grid_spots(miller_ref[0:1, :], miller_ref[1:2, :], miller_ref[2:3, :])
    row = lax.broadcasted_iota(jnp.int32, (POINTS, miller_ref.shape[1]), 0)
    weights = weights_ref[...]
    upper = weights.astype(jnp.bfloat16)
    lower = (weights - upper.astype(jnp.float32)).astype(jnp.bfloat16)
    for held, out_ref in ((core, own_ref), (1 - core, other_ref)):
        wanted = row + (held * PLANES + plane) * POINTS
        match = jnp.where(wanted == spots, 1.0, 0.0).astype(jnp.bfloat16)
        summed = jnp.dot(match, upper, preferred_element_type=jnp.float32)
        summed += jnp.dot(match, lower, preferred_element_type=jnp.float32)
        out_ref[...] = summed.astype(jnp.bfloat16)


def grid_weights(miller, weights):
    shape = jax.ShapeDtypeStruct((POINTS, F), jnp.bfloat16)
    return pl.pallas_call(
        weights_kernel,
        out_shape=(shape, shape),
        in_specs=[pl.BlockSpec(memory_space=pltpu.VMEM)] * 2,
        out_specs=(pl.BlockSpec(memory_space=pltpu.VMEM),) * 2,
        compiler_params=pltpu.CompilerParams(vmem_limit_bytes=8 << 20),
        cost_estimate=pl.CostEstimate(
            flops=8 * POINTS * 512 * F, bytes_accessed=512 * F * 4, transcendentals=0
        ),
        name="grid_weights",
    )(miller, weights)


def plane_sum_kernel(arrived_ref, out_ref):
    total = arrived_ref[0].astype(jnp.float32)
    for peer in range(1, PLANES):
        total += arrived_ref[peer].astype(jnp.float32)
    sent = total.astype(jnp.bfloat16)
    for peer in range(4):
        out_ref[peer] = sent


def plane_sum(arrived):
    return pl.pallas_call(
        plane_sum_kernel,
        out_shape=jax.ShapeDtypeStruct((4, COLUMN, F), jnp.bfloat16),
        in_specs=[pl.BlockSpec(memory_space=pltpu.VMEM)],
        out_specs=pl.BlockSpec(memory_space=pltpu.VMEM),
        compiler_params=pltpu.CompilerParams(vmem_limit_bytes=8 << 20),
        name="plane_sum",
    )(arrived)


def filter_kernel(arrived_ref, near_ref, far_ref, out_ref, total, filtered):
    total[...] = jnp.sum(arrived_ref[...].astype(jnp.float32), axis=0)
    weights = near_ref[...].astype(jnp.float32) + far_ref[...].astype(jnp.float32)
    for block in range(BLOCKS):
        start = block * BLOCK
        cosines, sines = total[start : start + OWN, :], total[start + OWN : start + BLOCK, :]
        power = jnp.sum(cosines * cosines + sines * sines, axis=1, keepdims=True) * (0.5 / F)
        scaled = weights[block * OWN : (block + 1) * OWN] * (1.0 / jnp.sqrt(power + 1e-05))
        filtered[start : start + OWN, :] = cosines * scaled
        filtered[start + OWN : start + BLOCK, :] = sines * scaled
    column = filtered[...].astype(jnp.bfloat16)
    for peer in range(PLANES):
        out_ref[peer] = column


def filter_column(arrived, near, far):
    return pl.pallas_call(
        filter_kernel,
        out_shape=jax.ShapeDtypeStruct((PLANES, COLUMN, F), jnp.bfloat16),
        in_specs=[pl.BlockSpec(memory_space=pltpu.VMEM)] * 3,
        out_specs=pl.BlockSpec(memory_space=pltpu.VMEM),
        scratch_shapes=[pltpu.VMEM((COLUMN, F), jnp.float32)] * 2,
        compiler_params=pltpu.CompilerParams(vmem_limit_bytes=8 << 20),
        name="filter_column",
    )(arrived, near, far)


def tables_kernel(place_ref, steps_ref, coords_ref, out_ref):
    parts = split_coords(coords_ref[...])
    steps = steps_ref[0].astype(jnp.bfloat16)
    block = 128
    for start in range(0, TILE, block):
        turns = lax.dot_general(
            parts[:, start : start + block], steps, OUTER, preferred_element_type=jnp.float32
        )
        out_ref[start : start + block, :] = cosine_of_turns(turns).astype(jnp.bfloat16)


def message_tables(place, steps, coords):
    width = 512
    return pl.pallas_call(
        tables_kernel,
        out_shape=jax.ShapeDtypeStruct((TILE, ALL_ROWS), jnp.bfloat16),
        grid_spec=pltpu.PrefetchScalarGridSpec(
            num_scalar_prefetch=1,
            grid=(ALL_ROWS // width,),
            in_specs=[
                pl.BlockSpec((1, 8, width), lambda t, place: (place[1], 0, t)),
                pl.BlockSpec((3, TILE), lambda t, place: (0, place[2])),
            ],
            out_specs=pl.BlockSpec((TILE, width), lambda t, place: (0, t)),
        ),
        compiler_params=pltpu.CompilerParams(vmem_limit_bytes=16 << 20),
        cost_estimate=pl.CostEstimate(
            flops=16 * TILE * ALL_ROWS, bytes_accessed=TILE * ALL_ROWS * 2, transcendentals=0
        ),
        name="message_tables",
    )(place, steps, coords)


def message_kernel(place_ref, tables_ref, filtered_ref, own_ref, other_ref, total):
    core = place_ref[1]
    total[...] = jnp.dot(tables_ref[...], filtered_ref[...], preferred_element_type=jnp.float32)
    half = TILE // 2
    own_ref[...] = total[pl.ds(pl.multiple_of(core * half, half), half), :]
    other = total[pl.ds(pl.multiple_of((1 - core) * half, half), half), :]
    other_ref[...] = other.astype(jnp.bfloat16)


def message_parts(place, tables, filtered):
    half = TILE // 2
    return pl.pallas_call(
        message_kernel,
        out_shape=(
            jax.ShapeDtypeStruct((half, F), jnp.float32),
            jax.ShapeDtypeStruct((half, F), jnp.bfloat16),
        ),
        in_specs=[
            pl.BlockSpec(memory_space=pltpu.SMEM),
            pl.BlockSpec(memory_space=pltpu.VMEM),
            pl.BlockSpec(memory_space=pltpu.VMEM),
        ],
        out_specs=(pl.BlockSpec(memory_space=pltpu.VMEM),) * 2,
        scratch_shapes=[pltpu.VMEM((TILE, F), jnp.float32)],
        compiler_params=pltpu.CompilerParams(vmem_limit_bytes=16 << 20),
        name="message",
    )(place, tables, filtered)


def update_kernel(
    place_ref, features_ref, own_ref, other_ref, gain_ref, w_in_ref, w_out_ref, out_ref
):
    message = own_ref[...] + other_ref[...].astype(jnp.float32)
    updated = features_ref[...].astype(jnp.float32) + message * (1.0 / math.sqrt(K))
    power = jnp.mean(updated * updated, axis=1, keepdims=True)
    normed = (updated / jnp.sqrt(power + 1e-06) * gain_ref[...]).astype(jnp.bfloat16)
    hidden = jnp.dot(normed, w_in_ref[...], preferred_element_type=jnp.float32)
    hidden = (hidden / (1.0 + jnp.exp(-hidden))).astype(jnp.bfloat16)
    added = jnp.dot(hidden, w_out_ref[...], preferred_element_type=jnp.float32)
    out_ref[...] = (updated + added).astype(jnp.bfloat16)


def update(place, features, own, other, gain, w_in, w_out):
    half = TILE // 2
    return pl.pallas_call(
        update_kernel,
        out_shape=jax.ShapeDtypeStruct((half, F), jnp.bfloat16),
        grid_spec=pltpu.PrefetchScalarGridSpec(
            num_scalar_prefetch=1,
            grid=(1,),
            in_specs=[
                pl.BlockSpec((half, F), lambda t, place: (place[0], 0)),
                pl.BlockSpec((half, F), lambda t, place: (0, 0)),
                pl.BlockSpec((half, F), lambda t, place: (0, 0)),
                pl.BlockSpec((1, F), lambda t, place: (0, 0)),
                pl.BlockSpec((F, F), lambda t, place: (0, 0)),
                pl.BlockSpec((F, F), lambda t, place: (0, 0)),
            ],
            out_specs=pl.BlockSpec((half, F), lambda t, place: (0, 0)),
        ),
        compiler_params=pltpu.CompilerParams(vmem_limit_bytes=8 << 20),
        name="update",
    )(place, features, own, other, gain, w_in, w_out)


def exchange(pieces, groups):
    return lax.all_to_all(
        pieces, AXES, split_axis=0, concat_axis=0, tiled=True, axis_index_groups=groups
    )


FIRST_STEPS = first_steps()
ALL_STEPS = all_steps()


def on_device(features, coords, miller, filter_weights, norm_gain, w_in, w_out):
    factors = partial_factors(jnp.asarray(FIRST_STEPS), coords, features)
    factors, coords, miller = lax.optimization_barrier((factors, coords, miller))
    number = lax.axis_index("atom") * 8 + lax.axis_index("wave")
    place = number // np.array([1, 1, 2], np.int32) % np.array([8, 2, 4], np.int32)
    arrived = exchange(factors, GROUPS_XY)
    weights, swapped = grid_weights(miller, filter_weights)
    weights += lax.ppermute(swapped, AXES, SWAP)
    weights += lax.ppermute(weights, AXES, OUTER_PAIRS)
    tables = message_tables(place, jnp.asarray(ALL_STEPS), coords)
    sums = plane_sum(arrived)
    sums, weights = lax.optimization_barrier((sums, weights))
    shares = exchange(sums, GROUPS_LO)
    filtered = filter_column(shares, weights, lax.ppermute(weights, AXES, INNER_PAIRS))
    filtered = exchange(filtered, GROUPS_XY).reshape(ALL_ROWS, F)
    own, other = message_parts(place, tables, filtered)
    other = lax.ppermute(other, AXES, SWAP)
    return update(place, features, own, other, norm_gain.reshape(1, F), w_in, w_out)


def solution(mesh):
    in_specs = (P("atom", None), P(None, "atom"), P(None, "wave"), P("wave", None), P(), P(), P())
    out_specs = P(("atom", "wave"), None)
    return jax.shard_map(
        on_device, mesh=mesh, in_specs=in_specs, out_specs=out_specs, check_vma=False
    )
```

```python
import functools
import itertools
import math

import jax
import jax.numpy as jnp
import numpy as np
from jax import lax
from jax.experimental import pallas as pl
from jax.experimental.pallas import tpu as pltpu
from jax.sharding import PartitionSpec as P

K = 4096
KMAX = 8
SIDE = 2 * KMAX + 1
PLANES = 16
BLOCKS = 4
OWN = 20
BLOCK = 2 * OWN
COLUMN = BLOCKS * BLOCK
ALL_ROWS = PLANES * COLUMN
MIDDLE = 8
POINTS = BLOCKS * OWN
F = 256
HALVES = 256
TILE = 512
AXES = ("atom", "wave")
OUTER = (((0,), (0,)), ((), ()))


def device(y, z_lo, x, z_hi, core):
    return (((y * 4 + z_lo) * 4 + x) * 4 + z_hi) * 2 + core


FOUR = range(4)
TWO = range(2)
GROUPS_XY = [
    [device(y, l, x, h, c) for y in FOUR for x in FOUR] for l in FOUR for h in FOUR for c in TWO
]
GROUPS_LO = [
    [device(y, l, x, h, c) for l in FOUR] for y in FOUR for x in FOUR for h in FOUR for c in TWO
]
SWAP = [
    (device(y, l, x, h, c), device(y, l, x, h, 1 - c))
    for y, l, x, h, c in itertools.product(FOUR, FOUR, FOUR, FOUR, TWO)
]
OUTER_PAIRS = [
    (device(y, l, x, h, c), device(y, l, x, 3 - h, c))
    for y, l, x, h, c in itertools.product(FOUR, FOUR, FOUR, FOUR, TWO)
]
INNER_PAIRS = [
    (device(y, l, x, h, c), device(y, l, x, h ^ 1, c))
    for y, l, x, h, c in itertools.product(FOUR, FOUR, FOUR, FOUR, TWO)
]


def row_line(core, block, spot):
    third = 2 * block + core + 1
    if spot < SIDE:
        return (spot - KMAX, 0, third), 1
    if spot == SIDE:
        return (4 * core + block + 1, 0, 0), 1
    if spot == SIDE + 1:
        return (0, KMAX, third), 0
    if (core, block) == (0, 0):
        return (0, MIDDLE, 0), 1
    if (core, block) == (0, 1):
        return (MIDDLE + 1, KMAX, 0), 0
    if (core, block) == (0, 2):
        return (KMAX, KMAX, MIDDLE + 1), 2
    return None


def column_of(vector, part):
    steps = np.zeros(8, np.float32)
    steps[0:3] = vector
    steps[3:6] = vector
    steps[6] = -0.25 * part
    return steps


def spot_of(row):
    if row < 2 * SIDE:
        return row % SIDE, row // SIDE
    extra = OWN - SIDE
    return SIDE + (row - 2 * SIDE) % extra, (row - 2 * SIDE) // extra


def row_steps(core, block, row, peer):
    spot, part = spot_of(row)
    line = row_line(core, block, spot)
    if line is None:
        return column_of((0, 0, 0), 1)
    vector = list(line[0])
    vector[line[1]] += peer - MIDDLE
    return column_of(vector, part)


def stride_steps(core, block, row):
    line = row_line(core, block, spot_of(row)[0])
    vector = [0, 0, 0]
    vector[1 if line is None else line[1]] = 1
    return column_of(vector, 0)


MAIN = 32
MIXED = range(MAIN, BLOCK)
AT = [0, 2 * BLOCK, 4 * BLOCK, 4 * BLOCK + 16]
STRIDES = 4 * BLOCK + 32
THIRD = STRIDES + 8 * BLOCKS
FIRST = THIRD + 8


def first_steps():
    out = np.zeros((2, 8, FIRST), np.float32)
    for core in range(2):
        columns = []
        for block in range(BLOCKS):
            rows = range(BLOCK) if block < 2 else MIXED
            columns += [row_steps(core, block, row, MIDDLE) for row in rows]
            columns += [row_steps(core, block, row, MIDDLE + 1) for row in rows]
        for block in range(BLOCKS):
            columns += [stride_steps(core, block, row) for row in MIXED]
        columns += [column_of((0, 0, 2), 0)] * 8
        out[core] = np.stack(columns, axis=1)
    return out


def all_steps():
    rows = list(itertools.product(range(PLANES), range(BLOCKS), range(BLOCK)))
    return np.stack(
        [np.stack([row_steps(c, b, r, q) for q, b, r in rows], axis=1) for c in range(2)]
    )


def split_coords(coords):
    high = (coords >> 8).astype(jnp.float32) * (1.0 / 256.0)
    low = (coords & 255).astype(jnp.float32) * (1.0 / 65536.0)
    ones = jnp.ones((2, coords.shape[1]), jnp.float32)
    return jnp.concatenate([high, low, ones], axis=0).astype(jnp.bfloat16)


def cosine_coefficients():
    nodes = 0.125 + 0.125 * np.cos(np.pi * (np.arange(400) + 0.5) / 400)
    fit = np.polynomial.chebyshev.Chebyshev.fit(
        nodes, np.cos(2 * np.pi * np.sqrt(nodes)), 5, domain=[0, 0.25]
    )
    return [float(c) for c in fit.convert(kind=np.polynomial.Polynomial).coef]


COSINE = cosine_coefficients()


def cosine_of_turns(turns):
    left = turns - jnp.round(turns)
    square = left * left
    total = jnp.full_like(square, COSINE[-1])
    for c in COSINE[-2::-1]:
        total = total * square + c
    return total


def factors_kernel(steps_ref, coords_ref, features_ref, out_ref, first, tables, total):
    tile = pl.program_id(0)

    @pl.when(tile == 0)
    def _():
        total[...] = jnp.zeros_like(total)

    core = lax.axis_index("wave") % 2
    parts = split_coords(coords_ref[...])
    steps = steps_ref[core].astype(jnp.bfloat16)
    turns = lax.dot_general(steps, parts, OUTER, preferred_element_type=jnp.float32)
    first[...] = cosine_of_turns(turns)
    features = features_ref[...]
    mains = {}
    for block in range(BLOCKS):
        for start in range(0, TILE, HALVES):
            lanes = pl.ds(start, HALVES)
            if block < 2:
                at = first[AT[block] : AT[block] + BLOCK, lanes]
                after = first[AT[block] + BLOCK : AT[block] + 2 * BLOCK, lanes]
            else:
                third = 2.0 * first[THIRD : THIRD + 1, lanes]
                main = [
                    third * near - far
                    for near, far in zip(mains[block - 1, start], mains[block - 2, start])
                ]
                mixed = [first[AT[block] + 8 * p : AT[block] + 8 * p + 8, lanes] for p in TWO]
                at, after = (jnp.concatenate([main[p], mixed[p]], axis=0) for p in TWO)
            mains[block, start] = at[:MAIN], after[:MAIN]
            mixed = 2.0 * first[STRIDES + 8 * block : STRIDES + 8 * block + 8, lanes]
            common = jnp.broadcast_to(mixed[0:1, :], (MAIN, HALVES))
            stride = jnp.concatenate([common, mixed], axis=0)
            held = {MIDDLE: at, MIDDLE + 1: after}
            for peer in range(MIDDLE, PLANES, 2):
                for later in (peer, peer + 1):
                    if later not in held:
                        held[later] = stride * held[later - 1] - held[later - 2]
                pair = jnp.concatenate([held[peer], held[peer + 1]], axis=0)
                tables[block, peer * BLOCK : (peer + 2) * BLOCK, lanes] = pair.astype(jnp.bfloat16)
            for peer in range(MIDDLE - 2, -1, -2):
                for earlier in (peer + 1, peer):
                    held[earlier] = stride * held[earlier + 1] - held[earlier + 2]
                pair = jnp.concatenate([held[peer], held[peer + 1]], axis=0)
                tables[block, peer * BLOCK : (peer + 2) * BLOCK, lanes] = pair.astype(jnp.bfloat16)
        total[block] += jnp.dot(tables[block], features, preferred_element_type=jnp.float32)

    @pl.when(tile == pl.num_programs(0) - 1)
    def _():
        for block in range(BLOCKS):
            for peer in range(PLANES):
                piece = total[block, peer * BLOCK : (peer + 1) * BLOCK, :]
                out_ref[peer, block * BLOCK : (block + 1) * BLOCK, :] = piece.astype(jnp.bfloat16)


def partial_factors(steps, coords, features):
    atoms = features.shape[0]
    return pl.pallas_call(
        factors_kernel,
        out_shape=jax.ShapeDtypeStruct((PLANES, COLUMN, F), jnp.bfloat16),
        grid=(atoms // TILE,),
        in_specs=[
            pl.BlockSpec((2, 8, FIRST), lambda t: (0, 0, 0)),
            pl.BlockSpec((3, TILE), lambda t: (0, t)),
            pl.BlockSpec((TILE, F), lambda t: (t, 0)),
        ],
        out_specs=pl.BlockSpec((PLANES, COLUMN, F), lambda t: (0, 0, 0)),
        scratch_shapes=[
            pltpu.VMEM((FIRST, TILE), jnp.float32),
            pltpu.VMEM((BLOCKS, PLANES * BLOCK, TILE), jnp.bfloat16),
            pltpu.VMEM((BLOCKS, PLANES * BLOCK, F), jnp.float32),
        ],
        cost_estimate=pl.CostEstimate(
            flops=2 * ALL_ROWS * atoms * F, bytes_accessed=atoms * F * 2, transcendentals=0
        ),
        name="factors",
    )(steps, coords, features)


def grid_spots(m0, m1, m2):
    flip = (m2 < 0) | ((m2 == 0) & ((m0 < 0) | ((m0 == 0) & (m1 < 0))))
    m0, m1, m2 = (jnp.where(flip, -m, m) for m in (m0, m1, m2))
    zero, last = m2 == 0, m1 == KMAX
    corner = last & (m0 == KMAX) & (m2 > 0)
    edge = zero & last & (m0 > 0)
    axis = zero & (m0 == 0)
    sheet = zero & (m0 > 0) & (m1 < KMAX)
    rim = last & (m0 < KMAX) & (m2 > 0)
    core = jnp.where(sheet, (m0 - 1) >> 2, (m2 - 1) & 1)
    block = jnp.where(sheet, (m0 - 1) & 3, (m2 - 1) >> 1)
    block = jnp.where(corner, 2, jnp.where(edge, 1, jnp.where(axis, 0, block)))
    core = jnp.where(corner | edge | axis, 0, core)
    peer = jnp.where(rim, m0 + KMAX, m1 + KMAX)
    peer = jnp.where(corner, m2 - 1, jnp.where(edge, m0 - 1, jnp.where(axis, m1, peer)))
    spot = jnp.where(sheet, SIDE, jnp.where(rim, SIDE + 1, m0 + KMAX))
    spot = jnp.where(corner | edge | axis, SIDE + 2, spot)
    return ((core * PLANES + peer) * BLOCKS + block) * OWN + spot


def weights_kernel(miller_ref, weights_ref, own_ref, other_ref):
    core, atom = lax.axis_index("wave") % 2, lax.axis_index("atom")
    plane = atom // 16 * 4 + atom % 4
    spots = grid_spots(miller_ref[0:1, :], miller_ref[1:2, :], miller_ref[2:3, :])
    row = lax.broadcasted_iota(jnp.int32, (POINTS, miller_ref.shape[1]), 0)
    weights = weights_ref[...]
    upper = weights.astype(jnp.bfloat16)
    lower = (weights - upper.astype(jnp.float32)).astype(jnp.bfloat16)
    for held, out_ref in ((core, own_ref), (1 - core, other_ref)):
        wanted = row + (held * PLANES + plane) * POINTS
        match = jnp.where(wanted == spots, 1.0, 0.0).astype(jnp.bfloat16)
        summed = jnp.dot(match, upper, preferred_element_type=jnp.float32)
        summed += jnp.dot(match, lower, preferred_element_type=jnp.float32)
        out_ref[...] = summed.astype(jnp.bfloat16)


def grid_weights(miller, weights):
    shape = jax.ShapeDtypeStruct((POINTS, F), jnp.bfloat16)
    return pl.pallas_call(
        weights_kernel,
        out_shape=(shape, shape),
        in_specs=[pl.BlockSpec(memory_space=pltpu.VMEM)] * 2,
        out_specs=(pl.BlockSpec(memory_space=pltpu.VMEM),) * 2,
        compiler_params=pltpu.CompilerParams(vmem_limit_bytes=8 << 20),
        cost_estimate=pl.CostEstimate(
            flops=8 * POINTS * 512 * F, bytes_accessed=512 * F * 4, transcendentals=0
        ),
        name="grid_weights",
    )(miller, weights)


def plane_sum_kernel(arrived_ref, out_ref):
    total = arrived_ref[0].astype(jnp.float32)
    for peer in range(1, PLANES):
        total += arrived_ref[peer].astype(jnp.float32)
    sent = total.astype(jnp.bfloat16)
    for peer in range(4):
        out_ref[peer] = sent


def plane_sum(arrived):
    return pl.pallas_call(
        plane_sum_kernel,
        out_shape=jax.ShapeDtypeStruct((4, COLUMN, F), jnp.bfloat16),
        in_specs=[pl.BlockSpec(memory_space=pltpu.VMEM)],
        out_specs=pl.BlockSpec(memory_space=pltpu.VMEM),
        compiler_params=pltpu.CompilerParams(vmem_limit_bytes=8 << 20),
        name="plane_sum",
    )(arrived)


def filter_kernel(arrived_ref, near_ref, far_ref, out_ref, total, filtered):
    total[...] = jnp.sum(arrived_ref[...].astype(jnp.float32), axis=0)
    weights = near_ref[...].astype(jnp.float32) + far_ref[...].astype(jnp.float32)
    extra = OWN - SIDE
    for block in range(BLOCKS):
        for row, spot, count in ((0, 0, SIDE), (2 * SIDE, SIDE, extra)):
            start, weight = block * BLOCK + row, block * OWN + spot
            cosines, sines = total[start : start + count, :], total[start + count : start + 2 * count, :]
            power = jnp.sum(cosines * cosines + sines * sines, axis=1, keepdims=True) * (0.5 / F)
            scaled = weights[weight : weight + count] * (1.0 / jnp.sqrt(power + 1e-05))
            filtered[start : start + count, :] = cosines * scaled
            filtered[start + count : start + 2 * count, :] = sines * scaled
    column = filtered[...].astype(jnp.bfloat16)
    for peer in range(PLANES):
        out_ref[peer] = column


def filter_column(arrived, near, far):
    return pl.pallas_call(
        filter_kernel,
        out_shape=jax.ShapeDtypeStruct((PLANES, COLUMN, F), jnp.bfloat16),
        in_specs=[pl.BlockSpec(memory_space=pltpu.VMEM)] * 3,
        out_specs=pl.BlockSpec(memory_space=pltpu.VMEM),
        scratch_shapes=[pltpu.VMEM((COLUMN, F), jnp.float32)] * 2,
        compiler_params=pltpu.CompilerParams(vmem_limit_bytes=8 << 20),
        name="filter_column",
    )(arrived, near, far)


def tables_kernel(place_ref, steps_ref, coords_ref, out_ref):
    parts = split_coords(coords_ref[...])
    steps = steps_ref[0].astype(jnp.bfloat16)
    block = 128
    for start in range(0, TILE, block):
        turns = lax.dot_general(
            parts[:, start : start + block], steps, OUTER, preferred_element_type=jnp.float32
        )
        out_ref[start : start + block, :] = cosine_of_turns(turns).astype(jnp.bfloat16)


def message_tables(place, steps, coords):
    width = 512
    return pl.pallas_call(
        tables_kernel,
        out_shape=jax.ShapeDtypeStruct((TILE, ALL_ROWS), jnp.bfloat16),
        grid_spec=pltpu.PrefetchScalarGridSpec(
            num_scalar_prefetch=1,
            grid=(ALL_ROWS // width,),
            in_specs=[
                pl.BlockSpec((1, 8, width), lambda t, place: (place[1], 0, t)),
                pl.BlockSpec((3, TILE), lambda t, place: (0, place[2])),
            ],
            out_specs=pl.BlockSpec((TILE, width), lambda t, place: (0, t)),
        ),
        compiler_params=pltpu.CompilerParams(vmem_limit_bytes=16 << 20),
        cost_estimate=pl.CostEstimate(
            flops=16 * TILE * ALL_ROWS, bytes_accessed=TILE * ALL_ROWS * 2, transcendentals=0
        ),
        name="message_tables",
    )(place, steps, coords)


def message_kernel(place_ref, tables_ref, filtered_ref, out_ref, *, own):
    half = TILE // 2
    core = place_ref[1] if own else 1 - place_ref[1]
    tables = tables_ref[pl.ds(pl.multiple_of(core * half, half), half), :]
    message = jnp.dot(tables, filtered_ref[...], preferred_element_type=jnp.float32)
    out_ref[...] = message.astype(out_ref.dtype)


def message_half(place, tables, filtered, own):
    half = TILE // 2
    return pl.pallas_call(
        functools.partial(message_kernel, own=own),
        out_shape=jax.ShapeDtypeStruct((half, F), jnp.float32 if own else jnp.bfloat16),
        in_specs=[
            pl.BlockSpec(memory_space=pltpu.SMEM),
            pl.BlockSpec(memory_space=pltpu.VMEM),
            pl.BlockSpec(memory_space=pltpu.VMEM),
        ],
        out_specs=pl.BlockSpec(memory_space=pltpu.VMEM),
        compiler_params=pltpu.CompilerParams(vmem_limit_bytes=16 << 20),
        cost_estimate=pl.CostEstimate(
            flops=2 * half * ALL_ROWS * F, bytes_accessed=4 * half * ALL_ROWS, transcendentals=0
        ),
        name="message_own" if own else "message_other",
    )(place, tables, filtered)


def update_kernel(
    place_ref, features_ref, own_ref, other_ref, gain_ref, w_in_ref, w_out_ref, out_ref
):
    message = own_ref[...] + other_ref[...].astype(jnp.float32)
    updated = features_ref[...].astype(jnp.float32) + message * (1.0 / math.sqrt(K))
    power = jnp.mean(updated * updated, axis=1, keepdims=True)
    normed = (updated / jnp.sqrt(power + 1e-06) * gain_ref[...]).astype(jnp.bfloat16)
    hidden = jnp.dot(normed, w_in_ref[...], preferred_element_type=jnp.float32)
    hidden = (hidden / (1.0 + jnp.exp(-hidden))).astype(jnp.bfloat16)
    added = jnp.dot(hidden, w_out_ref[...], preferred_element_type=jnp.float32)
    out_ref[...] = (updated + added).astype(jnp.bfloat16)


def update(place, features, own, other, gain, w_in, w_out):
    half = TILE // 2
    return pl.pallas_call(
        update_kernel,
        out_shape=jax.ShapeDtypeStruct((half, F), jnp.bfloat16),
        grid_spec=pltpu.PrefetchScalarGridSpec(
            num_scalar_prefetch=1,
            grid=(1,),
            in_specs=[
                pl.BlockSpec((half, F), lambda t, place: (place[0], 0)),
                pl.BlockSpec((half, F), lambda t, place: (0, 0)),
                pl.BlockSpec((half, F), lambda t, place: (0, 0)),
                pl.BlockSpec((1, F), lambda t, place: (0, 0)),
                pl.BlockSpec((F, F), lambda t, place: (0, 0)),
                pl.BlockSpec((F, F), lambda t, place: (0, 0)),
            ],
            out_specs=pl.BlockSpec((half, F), lambda t, place: (0, 0)),
        ),
        compiler_params=pltpu.CompilerParams(vmem_limit_bytes=8 << 20),
        name="update",
    )(place, features, own, other, gain, w_in, w_out)


def exchange(pieces, groups):
    return lax.all_to_all(
        pieces, AXES, split_axis=0, concat_axis=0, tiled=True, axis_index_groups=groups
    )


FIRST_STEPS = first_steps()
ALL_STEPS = all_steps()


def layer(features, coords, miller, filter_weights, norm_gain, w_in, w_out):
    factors = partial_factors(jnp.asarray(FIRST_STEPS), coords, features)
    factors, coords, miller = lax.optimization_barrier((factors, coords, miller))
    number = lax.axis_index("atom") * 8 + lax.axis_index("wave")
    place = number // np.array([1, 1, 2], np.int32) % np.array([8, 2, 4], np.int32)
    arrived = exchange(factors, GROUPS_XY)
    weights, swapped = grid_weights(miller, filter_weights)
    weights += lax.ppermute(swapped, AXES, SWAP)
    weights += lax.ppermute(weights, AXES, OUTER_PAIRS)
    arrived, weights = lax.optimization_barrier((arrived, weights))
    far_weights = lax.ppermute(weights, AXES, INNER_PAIRS)
    tables = message_tables(place, jnp.asarray(ALL_STEPS), coords)
    sums = plane_sum(arrived)
    shares = exchange(sums, GROUPS_LO)
    filtered = filter_column(shares, weights, far_weights)
    filtered = exchange(filtered, GROUPS_XY).reshape(ALL_ROWS, F)
    other = lax.ppermute(message_half(place, tables, filtered, False), AXES, SWAP)
    own = message_half(place, tables, filtered, True)
    return update(place, features, own, other, norm_gain.reshape(1, F), w_in, w_out)


def solution(mesh):
    in_specs = (P("atom", None), P(None, "atom"), P(None, "wave"), P("wave", None), P(), P(), P())
    out_specs = P(("atom", "wave"), None)
    return jax.shard_map(layer, mesh=mesh, in_specs=in_specs, out_specs=out_specs, check_vma=False)
```

```python
import functools
import itertools
import math

import jax
import jax.numpy as jnp
import numpy as np
from jax import lax
from jax.experimental import pallas as pl
from jax.experimental.pallas import tpu as pltpu
from jax.sharding import PartitionSpec as P

K = 4096
KMAX = 8
SIDE = 2 * KMAX + 1
PLANES = 16
BLOCKS = 4
OWN = 20
BLOCK = 2 * OWN
COLUMN = BLOCKS * BLOCK
HALF = COLUMN // 2
ALL_ROWS = PLANES * HALF
MIDDLE = 8
POINTS = BLOCKS * OWN // 2
F = 256
HALVES = 256
TILE = 512
AXES = ("atom", "wave")
OUTER = (((0,), (0,)), ((), ()))


def device(y, z_lo, x, z_hi, core):
    return (((y * 4 + z_lo) * 4 + x) * 4 + z_hi) * 2 + core


FOUR = range(4)
TWO = range(2)
GROUPS_XY = [
    [device(y, l, x, h, c) for y in FOUR for x in FOUR] for l in FOUR for h in FOUR for c in TWO
]
GROUPS_LO = [
    [device(y, l, x, h, c) for l in FOUR] for y in FOUR for x in FOUR for h in FOUR for c in TWO
]
SWAP = [
    (device(y, l, x, h, c), device(y, l, x, h, 1 - c))
    for y, l, x, h, c in itertools.product(FOUR, FOUR, FOUR, FOUR, TWO)
]
OUTER_PAIRS = [
    (device(y, l, x, h, c), device(y, l, x, 3 - h, c))
    for y, l, x, h, c in itertools.product(FOUR, FOUR, FOUR, FOUR, TWO)
]
INNER_PAIRS = [
    (device(y, l, x, h, c), device(y, l, x, h ^ 1, c))
    for y, l, x, h, c in itertools.product(FOUR, FOUR, FOUR, FOUR, TWO)
]


LINE_SAME = [
    (device(y, l, x, h, c), device(y, l ^ 1, x, h, c))
    for y, l, x, h, c in itertools.product(FOUR, FOUR, FOUR, FOUR, TWO)
]
LINE_CROSS = [
    (device(y, l, x, h, c), device(y, l ^ 1, x, h, 1 - c))
    for y, l, x, h, c in itertools.product(FOUR, FOUR, FOUR, FOUR, TWO)
]


def row_line(core, block, spot):
    third = 2 * block + core + 1
    if spot < SIDE:
        return (spot - KMAX, 0, third), 1
    if spot == SIDE:
        return (4 * core + block + 1, 0, 0), 1
    if spot == SIDE + 1:
        return (0, KMAX, third), 0
    if (core, block) == (0, 0):
        return (0, MIDDLE, 0), 1
    if (core, block) == (0, 1):
        return (MIDDLE + 1, KMAX, 0), 0
    if (core, block) == (0, 2):
        return (KMAX, KMAX, MIDDLE + 1), 2
    return None


def column_of(vector, part):
    steps = np.zeros(8, np.float32)
    steps[0:3] = vector
    steps[3:6] = vector
    steps[6] = -0.25 * part
    return steps


def spot_of(row):
    if row < 2 * SIDE:
        return row % SIDE, row // SIDE
    extra = OWN - SIDE
    return SIDE + (row - 2 * SIDE) % extra, (row - 2 * SIDE) // extra


def row_steps(core, block, row, peer):
    spot, part = spot_of(row)
    line = row_line(core, block, spot)
    if line is None:
        return column_of((0, 0, 0), 1)
    vector = list(line[0])
    vector[line[1]] += peer - MIDDLE
    return column_of(vector, part)


def stride_steps(core, block, row):
    line = row_line(core, block, spot_of(row)[0])
    vector = [0, 0, 0]
    vector[1 if line is None else line[1]] = 1
    return column_of(vector, 0)


MAIN = 32
MIXED = range(MAIN, BLOCK)
AT = [0, 2 * BLOCK, 4 * BLOCK, 4 * BLOCK + 16]
STRIDES = 4 * BLOCK + 32
THIRD = STRIDES + 8 * BLOCKS
FIRST = THIRD + 8


def first_steps():
    out = np.zeros((2, 8, FIRST), np.float32)
    for core in range(2):
        columns = []
        for block in range(BLOCKS):
            rows = range(BLOCK) if block < 2 else MIXED
            columns += [row_steps(core, block, row, MIDDLE) for row in rows]
            columns += [row_steps(core, block, row, MIDDLE + 1) for row in rows]
        for block in range(BLOCKS):
            columns += [stride_steps(core, block, row) for row in MIXED]
        columns += [column_of((0, 0, 2), 0)] * 8
        out[core] = np.stack(columns, axis=1)
    return out


def all_steps():
    out = []
    for core, part in itertools.product(TWO, TWO):
        rows = itertools.product(range(PLANES), (2 * part, 2 * part + 1), range(BLOCK))
        out.append(np.stack([row_steps(core, b, r, q) for q, b, r in rows], axis=1))
    return np.stack(out)


def split_coords(coords):
    high = (coords >> 8).astype(jnp.float32) * (1.0 / 256.0)
    low = (coords & 255).astype(jnp.float32) * (1.0 / 65536.0)
    ones = jnp.ones((2, coords.shape[1]), jnp.float32)
    return jnp.concatenate([high, low, ones], axis=0).astype(jnp.bfloat16)


def cosine_coefficients():
    nodes = 0.125 + 0.125 * np.cos(np.pi * (np.arange(400) + 0.5) / 400)
    fit = np.polynomial.chebyshev.Chebyshev.fit(
        nodes, np.cos(2 * np.pi * np.sqrt(nodes)), 5, domain=[0, 0.25]
    )
    return [float(c) for c in fit.convert(kind=np.polynomial.Polynomial).coef]


COSINE = cosine_coefficients()


def cosine_of_turns(turns):
    left = turns - jnp.round(turns)
    square = left * left
    total = jnp.full_like(square, COSINE[-1])
    for c in COSINE[-2::-1]:
        total = total * square + c
    return total


def factors_kernel(steps_ref, coords_ref, features_ref, out_ref, first, tables, total):
    tile = pl.program_id(0)

    @pl.when(tile == 0)
    def _():
        total[...] = jnp.zeros_like(total)

    core = lax.axis_index("wave") % 2
    parts = split_coords(coords_ref[...])
    steps = steps_ref[core].astype(jnp.bfloat16)
    turns = lax.dot_general(steps, parts, OUTER, preferred_element_type=jnp.float32)
    first[...] = cosine_of_turns(turns)
    features = features_ref[...]
    mains = {}
    for block in range(BLOCKS):
        for start in range(0, TILE, HALVES):
            lanes = pl.ds(start, HALVES)
            if block < 2:
                at = first[AT[block] : AT[block] + BLOCK, lanes]
                after = first[AT[block] + BLOCK : AT[block] + 2 * BLOCK, lanes]
            else:
                third = 2.0 * first[THIRD : THIRD + 1, lanes]
                main = [
                    third * near - far
                    for near, far in zip(mains[block - 1, start], mains[block - 2, start])
                ]
                mixed = [first[AT[block] + 8 * p : AT[block] + 8 * p + 8, lanes] for p in TWO]
                at, after = (jnp.concatenate([main[p], mixed[p]], axis=0) for p in TWO)
            mains[block, start] = at[:MAIN], after[:MAIN]
            mixed = 2.0 * first[STRIDES + 8 * block : STRIDES + 8 * block + 8, lanes]
            common = jnp.broadcast_to(mixed[0:1, :], (MAIN, HALVES))
            stride = jnp.concatenate([common, mixed], axis=0)
            held = {MIDDLE: at, MIDDLE + 1: after}
            for peer in range(MIDDLE, PLANES, 2):
                for later in (peer, peer + 1):
                    if later not in held:
                        held[later] = stride * held[later - 1] - held[later - 2]
                pair = jnp.concatenate([held[peer], held[peer + 1]], axis=0)
                tables[block, peer * BLOCK : (peer + 2) * BLOCK, lanes] = pair.astype(jnp.bfloat16)
            for peer in range(MIDDLE - 2, -1, -2):
                for earlier in (peer + 1, peer):
                    held[earlier] = stride * held[earlier + 1] - held[earlier + 2]
                pair = jnp.concatenate([held[peer], held[peer + 1]], axis=0)
                tables[block, peer * BLOCK : (peer + 2) * BLOCK, lanes] = pair.astype(jnp.bfloat16)
        total[block] += jnp.dot(tables[block], features, preferred_element_type=jnp.float32)

    @pl.when(tile == pl.num_programs(0) - 1)
    def _():
        for block in range(BLOCKS):
            for peer in range(PLANES):
                piece = total[block, peer * BLOCK : (peer + 1) * BLOCK, :]
                out_ref[peer, block * BLOCK : (block + 1) * BLOCK, :] = piece.astype(jnp.bfloat16)


def partial_factors(steps, coords, features):
    atoms = features.shape[0]
    return pl.pallas_call(
        factors_kernel,
        out_shape=jax.ShapeDtypeStruct((PLANES, COLUMN, F), jnp.bfloat16),
        grid=(atoms // TILE,),
        in_specs=[
            pl.BlockSpec((2, 8, FIRST), lambda t: (0, 0, 0)),
            pl.BlockSpec((3, TILE), lambda t: (0, t)),
            pl.BlockSpec((TILE, F), lambda t: (t, 0)),
        ],
        out_specs=pl.BlockSpec((PLANES, COLUMN, F), lambda t: (0, 0, 0)),
        scratch_shapes=[
            pltpu.VMEM((FIRST, TILE), jnp.float32),
            pltpu.VMEM((BLOCKS, PLANES * BLOCK, TILE), jnp.bfloat16),
            pltpu.VMEM((BLOCKS, PLANES * BLOCK, F), jnp.float32),
        ],
        cost_estimate=pl.CostEstimate(
            flops=2 * ALL_ROWS * atoms * F, bytes_accessed=atoms * F * 2, transcendentals=0
        ),
        name="factors",
    )(steps, coords, features)


def grid_spots(m0, m1, m2):
    flip = (m2 < 0) | ((m2 == 0) & ((m0 < 0) | ((m0 == 0) & (m1 < 0))))
    m0, m1, m2 = (jnp.where(flip, -m, m) for m in (m0, m1, m2))
    zero, last = m2 == 0, m1 == KMAX
    corner = last & (m0 == KMAX) & (m2 > 0)
    edge = zero & last & (m0 > 0)
    axis = zero & (m0 == 0)
    sheet = zero & (m0 > 0) & (m1 < KMAX)
    rim = last & (m0 < KMAX) & (m2 > 0)
    core = jnp.where(sheet, (m0 - 1) >> 2, (m2 - 1) & 1)
    block = jnp.where(sheet, (m0 - 1) & 3, (m2 - 1) >> 1)
    block = jnp.where(corner, 2, jnp.where(edge, 1, jnp.where(axis, 0, block)))
    core = jnp.where(corner | edge | axis, 0, core)
    peer = jnp.where(rim, m0 + KMAX, m1 + KMAX)
    peer = jnp.where(corner, m2 - 1, jnp.where(edge, m0 - 1, jnp.where(axis, m1, peer)))
    spot = jnp.where(sheet, SIDE, jnp.where(rim, SIDE + 1, m0 + KMAX))
    spot = jnp.where(corner | edge | axis, SIDE + 2, spot)
    return ((core * PLANES + peer) * BLOCKS + block) * OWN + spot


def weights_kernel(miller_ref, weights_ref, own_ref, other_ref):
    core, atom = lax.axis_index("wave") % 2, lax.axis_index("atom")
    plane, part = atom // 16 * 4 + atom % 4, atom // 4 % 2
    spots = grid_spots(miller_ref[0:1, :], miller_ref[1:2, :], miller_ref[2:3, :])
    row = lax.broadcasted_iota(jnp.int32, (POINTS, miller_ref.shape[1]), 0)
    weights = weights_ref[...]
    upper = weights.astype(jnp.bfloat16)
    lower = (weights - upper.astype(jnp.float32)).astype(jnp.bfloat16)
    for held, out_ref in ((core, own_ref), (1 - core, other_ref)):
        wanted = row + ((held * PLANES + plane) * 2 + part) * POINTS
        match = jnp.where(wanted == spots, 1.0, 0.0).astype(jnp.bfloat16)
        summed = jnp.dot(match, upper, preferred_element_type=jnp.float32)
        summed += jnp.dot(match, lower, preferred_element_type=jnp.float32)
        out_ref[...] = summed.astype(jnp.bfloat16)


def grid_weights(miller, weights):
    shape = jax.ShapeDtypeStruct((POINTS, F), jnp.bfloat16)
    return pl.pallas_call(
        weights_kernel,
        out_shape=(shape, shape),
        in_specs=[pl.BlockSpec(memory_space=pltpu.VMEM)] * 2,
        out_specs=(pl.BlockSpec(memory_space=pltpu.VMEM),) * 2,
        compiler_params=pltpu.CompilerParams(vmem_limit_bytes=8 << 20),
        cost_estimate=pl.CostEstimate(
            flops=8 * POINTS * 512 * F, bytes_accessed=512 * F * 4, transcendentals=0
        ),
        name="grid_weights",
    )(miller, weights)


def plane_sum_kernel(arrived_ref, out_ref):
    total = arrived_ref[0].astype(jnp.float32)
    for peer in range(1, PLANES):
        total += arrived_ref[peer].astype(jnp.float32)
    sent = total.astype(jnp.bfloat16)
    for peer in range(4):
        out_ref[peer] = sent[peer % 2 * HALF : (peer % 2 + 1) * HALF]


def plane_sum(arrived):
    return pl.pallas_call(
        plane_sum_kernel,
        out_shape=jax.ShapeDtypeStruct((4, HALF, F), jnp.bfloat16),
        in_specs=[pl.BlockSpec(memory_space=pltpu.VMEM)],
        out_specs=pl.BlockSpec(memory_space=pltpu.VMEM),
        compiler_params=pltpu.CompilerParams(vmem_limit_bytes=8 << 20),
        name="plane_sum",
    )(arrived)


def filter_kernel(arrived_ref, near_ref, far_ref, out_ref, total, filtered):
    total[...] = jnp.sum(arrived_ref[...].astype(jnp.float32), axis=0)
    weights = near_ref[...].astype(jnp.float32) + far_ref[...].astype(jnp.float32)
    extra = OWN - SIDE
    for block in range(BLOCKS // 2):
        for row, spot, count in ((0, 0, SIDE), (2 * SIDE, SIDE, extra)):
            start, weight = block * BLOCK + row, block * OWN + spot
            cosines, sines = total[start : start + count, :], total[start + count : start + 2 * count, :]
            power = jnp.sum(cosines * cosines + sines * sines, axis=1, keepdims=True) * (0.5 / F)
            scaled = weights[weight : weight + count] * (1.0 / jnp.sqrt(power + 1e-05))
            filtered[start : start + count, :] = cosines * scaled
            filtered[start + count : start + 2 * count, :] = sines * scaled
    column = filtered[...].astype(jnp.bfloat16)
    for peer in range(PLANES):
        out_ref[peer] = column


def filter_column(arrived, near, far):
    return pl.pallas_call(
        filter_kernel,
        out_shape=jax.ShapeDtypeStruct((PLANES, HALF, F), jnp.bfloat16),
        in_specs=[pl.BlockSpec(memory_space=pltpu.VMEM)] * 3,
        out_specs=pl.BlockSpec(memory_space=pltpu.VMEM),
        scratch_shapes=[pltpu.VMEM((HALF, F), jnp.float32)] * 2,
        compiler_params=pltpu.CompilerParams(vmem_limit_bytes=8 << 20),
        name="filter_column",
    )(arrived, near, far)


def tables_kernel(place_ref, steps_ref, own_ref, near_ref, out_ref):
    steps = steps_ref[0].astype(jnp.bfloat16)
    block = 128
    for side, coords_ref in enumerate((own_ref, near_ref)):
        parts = split_coords(coords_ref[...])
        for start in range(0, TILE, block):
            turns = lax.dot_general(
                parts[:, start : start + block], steps, OUTER, preferred_element_type=jnp.float32
            )
            rows = side * TILE + start
            out_ref[rows : rows + block, :] = cosine_of_turns(turns).astype(jnp.bfloat16)


def message_tables(place, steps, coords, near):
    width = 256
    return pl.pallas_call(
        tables_kernel,
        out_shape=jax.ShapeDtypeStruct((2 * TILE, ALL_ROWS), jnp.bfloat16),
        grid_spec=pltpu.PrefetchScalarGridSpec(
            num_scalar_prefetch=1,
            grid=(ALL_ROWS // width,),
            in_specs=[
                pl.BlockSpec((1, 8, width), lambda t, place: (place[3], 0, t)),
                pl.BlockSpec((3, TILE), lambda t, place: (0, place[2])),
                pl.BlockSpec((3, TILE), lambda t, place: (0, 0)),
            ],
            out_specs=pl.BlockSpec((2 * TILE, width), lambda t, place: (0, t)),
        ),
        compiler_params=pltpu.CompilerParams(vmem_limit_bytes=16 << 20),
        cost_estimate=pl.CostEstimate(
            flops=32 * TILE * ALL_ROWS, bytes_accessed=TILE * ALL_ROWS * 4, transcendentals=0
        ),
        name="message_tables",
    )(place, steps, coords, near)


def message_kernel(place_ref, tables_ref, filtered_ref, out_ref, *, far, own):
    half = TILE // 2
    core = place_ref[1] if own else 1 - place_ref[1]
    start = pl.multiple_of(core * half, half) + far * TILE
    tables = tables_ref[pl.ds(start, half), :]
    message = jnp.dot(tables, filtered_ref[...], preferred_element_type=jnp.float32)
    out_ref[...] = message.astype(out_ref.dtype)


def message_quarter(place, tables, filtered, far, own):
    half = TILE // 2
    kept = own and not far
    return pl.pallas_call(
        functools.partial(message_kernel, far=far, own=own),
        out_shape=jax.ShapeDtypeStruct((half, F), jnp.float32 if kept else jnp.bfloat16),
        in_specs=[
            pl.BlockSpec(memory_space=pltpu.SMEM),
            pl.BlockSpec(memory_space=pltpu.VMEM),
            pl.BlockSpec(memory_space=pltpu.VMEM),
        ],
        out_specs=pl.BlockSpec(memory_space=pltpu.VMEM),
        compiler_params=pltpu.CompilerParams(vmem_limit_bytes=16 << 20),
        cost_estimate=pl.CostEstimate(
            flops=2 * half * ALL_ROWS * F, bytes_accessed=4 * half * ALL_ROWS, transcendentals=0
        ),
    )(place, tables, filtered)


def update_kernel(
    place_ref, features_ref, own_ref, a_ref, b_ref, c_ref, gain_ref, w_in_ref, w_out_ref, out_ref
):
    message = own_ref[...]
    for part_ref in (a_ref, b_ref, c_ref):
        message += part_ref[...].astype(jnp.float32)
    updated = features_ref[...].astype(jnp.float32) + message * (1.0 / math.sqrt(K))
    power = jnp.mean(updated * updated, axis=1, keepdims=True)
    normed = (updated / jnp.sqrt(power + 1e-06) * gain_ref[...]).astype(jnp.bfloat16)
    hidden = jnp.dot(normed, w_in_ref[...], preferred_element_type=jnp.float32)
    hidden = (hidden / (1.0 + jnp.exp(-hidden))).astype(jnp.bfloat16)
    added = jnp.dot(hidden, w_out_ref[...], preferred_element_type=jnp.float32)
    out_ref[...] = (updated + added).astype(jnp.bfloat16)


def update(place, features, own, others, gain, w_in, w_out):
    half = TILE // 2
    return pl.pallas_call(
        update_kernel,
        out_shape=jax.ShapeDtypeStruct((half, F), jnp.bfloat16),
        grid_spec=pltpu.PrefetchScalarGridSpec(
            num_scalar_prefetch=1,
            grid=(1,),
            in_specs=[
                pl.BlockSpec((half, F), lambda t, place: (place[0], 0)),
                pl.BlockSpec((half, F), lambda t, place: (0, 0)),
                pl.BlockSpec((half, F), lambda t, place: (0, 0)),
                pl.BlockSpec((half, F), lambda t, place: (0, 0)),
                pl.BlockSpec((half, F), lambda t, place: (0, 0)),
                pl.BlockSpec((1, F), lambda t, place: (0, 0)),
                pl.BlockSpec((F, F), lambda t, place: (0, 0)),
                pl.BlockSpec((F, F), lambda t, place: (0, 0)),
            ],
            out_specs=pl.BlockSpec((half, F), lambda t, place: (0, 0)),
        ),
        compiler_params=pltpu.CompilerParams(vmem_limit_bytes=8 << 20),
        name="update",
    )(place, features, own, *others, gain, w_in, w_out)


def exchange(pieces, groups):
    return lax.all_to_all(
        pieces, AXES, split_axis=0, concat_axis=0, tiled=True, axis_index_groups=groups
    )


FIRST_STEPS = first_steps()
ALL_STEPS = all_steps()


def layer(features, coords, miller, filter_weights, norm_gain, w_in, w_out):
    factors = partial_factors(jnp.asarray(FIRST_STEPS), coords, features)
    factors, coords, miller = lax.optimization_barrier((factors, coords, miller))
    atom, wave = lax.axis_index("atom"), lax.axis_index("wave")
    core, high = wave % 2, wave // 2
    place = jnp.stack([wave, core, high, core * 2 + atom // 4 % 2]).astype(jnp.int32)
    arrived = exchange(factors, GROUPS_XY)
    weights, swapped = grid_weights(miller, filter_weights)
    weights += lax.ppermute(swapped, AXES, SWAP)
    weights += lax.ppermute(weights, AXES, OUTER_PAIRS)
    far_weights = lax.ppermute(weights, AXES, INNER_PAIRS)
    arrived, weights = lax.optimization_barrier((arrived, weights))
    sums = plane_sum(arrived)
    shares = exchange(sums, GROUPS_LO)
    filtered = filter_column(shares, weights, far_weights)
    filtered = exchange(filtered, GROUPS_XY).reshape(ALL_ROWS, F)
    near = lax.dynamic_slice_in_dim(coords, high * TILE, TILE, 1)
    near = lax.ppermute(near, AXES, LINE_SAME)
    tables = message_tables(place, jnp.asarray(ALL_STEPS), coords, near)
    quarter = functools.partial(message_quarter, place, tables, filtered)
    others = [
        lax.ppermute(quarter(far, own), AXES, pairs)
        for far, own, pairs in ((True, True, LINE_SAME), (True, False, LINE_CROSS), (False, False, SWAP))
    ]
    own = quarter(False, True)
    return update(place, features, own, others, norm_gain.reshape(1, F), w_in, w_out)


def solution(mesh):
    in_specs = (P("atom", None), P(None, "atom"), P(None, "wave"), P("wave", None), P(), P(), P())
    out_specs = P(("atom", "wave"), None)
    return jax.shard_map(layer, mesh=mesh, in_specs=in_specs, out_specs=out_specs, check_vma=False)
```

```python
import functools
import itertools
import math

import jax
import jax.numpy as jnp
import numpy as np
from jax import lax
from jax.experimental import pallas as pl
from jax.experimental.pallas import tpu as pltpu
from jax.sharding import PartitionSpec as P

K = 4096
KMAX = 8
SIDE = 2 * KMAX + 1
PLANES = 16
BLOCKS = 4
OWN = 20
BLOCK = 2 * OWN
COLUMN = BLOCKS * BLOCK
HALF = COLUMN // 2
ALL_ROWS = PLANES * HALF
MIDDLE = 8
POINTS = BLOCKS * OWN // 2
F = 256
HALVES = 256
TILE = 512
AXES = ("atom", "wave")
OUTER = (((0,), (0,)), ((), ()))


def device(y, z_lo, x, z_hi, core):
    return (((y * 4 + z_lo) * 4 + x) * 4 + z_hi) * 2 + core


FOUR = range(4)
TWO = range(2)
GROUPS_XY = [
    [device(y, l, x, h, c) for y in FOUR for x in FOUR] for l in FOUR for h in FOUR for c in TWO
]
GROUPS_LO = [
    [device(y, l, x, h, c) for l in FOUR] for y in FOUR for x in FOUR for h in FOUR for c in TWO
]
SWAP = [
    (device(y, l, x, h, c), device(y, l, x, h, 1 - c))
    for y, l, x, h, c in itertools.product(FOUR, FOUR, FOUR, FOUR, TWO)
]
OUTER_PAIRS = [
    (device(y, l, x, h, c), device(y, l, x, 3 - h, c))
    for y, l, x, h, c in itertools.product(FOUR, FOUR, FOUR, FOUR, TWO)
]
INNER_PAIRS = [
    (device(y, l, x, h, c), device(y, l, x, h ^ 1, c))
    for y, l, x, h, c in itertools.product(FOUR, FOUR, FOUR, FOUR, TWO)
]


LINE_SAME = [
    (device(y, l, x, h, c), device(y, l ^ 1, x, h, c))
    for y, l, x, h, c in itertools.product(FOUR, FOUR, FOUR, FOUR, TWO)
]
LINE_CROSS = [
    (device(y, l, x, h, c), device(y, l ^ 1, x, h, 1 - c))
    for y, l, x, h, c in itertools.product(FOUR, FOUR, FOUR, FOUR, TWO)
]


def row_line(core, block, spot):
    third = 2 * block + core + 1
    if spot < SIDE:
        return (spot - KMAX, 0, third), 1
    if spot == SIDE:
        return (4 * core + block + 1, 0, 0), 1
    if spot == SIDE + 1:
        return (0, KMAX, third), 0
    if (core, block) == (0, 0):
        return (0, MIDDLE, 0), 1
    if (core, block) == (0, 1):
        return (MIDDLE + 1, KMAX, 0), 0
    if (core, block) == (0, 2):
        return (KMAX, KMAX, MIDDLE + 1), 2
    return None


def column_of(vector, part):
    steps = np.zeros(8, np.float32)
    steps[0:3] = vector
    steps[3:6] = vector
    steps[6] = -0.25 * part
    return steps


def spot_of(row):
    if row < 2 * SIDE:
        return row % SIDE, row // SIDE
    extra = OWN - SIDE
    return SIDE + (row - 2 * SIDE) % extra, (row - 2 * SIDE) // extra


def row_steps(core, block, row, peer):
    spot, part = spot_of(row)
    line = row_line(core, block, spot)
    if line is None:
        return column_of((0, 0, 0), 1)
    vector = list(line[0])
    vector[line[1]] += peer - MIDDLE
    return column_of(vector, part)


def stride_steps(core, block, row):
    line = row_line(core, block, spot_of(row)[0])
    vector = [0, 0, 0]
    vector[1 if line is None else line[1]] = 1
    return column_of(vector, 0)


MAIN = 32
MIXED = range(MAIN, BLOCK)
AT = [0, 2 * BLOCK, 4 * BLOCK, 4 * BLOCK + 16]
STRIDES = 4 * BLOCK + 32
THIRD = STRIDES + 8 * BLOCKS
FIRST = THIRD + 8


def first_steps():
    out = np.zeros((2, 8, FIRST), np.float32)
    for core in range(2):
        columns = []
        for block in range(BLOCKS):
            rows = range(BLOCK) if block < 2 else MIXED
            columns += [row_steps(core, block, row, MIDDLE) for row in rows]
            columns += [row_steps(core, block, row, MIDDLE + 1) for row in rows]
        for block in range(BLOCKS):
            columns += [stride_steps(core, block, row) for row in MIXED]
        columns += [column_of((0, 0, 2), 0)] * 8
        out[core] = np.stack(columns, axis=1)
    return out


def all_steps():
    out = []
    for core, part in itertools.product(TWO, TWO):
        rows = itertools.product(range(PLANES), (2 * part, 2 * part + 1), range(BLOCK))
        out.append(np.stack([row_steps(core, b, r, q) for q, b, r in rows], axis=1))
    return np.stack(out)


def split_coords(coords):
    high = (coords >> 8).astype(jnp.float32) * (1.0 / 256.0)
    low = (coords & 255).astype(jnp.float32) * (1.0 / 65536.0)
    ones = jnp.ones((2, coords.shape[1]), jnp.float32)
    return jnp.concatenate([high, low, ones], axis=0).astype(jnp.bfloat16)


def cosine_coefficients():
    nodes = 0.125 + 0.125 * np.cos(np.pi * (np.arange(400) + 0.5) / 400)
    fit = np.polynomial.chebyshev.Chebyshev.fit(
        nodes, np.cos(2 * np.pi * np.sqrt(nodes)), 5, domain=[0, 0.25]
    )
    return [float(c) for c in fit.convert(kind=np.polynomial.Polynomial).coef]


COSINE = cosine_coefficients()


def cosine_of_turns(turns):
    left = turns - jnp.round(turns)
    square = left * left
    total = jnp.full_like(square, COSINE[-1])
    for c in COSINE[-2::-1]:
        total = total * square + c
    return total


def factors_kernel(
    steps_ref, coords_ref, features_ref, out_ref, features, first, tables, copied
):
    copy = pltpu.make_async_copy(features_ref, features, copied)
    copy.start()
    core = lax.axis_index("wave") % 2
    steps = steps_ref[core].astype(jnp.bfloat16)
    atoms = coords_ref.shape[1]
    for start in range(0, atoms, TILE):
        parts = split_coords(coords_ref[:, start : start + TILE])
        turns = lax.dot_general(steps, parts, OUTER, preferred_element_type=jnp.float32)
        first[:, start : start + TILE] = cosine_of_turns(turns)
    mains = {}
    for block in range(BLOCKS):
        for start in range(0, atoms, HALVES):
            lanes = pl.ds(start, HALVES)
            if block < 2:
                at = first[AT[block] : AT[block] + BLOCK, lanes]
                after = first[AT[block] + BLOCK : AT[block] + 2 * BLOCK, lanes]
            else:
                third = 2.0 * first[THIRD : THIRD + 1, lanes]
                main = [
                    third * near - far
                    for near, far in zip(mains[block - 1, start], mains[block - 2, start])
                ]
                mixed = [first[AT[block] + 8 * p : AT[block] + 8 * p + 8, lanes] for p in TWO]
                at, after = (jnp.concatenate([main[p], mixed[p]], axis=0) for p in TWO)
            mains[block, start] = at[:MAIN], after[:MAIN]
            mixed = 2.0 * first[STRIDES + 8 * block : STRIDES + 8 * block + 8, lanes]
            common = jnp.broadcast_to(mixed[0:1, :], (MAIN, HALVES))
            stride = jnp.concatenate([common, mixed], axis=0)
            held = {MIDDLE: at, MIDDLE + 1: after}
            for peer in range(MIDDLE, PLANES, 2):
                for later in (peer, peer + 1):
                    if later not in held:
                        held[later] = stride * held[later - 1] - held[later - 2]
                pair = jnp.concatenate([held[peer], held[peer + 1]], axis=0)
                tables[block, peer * BLOCK : (peer + 2) * BLOCK, lanes] = pair.astype(jnp.bfloat16)
            for peer in range(MIDDLE - 2, -1, -2):
                for earlier in (peer + 1, peer):
                    held[earlier] = stride * held[earlier + 1] - held[earlier + 2]
                pair = jnp.concatenate([held[peer], held[peer + 1]], axis=0)
                tables[block, peer * BLOCK : (peer + 2) * BLOCK, lanes] = pair.astype(jnp.bfloat16)
        if block == 0:
            copy.wait()
        summed = jnp.dot(tables[block], features[...], preferred_element_type=jnp.float32)
        for peer in range(PLANES):
            piece = summed[peer * BLOCK : (peer + 1) * BLOCK, :].astype(jnp.bfloat16)
            out_ref[peer, block * BLOCK : (block + 1) * BLOCK, :] = piece


def partial_factors(steps, coords, features):
    atoms = features.shape[0]
    return pl.pallas_call(
        factors_kernel,
        out_shape=jax.ShapeDtypeStruct((PLANES, COLUMN, F), jnp.bfloat16),
        in_specs=[
            pl.BlockSpec(memory_space=pltpu.VMEM),
            pl.BlockSpec(memory_space=pltpu.VMEM),
            pl.BlockSpec(memory_space=pl.ANY),
        ],
        out_specs=pl.BlockSpec(memory_space=pltpu.VMEM),
        scratch_shapes=[
            pltpu.VMEM((atoms, F), jnp.bfloat16),
            pltpu.VMEM((FIRST, atoms), jnp.float32),
            pltpu.VMEM((BLOCKS, PLANES * BLOCK, atoms), jnp.bfloat16),
            pltpu.SemaphoreType.DMA,
        ],
        cost_estimate=pl.CostEstimate(
            flops=2 * PLANES * COLUMN * atoms * F, bytes_accessed=atoms * F * 2, transcendentals=0
        ),
        name="factors",
    )(steps, coords, features)


def grid_spots(m0, m1, m2):
    flip = (m2 < 0) | ((m2 == 0) & ((m0 < 0) | ((m0 == 0) & (m1 < 0))))
    m0, m1, m2 = (jnp.where(flip, -m, m) for m in (m0, m1, m2))
    zero, last = m2 == 0, m1 == KMAX
    corner = last & (m0 == KMAX) & (m2 > 0)
    edge = zero & last & (m0 > 0)
    axis = zero & (m0 == 0)
    sheet = zero & (m0 > 0) & (m1 < KMAX)
    rim = last & (m0 < KMAX) & (m2 > 0)
    core = jnp.where(sheet, (m0 - 1) >> 2, (m2 - 1) & 1)
    block = jnp.where(sheet, (m0 - 1) & 3, (m2 - 1) >> 1)
    block = jnp.where(corner, 2, jnp.where(edge, 1, jnp.where(axis, 0, block)))
    core = jnp.where(corner | edge | axis, 0, core)
    peer = jnp.where(rim, m0 + KMAX, m1 + KMAX)
    peer = jnp.where(corner, m2 - 1, jnp.where(edge, m0 - 1, jnp.where(axis, m1, peer)))
    spot = jnp.where(sheet, SIDE, jnp.where(rim, SIDE + 1, m0 + KMAX))
    spot = jnp.where(corner | edge | axis, SIDE + 2, spot)
    return ((core * PLANES + peer) * BLOCKS + block) * OWN + spot


def weights_kernel(miller_ref, weights_ref, own_ref, other_ref):
    core, atom = lax.axis_index("wave") % 2, lax.axis_index("atom")
    plane, part = atom // 16 * 4 + atom % 4, atom // 4 % 2
    spots = grid_spots(miller_ref[0:1, :], miller_ref[1:2, :], miller_ref[2:3, :])
    row = lax.broadcasted_iota(jnp.int32, (POINTS, miller_ref.shape[1]), 0)
    weights = weights_ref[...]
    upper = weights.astype(jnp.bfloat16)
    lower = (weights - upper.astype(jnp.float32)).astype(jnp.bfloat16)
    for held, out_ref in ((core, own_ref), (1 - core, other_ref)):
        wanted = row + ((held * PLANES + plane) * 2 + part) * POINTS
        match = jnp.where(wanted == spots, 1.0, 0.0).astype(jnp.bfloat16)
        summed = jnp.dot(match, upper, preferred_element_type=jnp.float32)
        summed += jnp.dot(match, lower, preferred_element_type=jnp.float32)
        out_ref[...] = summed.astype(jnp.bfloat16)


def grid_weights(miller, weights):
    shape = jax.ShapeDtypeStruct((POINTS, F), jnp.bfloat16)
    return pl.pallas_call(
        weights_kernel,
        out_shape=(shape, shape),
        in_specs=[pl.BlockSpec(memory_space=pltpu.VMEM)] * 2,
        out_specs=(pl.BlockSpec(memory_space=pltpu.VMEM),) * 2,
        compiler_params=pltpu.CompilerParams(vmem_limit_bytes=8 << 20),
        cost_estimate=pl.CostEstimate(
            flops=8 * POINTS * 512 * F, bytes_accessed=512 * F * 4, transcendentals=0
        ),
        name="grid_weights",
    )(miller, weights)


def plane_sum_kernel(arrived_ref, out_ref):
    total = arrived_ref[0].astype(jnp.float32)
    for peer in range(1, PLANES):
        total += arrived_ref[peer].astype(jnp.float32)
    sent = total.astype(jnp.bfloat16)
    for peer in range(4):
        out_ref[peer] = sent[peer % 2 * HALF : (peer % 2 + 1) * HALF]


def plane_sum(arrived):
    return pl.pallas_call(
        plane_sum_kernel,
        out_shape=jax.ShapeDtypeStruct((4, HALF, F), jnp.bfloat16),
        in_specs=[pl.BlockSpec(memory_space=pltpu.VMEM)],
        out_specs=pl.BlockSpec(memory_space=pltpu.VMEM),
        compiler_params=pltpu.CompilerParams(vmem_limit_bytes=8 << 20),
        name="plane_sum",
    )(arrived)


def filter_kernel(arrived_ref, near_ref, far_ref, out_ref, total, filtered):
    total[...] = jnp.sum(arrived_ref[...].astype(jnp.float32), axis=0)
    weights = near_ref[...].astype(jnp.float32) + far_ref[...].astype(jnp.float32)
    extra = OWN - SIDE
    for block in range(BLOCKS // 2):
        for row, spot, count in ((0, 0, SIDE), (2 * SIDE, SIDE, extra)):
            start, weight = block * BLOCK + row, block * OWN + spot
            cosines, sines = total[start : start + count, :], total[start + count : start + 2 * count, :]
            power = jnp.sum(cosines * cosines + sines * sines, axis=1, keepdims=True) * (0.5 / F)
            scaled = weights[weight : weight + count] * (1.0 / jnp.sqrt(power + 1e-05))
            filtered[start : start + count, :] = cosines * scaled
            filtered[start + count : start + 2 * count, :] = sines * scaled
    column = filtered[...].astype(jnp.bfloat16)
    for peer in range(PLANES):
        out_ref[peer] = column


def filter_column(arrived, near, far):
    return pl.pallas_call(
        filter_kernel,
        out_shape=jax.ShapeDtypeStruct((PLANES, HALF, F), jnp.bfloat16),
        in_specs=[pl.BlockSpec(memory_space=pltpu.VMEM)] * 3,
        out_specs=pl.BlockSpec(memory_space=pltpu.VMEM),
        scratch_shapes=[pltpu.VMEM((HALF, F), jnp.float32)] * 2,
        compiler_params=pltpu.CompilerParams(vmem_limit_bytes=8 << 20),
        name="filter_column",
    )(arrived, near, far)


def tables_kernel(place_ref, steps_ref, own_ref, near_ref, out_ref):
    steps = steps_ref[0].astype(jnp.bfloat16)
    block = 128
    for side, coords_ref in enumerate((own_ref, near_ref)):
        parts = split_coords(coords_ref[...])
        for start in range(0, TILE, block):
            turns = lax.dot_general(
                parts[:, start : start + block], steps, OUTER, preferred_element_type=jnp.float32
            )
            rows = side * TILE + start
            out_ref[rows : rows + block, :] = cosine_of_turns(turns).astype(jnp.bfloat16)


def message_tables(place, steps, coords, near):
    width = 256
    return pl.pallas_call(
        tables_kernel,
        out_shape=jax.ShapeDtypeStruct((2 * TILE, ALL_ROWS), jnp.bfloat16),
        grid_spec=pltpu.PrefetchScalarGridSpec(
            num_scalar_prefetch=1,
            grid=(ALL_ROWS // width,),
            in_specs=[
                pl.BlockSpec((1, 8, width), lambda t, place: (place[3], 0, t)),
                pl.BlockSpec((3, TILE), lambda t, place: (0, place[2])),
                pl.BlockSpec((3, TILE), lambda t, place: (0, 0)),
            ],
            out_specs=pl.BlockSpec((2 * TILE, width), lambda t, place: (0, t)),
        ),
        compiler_params=pltpu.CompilerParams(vmem_limit_bytes=16 << 20),
        cost_estimate=pl.CostEstimate(
            flops=32 * TILE * ALL_ROWS, bytes_accessed=TILE * ALL_ROWS * 4, transcendentals=0
        ),
        name="message_tables",
    )(place, steps, coords, near)


def message_kernel(place_ref, tables_ref, filtered_ref, out_ref, *, far, own):
    half = TILE // 2
    core = place_ref[1] if own else 1 - place_ref[1]
    start = pl.multiple_of(core * half, half) + far * TILE
    tables = tables_ref[pl.ds(start, half), :]
    message = jnp.dot(tables, filtered_ref[...], preferred_element_type=jnp.float32)
    out_ref[...] = message.astype(out_ref.dtype)


def message_quarter(place, tables, filtered, far, own):
    half = TILE // 2
    kept = own and not far
    return pl.pallas_call(
        functools.partial(message_kernel, far=far, own=own),
        out_shape=jax.ShapeDtypeStruct((half, F), jnp.float32 if kept else jnp.bfloat16),
        in_specs=[
            pl.BlockSpec(memory_space=pltpu.SMEM),
            pl.BlockSpec(memory_space=pltpu.VMEM),
            pl.BlockSpec(memory_space=pltpu.VMEM),
        ],
        out_specs=pl.BlockSpec(memory_space=pltpu.VMEM),
        compiler_params=pltpu.CompilerParams(vmem_limit_bytes=16 << 20),
        cost_estimate=pl.CostEstimate(
            flops=2 * half * ALL_ROWS * F, bytes_accessed=4 * half * ALL_ROWS, transcendentals=0
        ),
    )(place, tables, filtered)


def update_kernel(
    place_ref, features_ref, own_ref, a_ref, b_ref, c_ref, gain_ref, w_in_ref, w_out_ref, out_ref
):
    message = own_ref[...]
    for part_ref in (a_ref, b_ref, c_ref):
        message += part_ref[...].astype(jnp.float32)
    updated = features_ref[...].astype(jnp.float32) + message * (1.0 / math.sqrt(K))
    power = jnp.mean(updated * updated, axis=1, keepdims=True)
    normed = (updated / jnp.sqrt(power + 1e-06) * gain_ref[...]).astype(jnp.bfloat16)
    hidden = jnp.dot(normed, w_in_ref[...], preferred_element_type=jnp.float32)
    hidden = (hidden / (1.0 + jnp.exp(-hidden))).astype(jnp.bfloat16)
    added = jnp.dot(hidden, w_out_ref[...], preferred_element_type=jnp.float32)
    out_ref[...] = (updated + added).astype(jnp.bfloat16)


def update(place, features, own, others, gain, w_in, w_out):
    half = TILE // 2
    return pl.pallas_call(
        update_kernel,
        out_shape=jax.ShapeDtypeStruct((half, F), jnp.bfloat16),
        grid_spec=pltpu.PrefetchScalarGridSpec(
            num_scalar_prefetch=1,
            grid=(1,),
            in_specs=[
                pl.BlockSpec((half, F), lambda t, place: (place[0], 0)),
                pl.BlockSpec((half, F), lambda t, place: (0, 0)),
                pl.BlockSpec((half, F), lambda t, place: (0, 0)),
                pl.BlockSpec((half, F), lambda t, place: (0, 0)),
                pl.BlockSpec((half, F), lambda t, place: (0, 0)),
                pl.BlockSpec((1, F), lambda t, place: (0, 0)),
                pl.BlockSpec((F, F), lambda t, place: (0, 0)),
                pl.BlockSpec((F, F), lambda t, place: (0, 0)),
            ],
            out_specs=pl.BlockSpec((half, F), lambda t, place: (0, 0)),
        ),
        compiler_params=pltpu.CompilerParams(vmem_limit_bytes=8 << 20),
        name="update",
    )(place, features, own, *others, gain, w_in, w_out)


def exchange(pieces, groups):
    return lax.all_to_all(
        pieces, AXES, split_axis=0, concat_axis=0, tiled=True, axis_index_groups=groups
    )


FIRST_STEPS = first_steps()
ALL_STEPS = all_steps()


def layer(features, coords, miller, filter_weights, norm_gain, w_in, w_out):
    factors = partial_factors(jnp.asarray(FIRST_STEPS), coords, features)
    factors, coords, miller = lax.optimization_barrier((factors, coords, miller))
    atom, wave = lax.axis_index("atom"), lax.axis_index("wave")
    core, high = wave % 2, wave // 2
    place = jnp.stack([wave, core, high, core * 2 + atom // 4 % 2]).astype(jnp.int32)
    arrived = exchange(factors, GROUPS_XY)
    weights, swapped = grid_weights(miller, filter_weights)
    weights += lax.ppermute(swapped, AXES, SWAP)
    weights += lax.ppermute(weights, AXES, OUTER_PAIRS)
    far_weights = lax.ppermute(weights, AXES, INNER_PAIRS)
    arrived, weights = lax.optimization_barrier((arrived, weights))
    sums = plane_sum(arrived)
    sums, coords = lax.optimization_barrier((sums, coords))
    near = lax.dynamic_slice_in_dim(coords, high * TILE, TILE, 1)
    shares = exchange(sums, GROUPS_LO)
    near = lax.ppermute(near, AXES, LINE_SAME)
    shares, near = lax.optimization_barrier((shares, near))
    filtered = filter_column(shares, weights, far_weights)
    filtered = exchange(filtered, GROUPS_XY).reshape(ALL_ROWS, F)
    tables = message_tables(place, jnp.asarray(ALL_STEPS), coords, near)
    quarter = functools.partial(message_quarter, place, tables, filtered)
    others = []
    for far, own, pairs in ((True, True, LINE_SAME), (True, False, LINE_CROSS), (False, False, SWAP)):
        part = quarter(far, own)
        others.append(lax.ppermute(part, AXES, pairs))
    own = quarter(False, True)
    return update(place, features, own, others, norm_gain.reshape(1, F), w_in, w_out)


def solution(mesh):
    in_specs = (P("atom", None), P(None, "atom"), P(None, "wave"), P("wave", None), P(), P(), P())
    out_specs = P(("atom", "wave"), None)
    return jax.shard_map(layer, mesh=mesh, in_specs=in_specs, out_specs=out_specs, check_vma=False)
```

```python
import functools
import itertools
import math

import jax
import jax.numpy as jnp
import numpy as np
from jax import lax
from jax.experimental import pallas as pl
from jax.experimental.pallas import tpu as pltpu
from jax.sharding import PartitionSpec as P

K = 4096
KMAX = 8
SIDE = 2 * KMAX + 1
PLANES = 16
BLOCKS = 4
OWN = 20
BLOCK = 2 * OWN
COLUMN = BLOCKS * BLOCK
HALF = COLUMN // 2
ALL_ROWS = PLANES * HALF
MIDDLE = 8
POINTS = BLOCKS * OWN // 2
F = 256
HALVES = 256
TILE = 512
AXES = ("atom", "wave")
OUTER = (((0,), (0,)), ((), ()))


def device(y, z_lo, x, z_hi, core):
    return (((y * 4 + z_lo) * 4 + x) * 4 + z_hi) * 2 + core


FOUR = range(4)
TWO = range(2)
GROUPS_XY = [
    [device(y, l, x, h, c) for y in FOUR for x in FOUR] for l in FOUR for h in FOUR for c in TWO
]
GROUPS_LO = [
    [device(y, l, x, h, c) for l in FOUR] for y in FOUR for x in FOUR for h in FOUR for c in TWO
]
SWAP = [
    (device(y, l, x, h, c), device(y, l, x, h, 1 - c))
    for y, l, x, h, c in itertools.product(FOUR, FOUR, FOUR, FOUR, TWO)
]
OUTER_PAIRS = [
    (device(y, l, x, h, c), device(y, l, x, 3 - h, c))
    for y, l, x, h, c in itertools.product(FOUR, FOUR, FOUR, FOUR, TWO)
]
INNER_PAIRS = [
    (device(y, l, x, h, c), device(y, l, x, h ^ 1, c))
    for y, l, x, h, c in itertools.product(FOUR, FOUR, FOUR, FOUR, TWO)
]


LINE_SAME = [
    (device(y, l, x, h, c), device(y, l ^ 1, x, h, c))
    for y, l, x, h, c in itertools.product(FOUR, FOUR, FOUR, FOUR, TWO)
]
LINE_CROSS = [
    (device(y, l, x, h, c), device(y, l ^ 1, x, h, 1 - c))
    for y, l, x, h, c in itertools.product(FOUR, FOUR, FOUR, FOUR, TWO)
]


def row_line(core, block, spot):
    third = 2 * block + core + 1
    if spot < SIDE:
        return (spot - KMAX, 0, third), 1
    if spot == SIDE:
        return (4 * core + block + 1, 0, 0), 1
    if spot == SIDE + 1:
        return (0, KMAX, third), 0
    if (core, block) == (0, 0):
        return (0, MIDDLE, 0), 1
    if (core, block) == (0, 1):
        return (MIDDLE + 1, KMAX, 0), 0
    if (core, block) == (0, 2):
        return (KMAX, KMAX, MIDDLE + 1), 2
    return None


def column_of(vector, part):
    steps = np.zeros(8, np.float32)
    steps[0:3] = vector
    steps[3:6] = vector
    steps[6] = -0.25 * part
    return steps


def spot_of(row):
    if row < 2 * SIDE:
        return row % SIDE, row // SIDE
    extra = OWN - SIDE
    return SIDE + (row - 2 * SIDE) % extra, (row - 2 * SIDE) // extra


def row_steps(core, block, row, peer):
    spot, part = spot_of(row)
    line = row_line(core, block, spot)
    if line is None:
        return column_of((0, 0, 0), 1)
    vector = list(line[0])
    vector[line[1]] += peer - MIDDLE
    return column_of(vector, part)


def stride_steps(core, block, row):
    line = row_line(core, block, spot_of(row)[0])
    vector = [0, 0, 0]
    vector[1 if line is None else line[1]] = 1
    return column_of(vector, 0)


MAIN = 32
MIXED = range(MAIN, BLOCK)
AT = [0, 2 * BLOCK, 4 * BLOCK, 4 * BLOCK + 16]
STRIDES = 4 * BLOCK + 32
THIRD = STRIDES + 8 * BLOCKS
FIRST = THIRD + 8


def first_steps():
    out = np.zeros((2, 8, FIRST), np.float32)
    for core in range(2):
        columns = []
        for block in range(BLOCKS):
            rows = range(BLOCK) if block < 2 else MIXED
            columns += [row_steps(core, block, row, MIDDLE) for row in rows]
            columns += [row_steps(core, block, row, MIDDLE + 1) for row in rows]
        for block in range(BLOCKS):
            columns += [stride_steps(core, block, row) for row in MIXED]
        columns += [column_of((0, 0, 2), 0)] * 8
        out[core] = np.stack(columns, axis=1)
    return out


def all_steps():
    out = []
    for core, part in itertools.product(TWO, TWO):
        rows = itertools.product(range(PLANES), (2 * part, 2 * part + 1), range(BLOCK))
        out.append(np.stack([row_steps(core, b, r, q) for q, b, r in rows], axis=1))
    return np.stack(out)


def split_coords(coords):
    high = (coords >> 8).astype(jnp.float32) * (1.0 / 256.0)
    low = (coords & 255).astype(jnp.float32) * (1.0 / 65536.0)
    ones = jnp.ones((2, coords.shape[1]), jnp.float32)
    return jnp.concatenate([high, low, ones], axis=0).astype(jnp.bfloat16)


def cosine_coefficients():
    nodes = 0.125 + 0.125 * np.cos(np.pi * (np.arange(400) + 0.5) / 400)
    fit = np.polynomial.chebyshev.Chebyshev.fit(
        nodes, np.cos(2 * np.pi * np.sqrt(nodes)), 5, domain=[0, 0.25]
    )
    return [float(c) for c in fit.convert(kind=np.polynomial.Polynomial).coef]


COSINE = cosine_coefficients()


def cosine_of_turns(turns):
    left = turns - jnp.round(turns)
    square = left * left
    total = jnp.full_like(square, COSINE[-1])
    for c in COSINE[-2::-1]:
        total = total * square + c
    return total


def factors_kernel(
    steps_ref, coords_ref, features_ref, out_ref, features, first, tables, copied
):
    copy = pltpu.make_async_copy(features_ref, features, copied)
    copy.start()
    core = lax.axis_index("wave") % 2
    steps = steps_ref[core].astype(jnp.bfloat16)
    atoms = coords_ref.shape[1]
    for start in range(0, atoms, TILE):
        parts = split_coords(coords_ref[:, start : start + TILE])
        turns = lax.dot_general(steps, parts, OUTER, preferred_element_type=jnp.float32)
        first[:, start : start + TILE] = cosine_of_turns(turns)
    mains = {}
    for block in range(BLOCKS):
        for start in range(0, atoms, HALVES):
            lanes = pl.ds(start, HALVES)
            if block < 2:
                at = first[AT[block] : AT[block] + BLOCK, lanes]
                after = first[AT[block] + BLOCK : AT[block] + 2 * BLOCK, lanes]
            else:
                third = 2.0 * first[THIRD : THIRD + 1, lanes]
                main = [
                    third * near - far
                    for near, far in zip(mains[block - 1, start], mains[block - 2, start])
                ]
                mixed = [first[AT[block] + 8 * p : AT[block] + 8 * p + 8, lanes] for p in TWO]
                at, after = (jnp.concatenate([main[p], mixed[p]], axis=0) for p in TWO)
            mains[block, start] = at[:MAIN], after[:MAIN]
            mixed = 2.0 * first[STRIDES + 8 * block : STRIDES + 8 * block + 8, lanes]
            common = jnp.broadcast_to(mixed[0:1, :], (MAIN, HALVES))
            stride = jnp.concatenate([common, mixed], axis=0)
            held = {MIDDLE: at, MIDDLE + 1: after}
            for peer in range(MIDDLE, PLANES, 2):
                for later in (peer, peer + 1):
                    if later not in held:
                        held[later] = stride * held[later - 1] - held[later - 2]
                pair = jnp.concatenate([held[peer], held[peer + 1]], axis=0)
                tables[block, peer * BLOCK : (peer + 2) * BLOCK, lanes] = pair.astype(jnp.bfloat16)
            for peer in range(MIDDLE - 2, -1, -2):
                for earlier in (peer + 1, peer):
                    held[earlier] = stride * held[earlier + 1] - held[earlier + 2]
                pair = jnp.concatenate([held[peer], held[peer + 1]], axis=0)
                tables[block, peer * BLOCK : (peer + 2) * BLOCK, lanes] = pair.astype(jnp.bfloat16)
        if block == 0:
            copy.wait()
        summed = jnp.dot(tables[block], features[...], preferred_element_type=jnp.float32)
        for peer in range(PLANES):
            piece = summed[peer * BLOCK : (peer + 1) * BLOCK, :].astype(jnp.bfloat16)
            out_ref[peer, block * BLOCK : (block + 1) * BLOCK, :] = piece


def partial_factors(steps, coords, features):
    atoms = features.shape[0]
    return pl.pallas_call(
        factors_kernel,
        out_shape=jax.ShapeDtypeStruct((PLANES, COLUMN, F), jnp.bfloat16),
        in_specs=[
            pl.BlockSpec(memory_space=pltpu.VMEM),
            pl.BlockSpec(memory_space=pltpu.VMEM),
            pl.BlockSpec(memory_space=pl.ANY),
        ],
        out_specs=pl.BlockSpec(memory_space=pltpu.VMEM),
        scratch_shapes=[
            pltpu.VMEM((atoms, F), jnp.bfloat16),
            pltpu.VMEM((FIRST, atoms), jnp.float32),
            pltpu.VMEM((BLOCKS, PLANES * BLOCK, atoms), jnp.bfloat16),
            pltpu.SemaphoreType.DMA,
        ],
        cost_estimate=pl.CostEstimate(
            flops=2 * PLANES * COLUMN * atoms * F, bytes_accessed=atoms * F * 2, transcendentals=0
        ),
        name="factors",
    )(steps, coords, features)


def grid_spots(m0, m1, m2):
    flip = (m2 < 0) | ((m2 == 0) & ((m0 < 0) | ((m0 == 0) & (m1 < 0))))
    m0, m1, m2 = (jnp.where(flip, -m, m) for m in (m0, m1, m2))
    zero, last = m2 == 0, m1 == KMAX
    corner = last & (m0 == KMAX) & (m2 > 0)
    edge = zero & last & (m0 > 0)
    axis = zero & (m0 == 0)
    sheet = zero & (m0 > 0) & (m1 < KMAX)
    rim = last & (m0 < KMAX) & (m2 > 0)
    core = jnp.where(sheet, (m0 - 1) >> 2, (m2 - 1) & 1)
    block = jnp.where(sheet, (m0 - 1) & 3, (m2 - 1) >> 1)
    block = jnp.where(corner, 2, jnp.where(edge, 1, jnp.where(axis, 0, block)))
    core = jnp.where(corner | edge | axis, 0, core)
    peer = jnp.where(rim, m0 + KMAX, m1 + KMAX)
    peer = jnp.where(corner, m2 - 1, jnp.where(edge, m0 - 1, jnp.where(axis, m1, peer)))
    spot = jnp.where(sheet, SIDE, jnp.where(rim, SIDE + 1, m0 + KMAX))
    spot = jnp.where(corner | edge | axis, SIDE + 2, spot)
    return ((core * PLANES + peer) * BLOCKS + block) * OWN + spot


def weights_kernel(miller_ref, weights_ref, out_ref):
    core, atom = lax.axis_index("wave") % 2, lax.axis_index("atom")
    plane, part = atom // 16 * 4 + atom % 4, atom // 4 % 2
    spots = grid_spots(miller_ref[0:1, :], miller_ref[1:2, :], miller_ref[2:3, :])
    row = lax.broadcasted_iota(jnp.int32, (POINTS, miller_ref.shape[1]), 0)
    weights = weights_ref[...]
    upper = weights.astype(jnp.bfloat16)
    lower = (weights - upper.astype(jnp.float32)).astype(jnp.bfloat16)
    for turn, held in enumerate((core, 1 - core)):
        wanted = row + ((held * PLANES + plane) * 2 + part) * POINTS
        match = jnp.where(wanted == spots, 1.0, 0.0).astype(jnp.bfloat16)
        summed = jnp.dot(match, upper, preferred_element_type=jnp.float32)
        summed += jnp.dot(match, lower, preferred_element_type=jnp.float32)
        out_ref[turn * POINTS : (turn + 1) * POINTS, :] = summed.astype(jnp.bfloat16)


def grid_weights(miller, weights):
    return pl.pallas_call(
        weights_kernel,
        out_shape=jax.ShapeDtypeStruct((2 * POINTS, F), jnp.bfloat16),
        in_specs=[pl.BlockSpec(memory_space=pltpu.VMEM)] * 2,
        out_specs=pl.BlockSpec(memory_space=pltpu.VMEM),
        compiler_params=pltpu.CompilerParams(vmem_limit_bytes=8 << 20),
        cost_estimate=pl.CostEstimate(
            flops=8 * POINTS * 512 * F, bytes_accessed=512 * F * 4, transcendentals=0
        ),
        name="grid_weights",
    )(miller, weights)


def plane_sum_kernel(arrived_ref, out_ref):
    total = arrived_ref[0].astype(jnp.float32)
    for peer in range(1, PLANES):
        total += arrived_ref[peer].astype(jnp.float32)
    sent = total.astype(jnp.bfloat16)
    for peer in range(4):
        out_ref[peer] = sent[peer % 2 * HALF : (peer % 2 + 1) * HALF]


def plane_sum(arrived):
    return pl.pallas_call(
        plane_sum_kernel,
        out_shape=jax.ShapeDtypeStruct((4, HALF, F), jnp.bfloat16),
        in_specs=[pl.BlockSpec(memory_space=pltpu.VMEM)],
        out_specs=pl.BlockSpec(memory_space=pltpu.VMEM),
        compiler_params=pltpu.CompilerParams(vmem_limit_bytes=8 << 20),
        name="plane_sum",
    )(arrived)


def filter_kernel(arrived_ref, near_ref, far_ref, out_ref, total, filtered):
    total[...] = jnp.sum(arrived_ref[...].astype(jnp.float32), axis=0)
    weights = near_ref[...].astype(jnp.float32) + far_ref[...].astype(jnp.float32)
    extra = OWN - SIDE
    for block in range(BLOCKS // 2):
        for row, spot, count in ((0, 0, SIDE), (2 * SIDE, SIDE, extra)):
            start, weight = block * BLOCK + row, block * OWN + spot
            cosines, sines = total[start : start + count, :], total[start + count : start + 2 * count, :]
            power = jnp.sum(cosines * cosines + sines * sines, axis=1, keepdims=True) * (0.5 / F)
            scaled = weights[weight : weight + count] * (1.0 / jnp.sqrt(power + 1e-05))
            filtered[start : start + count, :] = cosines * scaled
            filtered[start + count : start + 2 * count, :] = sines * scaled
    column = filtered[...].astype(jnp.bfloat16)
    for peer in range(PLANES):
        out_ref[peer] = column


def filter_column(arrived, near, far):
    return pl.pallas_call(
        filter_kernel,
        out_shape=jax.ShapeDtypeStruct((PLANES, HALF, F), jnp.bfloat16),
        in_specs=[pl.BlockSpec(memory_space=pltpu.VMEM)] * 3,
        out_specs=pl.BlockSpec(memory_space=pltpu.VMEM),
        scratch_shapes=[pltpu.VMEM((HALF, F), jnp.float32)] * 2,
        compiler_params=pltpu.CompilerParams(vmem_limit_bytes=8 << 20),
        name="filter_column",
    )(arrived, near, far)


def tables_kernel(place_ref, steps_ref, own_ref, near_ref, out_ref):
    steps = steps_ref[0].astype(jnp.bfloat16)
    block = 128
    for side, coords_ref in enumerate((own_ref, near_ref)):
        parts = split_coords(coords_ref[...])
        for start in range(0, TILE, block):
            turns = lax.dot_general(
                parts[:, start : start + block], steps, OUTER, preferred_element_type=jnp.float32
            )
            rows = side * TILE + start
            out_ref[rows : rows + block, :] = cosine_of_turns(turns).astype(jnp.bfloat16)


def message_tables(place, steps, coords, near):
    width = 256
    return pl.pallas_call(
        tables_kernel,
        out_shape=jax.ShapeDtypeStruct((2 * TILE, ALL_ROWS), jnp.bfloat16),
        grid_spec=pltpu.PrefetchScalarGridSpec(
            num_scalar_prefetch=1,
            grid=(ALL_ROWS // width,),
            in_specs=[
                pl.BlockSpec((1, 8, width), lambda t, place: (place[3], 0, t)),
                pl.BlockSpec((3, TILE), lambda t, place: (0, place[2])),
                pl.BlockSpec((3, TILE), lambda t, place: (0, 0)),
            ],
            out_specs=pl.BlockSpec((2 * TILE, width), lambda t, place: (0, t)),
        ),
        compiler_params=pltpu.CompilerParams(vmem_limit_bytes=16 << 20),
        cost_estimate=pl.CostEstimate(
            flops=32 * TILE * ALL_ROWS, bytes_accessed=TILE * ALL_ROWS * 4, transcendentals=0
        ),
        name="message_tables",
    )(place, steps, coords, near)


def message_kernel(place_ref, tables_ref, filtered_ref, out_ref, *, far, own):
    half = TILE // 2
    core = place_ref[1] if own else 1 - place_ref[1]
    start = pl.multiple_of(core * half, half) + far * TILE
    tables = tables_ref[pl.ds(start, half), :]
    message = jnp.dot(tables, filtered_ref[...], preferred_element_type=jnp.float32)
    out_ref[...] = message.astype(out_ref.dtype)


def message_quarter(place, tables, filtered, far, own):
    half = TILE // 2
    kept = own and not far
    return pl.pallas_call(
        functools.partial(message_kernel, far=far, own=own),
        out_shape=jax.ShapeDtypeStruct((half, F), jnp.float32 if kept else jnp.bfloat16),
        in_specs=[
            pl.BlockSpec(memory_space=pltpu.SMEM),
            pl.BlockSpec(memory_space=pltpu.VMEM),
            pl.BlockSpec(memory_space=pltpu.VMEM),
        ],
        out_specs=pl.BlockSpec(memory_space=pltpu.VMEM),
        compiler_params=pltpu.CompilerParams(vmem_limit_bytes=16 << 20),
        cost_estimate=pl.CostEstimate(
            flops=2 * half * ALL_ROWS * F, bytes_accessed=4 * half * ALL_ROWS, transcendentals=0
        ),
    )(place, tables, filtered)


def update_kernel(
    place_ref, features_ref, own_ref, a_ref, b_ref, c_ref, gain_ref, w_in_ref, w_out_ref, out_ref
):
    gain, w_in, w_out = gain_ref[...], w_in_ref[...], w_out_ref[...]
    chunk = own_ref.shape[0] // 4
    for start in range(0, own_ref.shape[0], chunk):
        rows = pl.ds(start, chunk)
        message = own_ref[rows, :]
        for part_ref in (a_ref, b_ref, c_ref):
            message += part_ref[rows, :].astype(jnp.float32)
        updated = features_ref[rows, :].astype(jnp.float32) + message * (1.0 / math.sqrt(K))
        power = jnp.mean(updated * updated, axis=1, keepdims=True)
        normed = (updated / jnp.sqrt(power + 1e-06) * gain).astype(jnp.bfloat16)
        hidden = jnp.dot(normed, w_in, preferred_element_type=jnp.float32)
        hidden = (hidden / (1.0 + jnp.exp(-hidden))).astype(jnp.bfloat16)
        added = jnp.dot(hidden, w_out, preferred_element_type=jnp.float32)
        out_ref[rows, :] = (updated + added).astype(jnp.bfloat16)


def update(place, features, own, others, gain, w_in, w_out):
    half = TILE // 2
    return pl.pallas_call(
        update_kernel,
        out_shape=jax.ShapeDtypeStruct((half, F), jnp.bfloat16),
        grid_spec=pltpu.PrefetchScalarGridSpec(
            num_scalar_prefetch=1,
            grid=(1,),
            in_specs=[
                pl.BlockSpec((half, F), lambda t, place: (place[0], 0)),
                pl.BlockSpec((half, F), lambda t, place: (0, 0)),
                pl.BlockSpec((half, F), lambda t, place: (0, 0)),
                pl.BlockSpec((half, F), lambda t, place: (0, 0)),
                pl.BlockSpec((half, F), lambda t, place: (0, 0)),
                pl.BlockSpec((1, F), lambda t, place: (0, 0)),
                pl.BlockSpec((F, F), lambda t, place: (0, 0)),
                pl.BlockSpec((F, F), lambda t, place: (0, 0)),
            ],
            out_specs=pl.BlockSpec((half, F), lambda t, place: (0, 0)),
        ),
        compiler_params=pltpu.CompilerParams(vmem_limit_bytes=8 << 20),
        name="update",
    )(place, features, own, *others, gain, w_in, w_out)


def exchange(pieces, groups):
    return lax.all_to_all(
        pieces, AXES, split_axis=0, concat_axis=0, tiled=True, axis_index_groups=groups
    )


FIRST_STEPS = first_steps()
ALL_STEPS = all_steps()


def layer(features, coords, miller, filter_weights, norm_gain, w_in, w_out):
    factors = partial_factors(jnp.asarray(FIRST_STEPS), coords, features)
    factors, coords, miller = lax.optimization_barrier((factors, coords, miller))
    atom, wave = lax.axis_index("atom"), lax.axis_index("wave")
    core, high = wave % 2, wave // 2
    place = jnp.stack([wave, core, high, core * 2 + atom // 4 % 2]).astype(jnp.int32)
    arrived = exchange(factors, GROUPS_XY)
    weights = grid_weights(miller, filter_weights)
    weights += lax.ppermute(weights, AXES, OUTER_PAIRS)
    far_weights = lax.ppermute(weights, AXES, INNER_PAIRS)
    arrived, weights = lax.optimization_barrier((arrived, weights))
    sums = plane_sum(arrived)
    shares = exchange(sums, GROUPS_LO)
    weights += far_weights
    swapped = lax.ppermute(weights[POINTS:], AXES, SWAP)
    filtered = filter_column(shares, weights[:POINTS], swapped)
    filtered, coords = lax.optimization_barrier((filtered, coords))
    near = lax.dynamic_slice_in_dim(coords, high * TILE, TILE, 1)
    near = lax.ppermute(near, AXES, LINE_SAME)
    filtered = exchange(filtered, GROUPS_XY).reshape(ALL_ROWS, F)
    tables = message_tables(place, jnp.asarray(ALL_STEPS), coords, near)
    quarter = functools.partial(message_quarter, place, tables, filtered)
    others = []
    for far, own, pairs in ((True, True, LINE_SAME), (True, False, LINE_CROSS), (False, False, SWAP)):
        part = quarter(far, own)
        others.append(lax.ppermute(part, AXES, pairs))
    own = quarter(False, True)
    return update(place, features, own, others, norm_gain.reshape(1, F), w_in, w_out)


def solution(mesh):
    in_specs = (P("atom", None), P(None, "atom"), P(None, "wave"), P("wave", None), P(), P(), P())
    out_specs = P(("atom", "wave"), None)
    return jax.shard_map(layer, mesh=mesh, in_specs=in_specs, out_specs=out_specs, check_vma=False)
```

```python
import functools
import itertools
import math

import jax
import jax.numpy as jnp
import numpy as np
from jax import lax
from jax.experimental import pallas as pl
from jax.experimental.pallas import tpu as pltpu
from jax.sharding import PartitionSpec as P

K = 4096
KMAX = 8
SIDE = 2 * KMAX + 1
PLANES = 16
BLOCKS = 4
OWN = 20
BLOCK = 2 * OWN
COLUMN = BLOCKS * BLOCK
HALF = COLUMN // 2
ALL_ROWS = PLANES * HALF
MIDDLE = 8
POINTS = BLOCKS * OWN // 2
F = 256
HALVES = 256
TILE = 512
AXES = ("atom", "wave")
OUTER = (((0,), (0,)), ((), ()))


def device(y, z_lo, x, z_hi, core):
    return (((y * 4 + z_lo) * 4 + x) * 4 + z_hi) * 2 + core


FOUR = range(4)
TWO = range(2)
GROUPS_XY = [
    [device(y, l, x, h, c) for y in FOUR for x in FOUR] for l in FOUR for h in FOUR for c in TWO
]
GROUPS_LO = [
    [device(y, l, x, h, c) for l in FOUR] for y in FOUR for x in FOUR for h in FOUR for c in TWO
]
SWAP = [
    (device(y, l, x, h, c), device(y, l, x, h, 1 - c))
    for y, l, x, h, c in itertools.product(FOUR, FOUR, FOUR, FOUR, TWO)
]
OUTER_PAIRS = [
    (device(y, l, x, h, c), device(y, l, x, 3 - h, c))
    for y, l, x, h, c in itertools.product(FOUR, FOUR, FOUR, FOUR, TWO)
]
INNER_PAIRS = [
    (device(y, l, x, h, c), device(y, l, x, h ^ 1, c))
    for y, l, x, h, c in itertools.product(FOUR, FOUR, FOUR, FOUR, TWO)
]


LINE_SAME = [
    (device(y, l, x, h, c), device(y, l ^ 1, x, h, c))
    for y, l, x, h, c in itertools.product(FOUR, FOUR, FOUR, FOUR, TWO)
]
LINE_CROSS = [
    (device(y, l, x, h, c), device(y, l ^ 1, x, h, 1 - c))
    for y, l, x, h, c in itertools.product(FOUR, FOUR, FOUR, FOUR, TWO)
]


def row_line(core, block, spot):
    third = 2 * block + core + 1
    if spot < SIDE:
        return (spot - KMAX, 0, third), 1
    if spot == SIDE:
        return (4 * core + block + 1, 0, 0), 1
    if spot == SIDE + 1:
        return (0, KMAX, third), 0
    if (core, block) == (0, 0):
        return (0, MIDDLE, 0), 1
    if (core, block) == (0, 1):
        return (MIDDLE + 1, KMAX, 0), 0
    if (core, block) == (0, 2):
        return (KMAX, KMAX, MIDDLE + 1), 2
    return None


def column_of(vector, part):
    steps = np.zeros(8, np.float32)
    steps[0:3] = vector
    steps[3:6] = vector
    steps[6] = -0.25 * part
    return steps


def spot_of(row):
    if row < 2 * SIDE:
        return row % SIDE, row // SIDE
    extra = OWN - SIDE
    return SIDE + (row - 2 * SIDE) % extra, (row - 2 * SIDE) // extra


def row_steps(core, block, row, peer):
    spot, part = spot_of(row)
    line = row_line(core, block, spot)
    if line is None:
        return column_of((0, 0, 0), 1)
    vector = list(line[0])
    vector[line[1]] += peer - MIDDLE
    return column_of(vector, part)


def stride_steps(core, block, row):
    line = row_line(core, block, spot_of(row)[0])
    vector = [0, 0, 0]
    vector[1 if line is None else line[1]] = 1
    return column_of(vector, 0)


MAIN = 32
MIXED = range(MAIN, BLOCK)
AT = [0, 2 * BLOCK, 4 * BLOCK, 4 * BLOCK + 16]
STRIDES = 4 * BLOCK + 32
THIRD = STRIDES + 8 * BLOCKS
FIRST = THIRD + 8


def first_steps():
    out = np.zeros((2, 8, FIRST), np.float32)
    for core in range(2):
        columns = []
        for block in range(BLOCKS):
            rows = range(BLOCK) if block < 2 else MIXED
            columns += [row_steps(core, block, row, MIDDLE) for row in rows]
            columns += [row_steps(core, block, row, MIDDLE + 1) for row in rows]
        for block in range(BLOCKS):
            columns += [stride_steps(core, block, row) for row in MIXED]
        columns += [column_of((0, 0, 2), 0)] * 8
        out[core] = np.stack(columns, axis=1)
    return out


def all_steps():
    out = []
    for core, part in itertools.product(TWO, TWO):
        rows = itertools.product(range(PLANES), (2 * part, 2 * part + 1), range(BLOCK))
        out.append(np.stack([row_steps(core, b, r, q) for q, b, r in rows], axis=1))
    return np.stack(out)


def split_coords(coords):
    high = (coords >> 8).astype(jnp.float32) * (1.0 / 256.0)
    low = (coords & 255).astype(jnp.float32) * (1.0 / 65536.0)
    ones = jnp.ones((2, coords.shape[1]), jnp.float32)
    return jnp.concatenate([high, low, ones], axis=0).astype(jnp.bfloat16)


def cosine_coefficients():
    nodes = 0.125 + 0.125 * np.cos(np.pi * (np.arange(400) + 0.5) / 400)
    fit = np.polynomial.chebyshev.Chebyshev.fit(
        nodes, np.cos(2 * np.pi * np.sqrt(nodes)), 5, domain=[0, 0.25]
    )
    return [float(c) for c in fit.convert(kind=np.polynomial.Polynomial).coef]


COSINE = cosine_coefficients()


def cosine_of_turns(turns):
    left = turns - jnp.round(turns)
    square = left * left
    total = jnp.full_like(square, COSINE[-1])
    for c in COSINE[-2::-1]:
        total = total * square + c
    return total


def factors_kernel(
    steps_ref, coords_ref, features_ref, out_ref, features, first, tables, total, copied
):
    copy = pltpu.make_async_copy(features_ref, features, copied)
    copy.start()
    core = lax.axis_index("wave") % 2
    steps = steps_ref[core].astype(jnp.bfloat16)
    part = coords_ref.shape[1] // 2
    for half in TWO:
        first_half(half, part, steps, coords_ref, first)
        mains = {}
        for block in range(BLOCKS):
            for start in range(half * part, (half + 1) * part, HALVES):
                fill_tables(block, start, first, mains, tables)
            if half == 0 and block == 0:
                copy.wait()
            atoms = pl.ds(half * part, part)
            added = jnp.dot(
                tables[block, :, atoms], features[atoms, :], preferred_element_type=jnp.float32
            )
            if half == 0:
                total[block] = added
                continue
            summed = total[block] + added
            for peer in range(PLANES):
                piece = summed[peer * BLOCK : (peer + 1) * BLOCK, :].astype(jnp.bfloat16)
                out_ref[peer, block * BLOCK : (block + 1) * BLOCK, :] = piece


def first_half(half, part, steps, coords_ref, first):
    for start in range(half * part, (half + 1) * part, TILE):
        parts = split_coords(coords_ref[:, start : start + TILE])
        turns = lax.dot_general(steps, parts, OUTER, preferred_element_type=jnp.float32)
        first[:, start : start + TILE] = cosine_of_turns(turns)


def fill_tables(block, start, first, mains, tables):
    lanes = pl.ds(start, HALVES)
    if block < 2:
        at = first[AT[block] : AT[block] + BLOCK, lanes]
        after = first[AT[block] + BLOCK : AT[block] + 2 * BLOCK, lanes]
    else:
        third = 2.0 * first[THIRD : THIRD + 1, lanes]
        main = [
            third * near - far
            for near, far in zip(mains[block - 1, start], mains[block - 2, start])
        ]
        mixed = [first[AT[block] + 8 * p : AT[block] + 8 * p + 8, lanes] for p in TWO]
        at, after = (jnp.concatenate([main[p], mixed[p]], axis=0) for p in TWO)
    mains[block, start] = at[:MAIN], after[:MAIN]
    mixed = 2.0 * first[STRIDES + 8 * block : STRIDES + 8 * block + 8, lanes]
    common = jnp.broadcast_to(mixed[0:1, :], (MAIN, HALVES))
    stride = jnp.concatenate([common, mixed], axis=0)
    held = {MIDDLE: at, MIDDLE + 1: after}
    for peer in range(MIDDLE, PLANES, 2):
        for later in (peer, peer + 1):
            if later not in held:
                held[later] = stride * held[later - 1] - held[later - 2]
        pair = jnp.concatenate([held[peer], held[peer + 1]], axis=0)
        tables[block, peer * BLOCK : (peer + 2) * BLOCK, lanes] = pair.astype(jnp.bfloat16)
    for peer in range(MIDDLE - 2, -1, -2):
        for earlier in (peer + 1, peer):
            held[earlier] = stride * held[earlier + 1] - held[earlier + 2]
        pair = jnp.concatenate([held[peer], held[peer + 1]], axis=0)
        tables[block, peer * BLOCK : (peer + 2) * BLOCK, lanes] = pair.astype(jnp.bfloat16)


def partial_factors(steps, coords, features):
    atoms = features.shape[0]
    return pl.pallas_call(
        factors_kernel,
        out_shape=jax.ShapeDtypeStruct((PLANES, COLUMN, F), jnp.bfloat16),
        in_specs=[
            pl.BlockSpec(memory_space=pltpu.VMEM),
            pl.BlockSpec(memory_space=pltpu.VMEM),
            pl.BlockSpec(memory_space=pl.ANY),
        ],
        out_specs=pl.BlockSpec(memory_space=pltpu.VMEM),
        scratch_shapes=[
            pltpu.VMEM((atoms, F), jnp.bfloat16),
            pltpu.VMEM((FIRST, atoms), jnp.float32),
            pltpu.VMEM((BLOCKS, PLANES * BLOCK, atoms), jnp.bfloat16),
            pltpu.VMEM((BLOCKS, PLANES * BLOCK, F), jnp.float32),
            pltpu.SemaphoreType.DMA,
        ],
        cost_estimate=pl.CostEstimate(
            flops=2 * PLANES * COLUMN * atoms * F, bytes_accessed=atoms * F * 2, transcendentals=0
        ),
        name="factors",
    )(steps, coords, features)


def grid_spots(m0, m1, m2):
    flip = (m2 < 0) | ((m2 == 0) & ((m0 < 0) | ((m0 == 0) & (m1 < 0))))
    m0, m1, m2 = (jnp.where(flip, -m, m) for m in (m0, m1, m2))
    zero, last = m2 == 0, m1 == KMAX
    corner = last & (m0 == KMAX) & (m2 > 0)
    edge = zero & last & (m0 > 0)
    axis = zero & (m0 == 0)
    sheet = zero & (m0 > 0) & (m1 < KMAX)
    rim = last & (m0 < KMAX) & (m2 > 0)
    core = jnp.where(sheet, (m0 - 1) >> 2, (m2 - 1) & 1)
    block = jnp.where(sheet, (m0 - 1) & 3, (m2 - 1) >> 1)
    block = jnp.where(corner, 2, jnp.where(edge, 1, jnp.where(axis, 0, block)))
    core = jnp.where(corner | edge | axis, 0, core)
    peer = jnp.where(rim, m0 + KMAX, m1 + KMAX)
    peer = jnp.where(corner, m2 - 1, jnp.where(edge, m0 - 1, jnp.where(axis, m1, peer)))
    spot = jnp.where(sheet, SIDE, jnp.where(rim, SIDE + 1, m0 + KMAX))
    spot = jnp.where(corner | edge | axis, SIDE + 2, spot)
    return ((core * PLANES + peer) * BLOCKS + block) * OWN + spot


def weights_kernel(miller_ref, weights_ref, out_ref):
    core, atom = lax.axis_index("wave") % 2, lax.axis_index("atom")
    plane, part = atom // 16 * 4 + atom % 4, atom // 4 % 2
    spots = grid_spots(miller_ref[0:1, :], miller_ref[1:2, :], miller_ref[2:3, :])
    row = lax.broadcasted_iota(jnp.int32, (POINTS, miller_ref.shape[1]), 0)
    weights = weights_ref[...]
    upper = weights.astype(jnp.bfloat16)
    lower = (weights - upper.astype(jnp.float32)).astype(jnp.bfloat16)
    for turn, held in enumerate((core, 1 - core)):
        wanted = row + ((held * PLANES + plane) * 2 + part) * POINTS
        match = jnp.where(wanted == spots, 1.0, 0.0).astype(jnp.bfloat16)
        summed = jnp.dot(match, upper, preferred_element_type=jnp.float32)
        summed += jnp.dot(match, lower, preferred_element_type=jnp.float32)
        out_ref[turn * POINTS : (turn + 1) * POINTS, :] = summed.astype(jnp.bfloat16)


def grid_weights(miller, weights):
    return pl.pallas_call(
        weights_kernel,
        out_shape=jax.ShapeDtypeStruct((2 * POINTS, F), jnp.bfloat16),
        in_specs=[pl.BlockSpec(memory_space=pltpu.VMEM)] * 2,
        out_specs=pl.BlockSpec(memory_space=pltpu.VMEM),
        compiler_params=pltpu.CompilerParams(vmem_limit_bytes=8 << 20),
        cost_estimate=pl.CostEstimate(
            flops=8 * POINTS * 512 * F, bytes_accessed=512 * F * 4, transcendentals=0
        ),
        name="grid_weights",
    )(miller, weights)


def plane_sum_kernel(arrived_ref, out_ref):
    total = arrived_ref[0].astype(jnp.float32)
    for peer in range(1, PLANES):
        total += arrived_ref[peer].astype(jnp.float32)
    sent = total.astype(jnp.bfloat16)
    for peer in range(4):
        out_ref[peer] = sent[peer % 2 * HALF : (peer % 2 + 1) * HALF]


def plane_sum(arrived):
    return pl.pallas_call(
        plane_sum_kernel,
        out_shape=jax.ShapeDtypeStruct((4, HALF, F), jnp.bfloat16),
        in_specs=[pl.BlockSpec(memory_space=pltpu.VMEM)],
        out_specs=pl.BlockSpec(memory_space=pltpu.VMEM),
        compiler_params=pltpu.CompilerParams(vmem_limit_bytes=8 << 20),
        name="plane_sum",
    )(arrived)


def filter_kernel(arrived_ref, near_ref, far_ref, out_ref, total, filtered):
    total[...] = jnp.sum(arrived_ref[...].astype(jnp.float32), axis=0)
    weights = near_ref[...].astype(jnp.float32) + far_ref[...].astype(jnp.float32)
    extra = OWN - SIDE
    for block in range(BLOCKS // 2):
        for row, spot, count in ((0, 0, SIDE), (2 * SIDE, SIDE, extra)):
            start, weight = block * BLOCK + row, block * OWN + spot
            cosines, sines = total[start : start + count, :], total[start + count : start + 2 * count, :]
            power = jnp.sum(cosines * cosines + sines * sines, axis=1, keepdims=True) * (0.5 / F)
            scaled = weights[weight : weight + count] * (1.0 / jnp.sqrt(power + 1e-05))
            filtered[start : start + count, :] = cosines * scaled
            filtered[start + count : start + 2 * count, :] = sines * scaled
    column = filtered[...].astype(jnp.bfloat16)
    for peer in range(PLANES):
        out_ref[peer] = column


def filter_column(arrived, near, far):
    return pl.pallas_call(
        filter_kernel,
        out_shape=jax.ShapeDtypeStruct((PLANES, HALF, F), jnp.bfloat16),
        in_specs=[pl.BlockSpec(memory_space=pltpu.VMEM)] * 3,
        out_specs=pl.BlockSpec(memory_space=pltpu.VMEM),
        scratch_shapes=[pltpu.VMEM((HALF, F), jnp.float32)] * 2,
        compiler_params=pltpu.CompilerParams(vmem_limit_bytes=8 << 20),
        name="filter_column",
    )(arrived, near, far)


def tables_kernel(place_ref, steps_ref, own_ref, near_ref, out_ref):
    steps = steps_ref[0].astype(jnp.bfloat16)
    block = 128
    for side, coords_ref in enumerate((own_ref, near_ref)):
        parts = split_coords(coords_ref[...])
        for start in range(0, TILE, block):
            turns = lax.dot_general(
                parts[:, start : start + block], steps, OUTER, preferred_element_type=jnp.float32
            )
            rows = side * TILE + start
            out_ref[rows : rows + block, :] = cosine_of_turns(turns).astype(jnp.bfloat16)


def message_tables(place, steps, coords, near):
    width = 256
    return pl.pallas_call(
        tables_kernel,
        out_shape=jax.ShapeDtypeStruct((2 * TILE, ALL_ROWS), jnp.bfloat16),
        grid_spec=pltpu.PrefetchScalarGridSpec(
            num_scalar_prefetch=1,
            grid=(ALL_ROWS // width,),
            in_specs=[
                pl.BlockSpec((1, 8, width), lambda t, place: (place[3], 0, t)),
                pl.BlockSpec((3, TILE), lambda t, place: (0, place[2])),
                pl.BlockSpec((3, TILE), lambda t, place: (0, 0)),
            ],
            out_specs=pl.BlockSpec((2 * TILE, width), lambda t, place: (0, t)),
        ),
        compiler_params=pltpu.CompilerParams(vmem_limit_bytes=16 << 20),
        cost_estimate=pl.CostEstimate(
            flops=32 * TILE * ALL_ROWS, bytes_accessed=TILE * ALL_ROWS * 4, transcendentals=0
        ),
        name="message_tables",
    )(place, steps, coords, near)


def message_kernel(place_ref, tables_ref, filtered_ref, out_ref, *, own):
    half = TILE // 2
    core = place_ref[1] if own else 1 - place_ref[1]
    start = pl.multiple_of(core * half, half)
    filtered = filtered_ref[...]
    for side in TWO:
        tables = tables_ref[pl.ds(start + side * TILE, half), :]
        message = jnp.dot(tables, filtered, preferred_element_type=jnp.float32)
        out_ref[side] = message.astype(out_ref.dtype)


def message_halves(place, tables, filtered, own):
    half = TILE // 2
    dtype = jnp.float32 if own else jnp.bfloat16
    return pl.pallas_call(
        functools.partial(message_kernel, own=own),
        out_shape=jax.ShapeDtypeStruct((2, half, F), dtype),
        in_specs=[
            pl.BlockSpec(memory_space=pltpu.SMEM),
            pl.BlockSpec(memory_space=pltpu.VMEM),
            pl.BlockSpec(memory_space=pltpu.VMEM),
        ],
        out_specs=pl.BlockSpec(memory_space=pltpu.VMEM),
        compiler_params=pltpu.CompilerParams(vmem_limit_bytes=16 << 20),
        cost_estimate=pl.CostEstimate(
            flops=4 * half * ALL_ROWS * F, bytes_accessed=8 * half * ALL_ROWS, transcendentals=0
        ),
        name="message_own" if own else "message_other",
    )(place, tables, filtered)


def update_kernel(
    place_ref, features_ref, owns_ref, others_ref, far_ref, gain_ref, w_in_ref, w_out_ref, out_ref
):
    gain, w_in, w_out = gain_ref[...], w_in_ref[...], w_out_ref[...]
    half = TILE // 2
    base = pl.multiple_of(place_ref[0] * half, half)
    chunk = half // 2
    for start in range(0, half, chunk):
        rows = pl.ds(start, chunk)
        message = owns_ref[0, rows, :] + others_ref[0, rows, :].astype(jnp.float32)
        message += far_ref[rows, :].astype(jnp.float32)
        features = features_ref[pl.ds(base + start, chunk), :].astype(jnp.float32)
        updated = features + message * (1.0 / math.sqrt(K))
        power = jnp.mean(updated * updated, axis=1, keepdims=True)
        normed = (updated / jnp.sqrt(power + 1e-06) * gain).astype(jnp.bfloat16)
        hidden = jnp.dot(normed, w_in, preferred_element_type=jnp.float32)
        hidden = (hidden / (1.0 + jnp.exp(-hidden))).astype(jnp.bfloat16)
        added = jnp.dot(hidden, w_out, preferred_element_type=jnp.float32)
        out_ref[rows, :] = (updated + added).astype(jnp.bfloat16)


def update(place, features, owns, others, far, gain, w_in, w_out):
    return pl.pallas_call(
        update_kernel,
        out_shape=jax.ShapeDtypeStruct((TILE // 2, F), jnp.bfloat16),
        in_specs=[pl.BlockSpec(memory_space=pltpu.SMEM)]
        + [pl.BlockSpec(memory_space=pltpu.VMEM)] * 7,
        out_specs=pl.BlockSpec(memory_space=pltpu.VMEM),
        compiler_params=pltpu.CompilerParams(vmem_limit_bytes=8 << 20),
        name="update",
    )(place, features, owns, others, far, gain, w_in, w_out)


def exchange(pieces, groups):
    return lax.all_to_all(
        pieces, AXES, split_axis=0, concat_axis=0, tiled=True, axis_index_groups=groups
    )


FIRST_STEPS = first_steps()
ALL_STEPS = all_steps()


def layer(features, coords, miller, filter_weights, norm_gain, w_in, w_out):
    factors = partial_factors(jnp.asarray(FIRST_STEPS), coords, features)
    factors, coords, miller = lax.optimization_barrier((factors, coords, miller))
    atom, wave = lax.axis_index("atom"), lax.axis_index("wave")
    core, high = wave % 2, wave // 2
    place = jnp.stack([wave, core, high, core * 2 + atom // 4 % 2]).astype(jnp.int32)
    arrived = exchange(factors, GROUPS_XY)
    weights = grid_weights(miller, filter_weights)
    weights += lax.ppermute(weights, AXES, OUTER_PAIRS)
    far_weights = lax.ppermute(weights, AXES, INNER_PAIRS)
    arrived, weights = lax.optimization_barrier((arrived, weights))
    sums = plane_sum(arrived)
    shares = exchange(sums, GROUPS_LO)
    weights += far_weights
    swapped = lax.ppermute(weights[POINTS:], AXES, SWAP)
    filtered = filter_column(shares, weights[:POINTS], swapped)
    filtered, coords = lax.optimization_barrier((filtered, coords))
    near = lax.dynamic_slice_in_dim(coords, high * TILE, TILE, 1)
    near = lax.ppermute(near, AXES, LINE_SAME)
    filtered = exchange(filtered, GROUPS_XY).reshape(ALL_ROWS, F)
    tables = message_tables(place, jnp.asarray(ALL_STEPS), coords, near)
    others = message_halves(place, tables, filtered, False)
    others = lax.ppermute(others, AXES, SWAP)
    owns = message_halves(place, tables, filtered, True)
    far = (owns[1] + others[1].astype(jnp.float32)).astype(jnp.bfloat16)
    far = lax.ppermute(far, AXES, LINE_SAME)
    return update(place, features, owns, others, far, norm_gain.reshape(1, F), w_in, w_out)


def solution(mesh):
    in_specs = (P("atom", None), P(None, "atom"), P(None, "wave"), P("wave", None), P(), P(), P())
    out_specs = P(("atom", "wave"), None)
    return jax.shard_map(layer, mesh=mesh, in_specs=in_specs, out_specs=out_specs, check_vma=False)
```

```python
import functools
import itertools
import math

import jax
import jax.numpy as jnp
import numpy as np
from jax import lax
from jax.experimental import pallas as pl
from jax.experimental.pallas import tpu as pltpu
from jax.sharding import PartitionSpec as P

K = 4096
KMAX = 8
SIDE = 2 * KMAX + 1
PLANES = 16
BLOCKS = 4
OWN = 20
BLOCK = 2 * OWN
COLUMN = BLOCKS * BLOCK
HALF = COLUMN // 2
ALL_ROWS = PLANES * HALF
MIDDLE = 8
POINTS = BLOCKS * OWN // 2
F = 256
HALVES = 256
TILE = 512
AXES = ("atom", "wave")
OUTER = (((0,), (0,)), ((), ()))


def device(y, z_lo, x, z_hi, core):
    return (((y * 4 + z_lo) * 4 + x) * 4 + z_hi) * 2 + core


FOUR = range(4)
TWO = range(2)
GROUPS_XY = [
    [device(y, l, x, h, c) for y in FOUR for x in FOUR] for l in FOUR for h in FOUR for c in TWO
]
GROUPS_LO = [
    [device(y, l, x, h, c) for l in FOUR] for y in FOUR for x in FOUR for h in FOUR for c in TWO
]
SWAP = [
    (device(y, l, x, h, c), device(y, l, x, h, 1 - c))
    for y, l, x, h, c in itertools.product(FOUR, FOUR, FOUR, FOUR, TWO)
]
OUTER_PAIRS = [
    (device(y, l, x, h, c), device(y, l, x, 3 - h, c))
    for y, l, x, h, c in itertools.product(FOUR, FOUR, FOUR, FOUR, TWO)
]
INNER_PAIRS = [
    (device(y, l, x, h, c), device(y, l, x, h ^ 1, c))
    for y, l, x, h, c in itertools.product(FOUR, FOUR, FOUR, FOUR, TWO)
]


LINE_SAME = [
    (device(y, l, x, h, c), device(y, l ^ 1, x, h, c))
    for y, l, x, h, c in itertools.product(FOUR, FOUR, FOUR, FOUR, TWO)
]
LINE_CROSS = [
    (device(y, l, x, h, c), device(y, l ^ 1, x, h, 1 - c))
    for y, l, x, h, c in itertools.product(FOUR, FOUR, FOUR, FOUR, TWO)
]


def row_line(core, block, spot):
    third = 2 * block + core + 1
    if spot < SIDE:
        return (spot - KMAX, 0, third), 1
    if spot == SIDE:
        return (4 * core + block + 1, 0, 0), 1
    if spot == SIDE + 1:
        return (0, KMAX, third), 0
    if (core, block) == (0, 0):
        return (0, MIDDLE, 0), 1
    if (core, block) == (0, 1):
        return (MIDDLE + 1, KMAX, 0), 0
    if (core, block) == (0, 2):
        return (KMAX, KMAX, MIDDLE + 1), 2
    return None


def column_of(vector, part):
    steps = np.zeros(8, np.float32)
    steps[0:3] = vector
    steps[3:6] = vector
    steps[6] = -0.25 * part
    return steps


def spot_of(row):
    if row < 2 * SIDE:
        return row % SIDE, row // SIDE
    extra = OWN - SIDE
    return SIDE + (row - 2 * SIDE) % extra, (row - 2 * SIDE) // extra


def row_steps(core, block, row, peer):
    spot, part = spot_of(row)
    line = row_line(core, block, spot)
    if line is None:
        return column_of((0, 0, 0), 1)
    vector = list(line[0])
    vector[line[1]] += peer - MIDDLE
    return column_of(vector, part)


def stride_steps(core, block, row):
    line = row_line(core, block, spot_of(row)[0])
    vector = [0, 0, 0]
    vector[1 if line is None else line[1]] = 1
    return column_of(vector, 0)


MAIN = 32
MIXED = range(MAIN, BLOCK)
AT = [0, 2 * BLOCK, 4 * BLOCK, 4 * BLOCK + 16]
STRIDES = 4 * BLOCK + 32
THIRD = STRIDES + 8 * BLOCKS
FIRST = THIRD + 8


def first_steps():
    out = np.zeros((2, 8, FIRST), np.float32)
    for core in range(2):
        columns = []
        for block in range(BLOCKS):
            rows = range(BLOCK) if block < 2 else MIXED
            columns += [row_steps(core, block, row, MIDDLE) for row in rows]
            columns += [row_steps(core, block, row, MIDDLE + 1) for row in rows]
        for block in range(BLOCKS):
            columns += [stride_steps(core, block, row) for row in MIXED]
        columns += [column_of((0, 0, 2), 0)] * 8
        out[core] = np.stack(columns, axis=1)
    return out


def all_steps():
    out = []
    for core, part in itertools.product(TWO, TWO):
        rows = itertools.product(range(PLANES), (2 * part, 2 * part + 1), range(BLOCK))
        out.append(np.stack([row_steps(core, b, r, q) for q, b, r in rows], axis=1))
    return np.stack(out)


def split_coords(coords):
    high = (coords >> 8).astype(jnp.float32) * (1.0 / 256.0)
    low = (coords & 255).astype(jnp.float32) * (1.0 / 65536.0)
    ones = jnp.ones((2, coords.shape[1]), jnp.float32)
    return jnp.concatenate([high, low, ones], axis=0).astype(jnp.bfloat16)


def cosine_coefficients():
    nodes = 0.125 + 0.125 * np.cos(np.pi * (np.arange(400) + 0.5) / 400)
    fit = np.polynomial.chebyshev.Chebyshev.fit(
        nodes, np.cos(2 * np.pi * np.sqrt(nodes)), 5, domain=[0, 0.25]
    )
    return [float(c) for c in fit.convert(kind=np.polynomial.Polynomial).coef]


COSINE = cosine_coefficients()


def cosine_of_turns(turns):
    left = turns - jnp.round(turns)
    square = left * left
    total = jnp.full_like(square, COSINE[-1])
    for c in COSINE[-2::-1]:
        total = total * square + c
    return total


def factors_kernel(
    steps_ref, coords_ref, features_ref, out_ref, features, first, tables, copied
):
    copy = pltpu.make_async_copy(features_ref, features, copied)
    copy.start()
    core = lax.axis_index("wave") % 2
    steps = steps_ref[core].astype(jnp.bfloat16)
    atoms = coords_ref.shape[1]
    for start in range(0, atoms, TILE):
        parts = split_coords(coords_ref[:, start : start + TILE])
        turns = lax.dot_general(steps, parts, OUTER, preferred_element_type=jnp.float32)
        first[:, start : start + TILE] = cosine_of_turns(turns)
    mains = {}
    for block in range(BLOCKS):
        for start in range(0, atoms, HALVES):
            lanes = pl.ds(start, HALVES)
            if block < 2:
                at = first[AT[block] : AT[block] + BLOCK, lanes]
                after = first[AT[block] + BLOCK : AT[block] + 2 * BLOCK, lanes]
            else:
                third = 2.0 * first[THIRD : THIRD + 1, lanes]
                main = [
                    third * near - far
                    for near, far in zip(mains[block - 1, start], mains[block - 2, start])
                ]
                mixed = [first[AT[block] + 8 * p : AT[block] + 8 * p + 8, lanes] for p in TWO]
                at, after = (jnp.concatenate([main[p], mixed[p]], axis=0) for p in TWO)
            mains[block, start] = at[:MAIN], after[:MAIN]
            mixed = 2.0 * first[STRIDES + 8 * block : STRIDES + 8 * block + 8, lanes]
            common = jnp.broadcast_to(mixed[0:1, :], (MAIN, HALVES))
            stride = jnp.concatenate([common, mixed], axis=0)
            held = {MIDDLE: at, MIDDLE + 1: after}
            for peer in range(MIDDLE, PLANES, 2):
                for later in (peer, peer + 1):
                    if later not in held:
                        held[later] = stride * held[later - 1] - held[later - 2]
                pair = jnp.concatenate([held[peer], held[peer + 1]], axis=0)
                tables[block, peer * BLOCK : (peer + 2) * BLOCK, lanes] = pair.astype(jnp.bfloat16)
            for peer in range(MIDDLE - 2, -1, -2):
                for earlier in (peer + 1, peer):
                    held[earlier] = stride * held[earlier + 1] - held[earlier + 2]
                pair = jnp.concatenate([held[peer], held[peer + 1]], axis=0)
                tables[block, peer * BLOCK : (peer + 2) * BLOCK, lanes] = pair.astype(jnp.bfloat16)
        if block == 0:
            copy.wait()
        summed = jnp.dot(tables[block], features[...], preferred_element_type=jnp.float32)
        for peer in range(PLANES):
            piece = summed[peer * BLOCK : (peer + 1) * BLOCK, :].astype(jnp.bfloat16)
            out_ref[peer, block * BLOCK : (block + 1) * BLOCK, :] = piece


def partial_factors(steps, coords, features):
    atoms = features.shape[0]
    return pl.pallas_call(
        factors_kernel,
        out_shape=jax.ShapeDtypeStruct((PLANES, COLUMN, F), jnp.bfloat16),
        in_specs=[
            pl.BlockSpec(memory_space=pltpu.VMEM),
            pl.BlockSpec(memory_space=pltpu.VMEM),
            pl.BlockSpec(memory_space=pl.ANY),
        ],
        out_specs=pl.BlockSpec(memory_space=pltpu.VMEM),
        scratch_shapes=[
            pltpu.VMEM((atoms, F), jnp.bfloat16),
            pltpu.VMEM((FIRST, atoms), jnp.float32),
            pltpu.VMEM((BLOCKS, PLANES * BLOCK, atoms), jnp.bfloat16),
            pltpu.SemaphoreType.DMA,
        ],
        cost_estimate=pl.CostEstimate(
            flops=2 * PLANES * COLUMN * atoms * F, bytes_accessed=atoms * F * 2, transcendentals=0
        ),
        name="factors",
    )(steps, coords, features)


def grid_spots(m0, m1, m2):
    flip = (m2 < 0) | ((m2 == 0) & ((m0 < 0) | ((m0 == 0) & (m1 < 0))))
    m0, m1, m2 = (jnp.where(flip, -m, m) for m in (m0, m1, m2))
    zero, last = m2 == 0, m1 == KMAX
    corner = last & (m0 == KMAX) & (m2 > 0)
    edge = zero & last & (m0 > 0)
    axis = zero & (m0 == 0)
    sheet = zero & (m0 > 0) & (m1 < KMAX)
    rim = last & (m0 < KMAX) & (m2 > 0)
    core = jnp.where(sheet, (m0 - 1) >> 2, (m2 - 1) & 1)
    block = jnp.where(sheet, (m0 - 1) & 3, (m2 - 1) >> 1)
    block = jnp.where(corner, 2, jnp.where(edge, 1, jnp.where(axis, 0, block)))
    core = jnp.where(corner | edge | axis, 0, core)
    peer = jnp.where(rim, m0 + KMAX, m1 + KMAX)
    peer = jnp.where(corner, m2 - 1, jnp.where(edge, m0 - 1, jnp.where(axis, m1, peer)))
    spot = jnp.where(sheet, SIDE, jnp.where(rim, SIDE + 1, m0 + KMAX))
    spot = jnp.where(corner | edge | axis, SIDE + 2, spot)
    return ((core * PLANES + peer) * BLOCKS + block) * OWN + spot


def weights_kernel(miller_ref, weights_ref, out_ref):
    core, atom = lax.axis_index("wave") % 2, lax.axis_index("atom")
    plane, part = atom // 16 * 4 + atom % 4, atom // 4 % 2
    spots = grid_spots(miller_ref[0:1, :], miller_ref[1:2, :], miller_ref[2:3, :])
    row = lax.broadcasted_iota(jnp.int32, (POINTS, miller_ref.shape[1]), 0)
    weights = weights_ref[...]
    upper = weights.astype(jnp.bfloat16)
    lower = (weights - upper.astype(jnp.float32)).astype(jnp.bfloat16)
    for turn, held in enumerate((core, 1 - core)):
        wanted = row + ((held * PLANES + plane) * 2 + part) * POINTS
        match = jnp.where(wanted == spots, 1.0, 0.0).astype(jnp.bfloat16)
        summed = jnp.dot(match, upper, preferred_element_type=jnp.float32)
        summed += jnp.dot(match, lower, preferred_element_type=jnp.float32)
        out_ref[turn * POINTS : (turn + 1) * POINTS, :] = summed.astype(jnp.bfloat16)


def grid_weights(miller, weights):
    return pl.pallas_call(
        weights_kernel,
        out_shape=jax.ShapeDtypeStruct((2 * POINTS, F), jnp.bfloat16),
        in_specs=[pl.BlockSpec(memory_space=pltpu.VMEM)] * 2,
        out_specs=pl.BlockSpec(memory_space=pltpu.VMEM),
        compiler_params=pltpu.CompilerParams(vmem_limit_bytes=8 << 20),
        cost_estimate=pl.CostEstimate(
            flops=8 * POINTS * 512 * F, bytes_accessed=512 * F * 4, transcendentals=0
        ),
        name="grid_weights",
    )(miller, weights)


def plane_sum_kernel(arrived_ref, out_ref):
    total = arrived_ref[0].astype(jnp.float32)
    for peer in range(1, PLANES):
        total += arrived_ref[peer].astype(jnp.float32)
    sent = total.astype(jnp.bfloat16)
    for peer in range(4):
        out_ref[peer] = sent[peer % 2 * HALF : (peer % 2 + 1) * HALF]


def plane_sum(arrived):
    return pl.pallas_call(
        plane_sum_kernel,
        out_shape=jax.ShapeDtypeStruct((4, HALF, F), jnp.bfloat16),
        in_specs=[pl.BlockSpec(memory_space=pltpu.VMEM)],
        out_specs=pl.BlockSpec(memory_space=pltpu.VMEM),
        compiler_params=pltpu.CompilerParams(vmem_limit_bytes=8 << 20),
        name="plane_sum",
    )(arrived)


def filter_kernel(arrived_ref, near_ref, far_ref, out_ref, total, filtered):
    total[...] = jnp.sum(arrived_ref[...].astype(jnp.float32), axis=0)
    weights = near_ref[...].astype(jnp.float32) + far_ref[...].astype(jnp.float32)
    extra = OWN - SIDE
    for block in range(BLOCKS // 2):
        for row, spot, count in ((0, 0, SIDE), (2 * SIDE, SIDE, extra)):
            start, weight = block * BLOCK + row, block * OWN + spot
            cosines, sines = total[start : start + count, :], total[start + count : start + 2 * count, :]
            power = jnp.sum(cosines * cosines + sines * sines, axis=1, keepdims=True) * (0.5 / F)
            scaled = weights[weight : weight + count] * (1.0 / jnp.sqrt(power + 1e-05))
            filtered[start : start + count, :] = cosines * scaled
            filtered[start + count : start + 2 * count, :] = sines * scaled
    column = filtered[...].astype(jnp.bfloat16)
    for peer in range(PLANES):
        out_ref[peer] = column


def filter_column(arrived, near, far):
    return pl.pallas_call(
        filter_kernel,
        out_shape=jax.ShapeDtypeStruct((PLANES, HALF, F), jnp.bfloat16),
        in_specs=[pl.BlockSpec(memory_space=pltpu.VMEM)] * 3,
        out_specs=pl.BlockSpec(memory_space=pltpu.VMEM),
        scratch_shapes=[pltpu.VMEM((HALF, F), jnp.float32)] * 2,
        compiler_params=pltpu.CompilerParams(vmem_limit_bytes=8 << 20),
        name="filter_column",
    )(arrived, near, far)


def tables_kernel(place_ref, steps_ref, own_ref, near_ref, out_ref):
    steps = steps_ref[0].astype(jnp.bfloat16)
    block = 128
    for side, coords_ref in enumerate((own_ref, near_ref)):
        parts = split_coords(coords_ref[...])
        for start in range(0, TILE, block):
            turns = lax.dot_general(
                parts[:, start : start + block], steps, OUTER, preferred_element_type=jnp.float32
            )
            rows = side * TILE + start
            out_ref[rows : rows + block, :] = cosine_of_turns(turns).astype(jnp.bfloat16)


def message_tables(place, steps, coords, near):
    width = 256
    return pl.pallas_call(
        tables_kernel,
        out_shape=jax.ShapeDtypeStruct((2 * TILE, ALL_ROWS), jnp.bfloat16),
        grid_spec=pltpu.PrefetchScalarGridSpec(
            num_scalar_prefetch=1,
            grid=(ALL_ROWS // width,),
            in_specs=[
                pl.BlockSpec((1, 8, width), lambda t, place: (place[3], 0, t)),
                pl.BlockSpec((3, TILE), lambda t, place: (0, place[2])),
                pl.BlockSpec((3, TILE), lambda t, place: (0, 0)),
            ],
            out_specs=pl.BlockSpec((2 * TILE, width), lambda t, place: (0, t)),
        ),
        compiler_params=pltpu.CompilerParams(vmem_limit_bytes=16 << 20),
        cost_estimate=pl.CostEstimate(
            flops=32 * TILE * ALL_ROWS, bytes_accessed=TILE * ALL_ROWS * 4, transcendentals=0
        ),
        name="message_tables",
    )(place, steps, coords, near)


def message_kernel(tables_ref, filtered_ref, out_ref, *, own):
    half = TILE // 2
    core = lax.axis_index("wave") % 2
    core = core if own else 1 - core
    start = pl.multiple_of(core * half, half)
    filtered = filtered_ref[...]
    for side in TWO:
        tables = tables_ref[pl.ds(start + side * TILE, half), :]
        message = jnp.dot(tables, filtered, preferred_element_type=jnp.float32)
        out_ref[side] = message.astype(out_ref.dtype)


def message_halves(tables, filtered, own):
    half = TILE // 2
    dtype = jnp.float32 if own else jnp.bfloat16
    return pl.pallas_call(
        functools.partial(message_kernel, own=own),
        out_shape=jax.ShapeDtypeStruct((2, half, F), dtype),
        in_specs=[pl.BlockSpec(memory_space=pltpu.VMEM)] * 2,
        out_specs=pl.BlockSpec(memory_space=pltpu.VMEM),
        compiler_params=pltpu.CompilerParams(vmem_limit_bytes=16 << 20),
        cost_estimate=pl.CostEstimate(
            flops=4 * half * ALL_ROWS * F, bytes_accessed=8 * half * ALL_ROWS, transcendentals=0
        ),
        name="message_own" if own else "message_other",
    )(tables, filtered)


def update_kernel(
    features_ref, owns_ref, others_ref, far_ref, gain_ref, w_in_ref, w_out_ref, out_ref
):
    gain, w_in, w_out = gain_ref[...], w_in_ref[...], w_out_ref[...]
    half = TILE // 2
    base = pl.multiple_of(lax.axis_index("wave") * half, half)
    chunk = half // 2
    for start in range(0, half, chunk):
        rows = pl.ds(start, chunk)
        message = owns_ref[0, rows, :] + others_ref[0, rows, :].astype(jnp.float32)
        message += far_ref[rows, :].astype(jnp.float32)
        features = features_ref[pl.ds(base + start, chunk), :].astype(jnp.float32)
        updated = features + message * (1.0 / math.sqrt(K))
        power = jnp.mean(updated * updated, axis=1, keepdims=True)
        normed = (updated / jnp.sqrt(power + 1e-06) * gain).astype(jnp.bfloat16)
        hidden = jnp.dot(normed, w_in, preferred_element_type=jnp.float32)
        hidden = (hidden / (1.0 + jnp.exp(-hidden))).astype(jnp.bfloat16)
        added = jnp.dot(hidden, w_out, preferred_element_type=jnp.float32)
        out_ref[rows, :] = (updated + added).astype(jnp.bfloat16)


def update(features, owns, others, far, gain, w_in, w_out):
    return pl.pallas_call(
        update_kernel,
        out_shape=jax.ShapeDtypeStruct((TILE // 2, F), jnp.bfloat16),
        in_specs=[pl.BlockSpec(memory_space=pltpu.VMEM)] * 7,
        out_specs=pl.BlockSpec(memory_space=pltpu.VMEM),
        compiler_params=pltpu.CompilerParams(vmem_limit_bytes=8 << 20),
        name="update",
    )(features, owns, others, far, gain, w_in, w_out)


def exchange(pieces, groups):
    return lax.all_to_all(
        pieces, AXES, split_axis=0, concat_axis=0, tiled=True, axis_index_groups=groups
    )


FIRST_STEPS = first_steps()
ALL_STEPS = all_steps()


def layer(features, coords, miller, filter_weights, norm_gain, w_in, w_out):
    factors = partial_factors(jnp.asarray(FIRST_STEPS), coords, features)
    factors, coords, miller = lax.optimization_barrier((factors, coords, miller))
    atom, wave = lax.axis_index("atom"), lax.axis_index("wave")
    core, high = wave % 2, wave // 2
    place = jnp.stack([wave, core, high, core * 2 + atom // 4 % 2]).astype(jnp.int32)
    arrived = exchange(factors, GROUPS_XY)
    weights = grid_weights(miller, filter_weights)
    weights += lax.ppermute(weights, AXES, OUTER_PAIRS)
    far_weights = lax.ppermute(weights, AXES, INNER_PAIRS)
    arrived, weights = lax.optimization_barrier((arrived, weights))
    sums = plane_sum(arrived)
    shares = exchange(sums, GROUPS_LO)
    weights += far_weights
    swapped = lax.ppermute(weights[POINTS:], AXES, SWAP)
    filtered = filter_column(shares, weights[:POINTS], swapped)
    filtered, coords = lax.optimization_barrier((filtered, coords))
    near = lax.dynamic_slice_in_dim(coords, high * TILE, TILE, 1)
    near = lax.ppermute(near, AXES, LINE_SAME)
    filtered = exchange(filtered, GROUPS_XY).reshape(ALL_ROWS, F)
    tables = message_tables(place, jnp.asarray(ALL_STEPS), coords, near)
    others = message_halves(tables, filtered, False)
    others = lax.ppermute(others, AXES, SWAP)
    owns = message_halves(tables, filtered, True)
    far = (owns[1] + others[1].astype(jnp.float32)).astype(jnp.bfloat16)
    far = lax.ppermute(far, AXES, LINE_SAME)
    return update(features, owns, others, far, norm_gain.reshape(1, F), w_in, w_out)


def solution(mesh):
    in_specs = (P("atom", None), P(None, "atom"), P(None, "wave"), P("wave", None), P(), P(), P())
    out_specs = P(("atom", "wave"), None)
    return jax.shard_map(layer, mesh=mesh, in_specs=in_specs, out_specs=out_specs, check_vma=False)
```

```python
import functools
import itertools
import math

import jax
import jax.numpy as jnp
import numpy as np
from jax import lax
from jax.experimental import pallas as pl
from jax.experimental.pallas import tpu as pltpu
from jax.sharding import PartitionSpec as P

K = 4096
KMAX = 8
SIDE = 2 * KMAX + 1
PLANES = 16
BLOCKS = 4
OWN = 20
BLOCK = 2 * OWN
COLUMN = BLOCKS * BLOCK
HALF = COLUMN // 2
ALL_ROWS = PLANES * HALF
MIDDLE = 8
POINTS = BLOCKS * OWN // 2
F = 256
HALVES = 256
TILE = 512
AXES = ("atom", "wave")
OUTER = (((0,), (0,)), ((), ()))


def device(y, z_lo, x, z_hi, core):
    return (((y * 4 + z_lo) * 4 + x) * 4 + z_hi) * 2 + core


FOUR = range(4)
TWO = range(2)
GROUPS_XY = [
    [device(y, l, x, h, c) for y in FOUR for x in FOUR] for l in FOUR for h in FOUR for c in TWO
]
GROUPS_LO = [
    [device(y, l, x, h, c) for l in FOUR] for y in FOUR for x in FOUR for h in FOUR for c in TWO
]
SWAP = [
    (device(y, l, x, h, c), device(y, l, x, h, 1 - c))
    for y, l, x, h, c in itertools.product(FOUR, FOUR, FOUR, FOUR, TWO)
]
OUTER_PAIRS = [
    (device(y, l, x, h, c), device(y, l, x, 3 - h, c))
    for y, l, x, h, c in itertools.product(FOUR, FOUR, FOUR, FOUR, TWO)
]
INNER_PAIRS = [
    (device(y, l, x, h, c), device(y, l, x, h ^ 1, c))
    for y, l, x, h, c in itertools.product(FOUR, FOUR, FOUR, FOUR, TWO)
]


LINE_SAME = [
    (device(y, l, x, h, c), device(y, l ^ 1, x, h, c))
    for y, l, x, h, c in itertools.product(FOUR, FOUR, FOUR, FOUR, TWO)
]
LINE_CROSS = [
    (device(y, l, x, h, c), device(y, l ^ 1, x, h, 1 - c))
    for y, l, x, h, c in itertools.product(FOUR, FOUR, FOUR, FOUR, TWO)
]


def row_line(core, block, spot):
    third = 2 * block + core + 1
    if spot < SIDE:
        return (spot - KMAX, 0, third), 1
    if spot == SIDE:
        return (4 * core + block + 1, 0, 0), 1
    if spot == SIDE + 1:
        return (0, KMAX, third), 0
    if (core, block) == (0, 0):
        return (0, MIDDLE, 0), 1
    if (core, block) == (0, 1):
        return (MIDDLE + 1, KMAX, 0), 0
    if (core, block) == (0, 2):
        return (KMAX, KMAX, MIDDLE + 1), 2
    return None


def column_of(vector, part):
    steps = np.zeros(8, np.float32)
    steps[0:3] = vector
    steps[3:6] = vector
    steps[6] = -0.25 * part
    return steps


def spot_of(row):
    if row < 2 * SIDE:
        return row % SIDE, row // SIDE
    extra = OWN - SIDE
    return SIDE + (row - 2 * SIDE) % extra, (row - 2 * SIDE) // extra


def row_steps(core, block, row, peer):
    spot, part = spot_of(row)
    line = row_line(core, block, spot)
    if line is None:
        return column_of((0, 0, 0), 1)
    vector = list(line[0])
    vector[line[1]] += peer - MIDDLE
    return column_of(vector, part)


def stride_steps(core, block, row):
    line = row_line(core, block, spot_of(row)[0])
    vector = [0, 0, 0]
    vector[1 if line is None else line[1]] = 1
    return column_of(vector, 0)


MAIN = 32
MIXED = range(MAIN, BLOCK)
AT = [0, 2 * BLOCK, 4 * BLOCK, 4 * BLOCK + 16]
STRIDES = 4 * BLOCK + 32
THIRD = STRIDES + 8 * BLOCKS
FIRST = THIRD + 8


def first_steps():
    out = np.zeros((2, 8, FIRST), np.float32)
    for core in range(2):
        columns = []
        for block in range(BLOCKS):
            rows = range(BLOCK) if block < 2 else MIXED
            columns += [row_steps(core, block, row, MIDDLE) for row in rows]
            columns += [row_steps(core, block, row, MIDDLE + 1) for row in rows]
        for block in range(BLOCKS):
            columns += [stride_steps(core, block, row) for row in MIXED]
        columns += [column_of((0, 0, 2), 0)] * 8
        out[core] = np.stack(columns, axis=1)
    return out


def all_steps():
    out = []
    for core, part in itertools.product(TWO, TWO):
        rows = itertools.product(range(PLANES), (2 * part, 2 * part + 1), range(BLOCK))
        out.append(np.stack([row_steps(core, b, r, q) for q, b, r in rows], axis=1))
    return np.stack(out)


def split_coords(coords):
    high = (coords >> 8).astype(jnp.float32) * (1.0 / 256.0)
    low = (coords & 255).astype(jnp.float32) * (1.0 / 65536.0)
    ones = jnp.ones((2, coords.shape[1]), jnp.float32)
    return jnp.concatenate([high, low, ones], axis=0).astype(jnp.bfloat16)


def cosine_coefficients():
    nodes = 0.125 + 0.125 * np.cos(np.pi * (np.arange(400) + 0.5) / 400)
    fit = np.polynomial.chebyshev.Chebyshev.fit(
        nodes, np.cos(2 * np.pi * np.sqrt(nodes)), 5, domain=[0, 0.25]
    )
    return [float(c) for c in fit.convert(kind=np.polynomial.Polynomial).coef]


COSINE = cosine_coefficients()


def cosine_of_turns(turns):
    left = turns - jnp.round(turns)
    square = left * left
    total = jnp.full_like(square, COSINE[-1])
    for c in COSINE[-2::-1]:
        total = total * square + c
    return total


def factors_kernel(
    steps_ref, coords_ref, features_ref, out_ref, features, first, tables, made, copied, sent
):
    copy = pltpu.make_async_copy(features_ref, features, copied)
    copy.start()
    core = lax.axis_index("wave") % 2
    steps = steps_ref[core].astype(jnp.bfloat16)
    atoms = coords_ref.shape[1]
    for start in range(0, atoms, TILE):
        parts = split_coords(coords_ref[:, start : start + TILE])
        turns = lax.dot_general(steps, parts, OUTER, preferred_element_type=jnp.float32)
        first[:, start : start + TILE] = cosine_of_turns(turns)
    mains, sends = {}, []
    for block in range(BLOCKS):
        for start in range(0, atoms, HALVES):
            lanes = pl.ds(start, HALVES)
            if block < 2:
                at = first[AT[block] : AT[block] + BLOCK, lanes]
                after = first[AT[block] + BLOCK : AT[block] + 2 * BLOCK, lanes]
            else:
                third = 2.0 * first[THIRD : THIRD + 1, lanes]
                main = [
                    third * near - far
                    for near, far in zip(mains[block - 1, start], mains[block - 2, start])
                ]
                mixed = [first[AT[block] + 8 * p : AT[block] + 8 * p + 8, lanes] for p in TWO]
                at, after = (jnp.concatenate([main[p], mixed[p]], axis=0) for p in TWO)
            mains[block, start] = at[:MAIN], after[:MAIN]
            mixed = 2.0 * first[STRIDES + 8 * block : STRIDES + 8 * block + 8, lanes]
            common = jnp.broadcast_to(mixed[0:1, :], (MAIN, HALVES))
            stride = jnp.concatenate([common, mixed], axis=0)
            held = {MIDDLE: at, MIDDLE + 1: after}
            for peer in range(MIDDLE, PLANES, 2):
                for later in (peer, peer + 1):
                    if later not in held:
                        held[later] = stride * held[later - 1] - held[later - 2]
                pair = jnp.concatenate([held[peer], held[peer + 1]], axis=0)
                tables[block, peer * BLOCK : (peer + 2) * BLOCK, lanes] = pair.astype(jnp.bfloat16)
            for peer in range(MIDDLE - 2, -1, -2):
                for earlier in (peer + 1, peer):
                    held[earlier] = stride * held[earlier + 1] - held[earlier + 2]
                pair = jnp.concatenate([held[peer], held[peer + 1]], axis=0)
                tables[block, peer * BLOCK : (peer + 2) * BLOCK, lanes] = pair.astype(jnp.bfloat16)
        if block == 0:
            copy.wait()
        summed = jnp.dot(tables[block], features[...], preferred_element_type=jnp.float32)
        for peer in range(PLANES):
            piece = summed[peer * BLOCK : (peer + 1) * BLOCK, :].astype(jnp.bfloat16)
            made[block, peer] = piece
        for group in range(4):
            sends.append(
                pltpu.make_async_copy(
                    made.at[block, pl.ds(4 * group, 4)],
                    out_ref.at[pl.ds(4 * group, 4), pl.ds(block * BLOCK, BLOCK), :],
                    sent.at[block, group],
                )
            )
            sends[-1].start()
    for send in sends:
        send.wait()


def partial_factors(steps, coords, features):
    atoms = features.shape[0]
    return pl.pallas_call(
        factors_kernel,
        out_shape=jax.ShapeDtypeStruct((PLANES, COLUMN, F), jnp.bfloat16),
        in_specs=[
            pl.BlockSpec(memory_space=pltpu.VMEM),
            pl.BlockSpec(memory_space=pltpu.VMEM),
            pl.BlockSpec(memory_space=pl.ANY),
        ],
        out_specs=pl.BlockSpec(memory_space=pl.ANY),
        scratch_shapes=[
            pltpu.VMEM((atoms, F), jnp.bfloat16),
            pltpu.VMEM((FIRST, atoms), jnp.float32),
            pltpu.VMEM((BLOCKS, PLANES * BLOCK, atoms), jnp.bfloat16),
            pltpu.VMEM((BLOCKS, PLANES, BLOCK, F), jnp.bfloat16),
            pltpu.SemaphoreType.DMA,
            pltpu.SemaphoreType.DMA((BLOCKS, 4)),
        ],
        cost_estimate=pl.CostEstimate(
            flops=2 * PLANES * COLUMN * atoms * F, bytes_accessed=atoms * F * 2, transcendentals=0
        ),
        name="factors",
    )(steps, coords, features)


def grid_spots(m0, m1, m2):
    flip = (m2 < 0) | ((m2 == 0) & ((m0 < 0) | ((m0 == 0) & (m1 < 0))))
    m0, m1, m2 = (jnp.where(flip, -m, m) for m in (m0, m1, m2))
    zero, last = m2 == 0, m1 == KMAX
    corner = last & (m0 == KMAX) & (m2 > 0)
    edge = zero & last & (m0 > 0)
    axis = zero & (m0 == 0)
    sheet = zero & (m0 > 0) & (m1 < KMAX)
    rim = last & (m0 < KMAX) & (m2 > 0)
    core = jnp.where(sheet, (m0 - 1) >> 2, (m2 - 1) & 1)
    block = jnp.where(sheet, (m0 - 1) & 3, (m2 - 1) >> 1)
    block = jnp.where(corner, 2, jnp.where(edge, 1, jnp.where(axis, 0, block)))
    core = jnp.where(corner | edge | axis, 0, core)
    peer = jnp.where(rim, m0 + KMAX, m1 + KMAX)
    peer = jnp.where(corner, m2 - 1, jnp.where(edge, m0 - 1, jnp.where(axis, m1, peer)))
    spot = jnp.where(sheet, SIDE, jnp.where(rim, SIDE + 1, m0 + KMAX))
    spot = jnp.where(corner | edge | axis, SIDE + 2, spot)
    return ((core * PLANES + peer) * BLOCKS + block) * OWN + spot


def weights_kernel(miller_ref, weights_ref, out_ref):
    core, atom = lax.axis_index("wave") % 2, lax.axis_index("atom")
    plane, part = atom // 16 * 4 + atom % 4, atom // 4 % 2
    spots = grid_spots(miller_ref[0:1, :], miller_ref[1:2, :], miller_ref[2:3, :])
    row = lax.broadcasted_iota(jnp.int32, (POINTS, miller_ref.shape[1]), 0)
    weights = weights_ref[...]
    upper = weights.astype(jnp.bfloat16)
    lower = (weights - upper.astype(jnp.float32)).astype(jnp.bfloat16)
    for turn, held in enumerate((core, 1 - core)):
        wanted = row + ((held * PLANES + plane) * 2 + part) * POINTS
        match = jnp.where(wanted == spots, 1.0, 0.0).astype(jnp.bfloat16)
        summed = jnp.dot(match, upper, preferred_element_type=jnp.float32)
        summed += jnp.dot(match, lower, preferred_element_type=jnp.float32)
        out_ref[turn * POINTS : (turn + 1) * POINTS, :] = summed.astype(jnp.bfloat16)


def grid_weights(miller, weights):
    return pl.pallas_call(
        weights_kernel,
        out_shape=jax.ShapeDtypeStruct((2 * POINTS, F), jnp.bfloat16),
        in_specs=[pl.BlockSpec(memory_space=pltpu.VMEM)] * 2,
        out_specs=pl.BlockSpec(memory_space=pltpu.VMEM),
        compiler_params=pltpu.CompilerParams(vmem_limit_bytes=8 << 20),
        cost_estimate=pl.CostEstimate(
            flops=8 * POINTS * 512 * F, bytes_accessed=512 * F * 4, transcendentals=0
        ),
        name="grid_weights",
    )(miller, weights)


def plane_sum_kernel(arrived_ref, out_ref):
    total = arrived_ref[0].astype(jnp.float32)
    for peer in range(1, PLANES):
        total += arrived_ref[peer].astype(jnp.float32)
    sent = total.astype(jnp.bfloat16)
    for peer in range(4):
        out_ref[peer] = sent[peer % 2 * HALF : (peer % 2 + 1) * HALF]


def plane_sum(arrived):
    return pl.pallas_call(
        plane_sum_kernel,
        out_shape=jax.ShapeDtypeStruct((4, HALF, F), jnp.bfloat16),
        in_specs=[pl.BlockSpec(memory_space=pltpu.VMEM)],
        out_specs=pl.BlockSpec(memory_space=pltpu.VMEM),
        compiler_params=pltpu.CompilerParams(vmem_limit_bytes=8 << 20),
        name="plane_sum",
    )(arrived)


def filter_kernel(arrived_ref, near_ref, far_ref, out_ref, total, filtered, column, sent):
    total[...] = jnp.sum(arrived_ref[...].astype(jnp.float32), axis=0)
    weights = near_ref[...].astype(jnp.float32) + far_ref[...].astype(jnp.float32)
    extra = OWN - SIDE
    for block in range(BLOCKS // 2):
        for row, spot, count in ((0, 0, SIDE), (2 * SIDE, SIDE, extra)):
            start, weight = block * BLOCK + row, block * OWN + spot
            cosines, sines = total[start : start + count, :], total[start + count : start + 2 * count, :]
            power = jnp.sum(cosines * cosines + sines * sines, axis=1, keepdims=True) * (0.5 / F)
            scaled = weights[weight : weight + count] * (1.0 / jnp.sqrt(power + 1e-05))
            filtered[start : start + count, :] = cosines * scaled
            filtered[start + count : start + 2 * count, :] = sines * scaled
    column[...] = filtered[...].astype(jnp.bfloat16)
    sends = [
        pltpu.make_async_copy(column, out_ref.at[peer], sent.at[peer]) for peer in range(PLANES)
    ]
    for send in sends:
        send.start()
    for send in sends:
        send.wait()


def filter_column(arrived, near, far):
    return pl.pallas_call(
        filter_kernel,
        out_shape=jax.ShapeDtypeStruct((PLANES, HALF, F), jnp.bfloat16),
        in_specs=[pl.BlockSpec(memory_space=pltpu.VMEM)] * 3,
        out_specs=pl.BlockSpec(memory_space=pl.ANY),
        scratch_shapes=[
            pltpu.VMEM((HALF, F), jnp.float32),
            pltpu.VMEM((HALF, F), jnp.float32),
            pltpu.VMEM((HALF, F), jnp.bfloat16),
            pltpu.SemaphoreType.DMA((PLANES,)),
        ],
        compiler_params=pltpu.CompilerParams(vmem_limit_bytes=8 << 20),
        name="filter_column",
    )(arrived, near, far)


def tables_kernel(place_ref, steps_ref, own_ref, near_ref, out_ref):
    steps = steps_ref[0].astype(jnp.bfloat16)
    block = 128
    for side, coords_ref in enumerate((own_ref, near_ref)):
        parts = split_coords(coords_ref[...])
        for start in range(0, TILE, block):
            turns = lax.dot_general(
                parts[:, start : start + block], steps, OUTER, preferred_element_type=jnp.float32
            )
            rows = side * TILE + start
            out_ref[rows : rows + block, :] = cosine_of_turns(turns).astype(jnp.bfloat16)


def message_tables(place, steps, coords, near):
    width = 256
    return pl.pallas_call(
        tables_kernel,
        out_shape=jax.ShapeDtypeStruct((2 * TILE, ALL_ROWS), jnp.bfloat16),
        grid_spec=pltpu.PrefetchScalarGridSpec(
            num_scalar_prefetch=1,
            grid=(ALL_ROWS // width,),
            in_specs=[
                pl.BlockSpec((1, 8, width), lambda t, place: (place[3], 0, t)),
                pl.BlockSpec((3, TILE), lambda t, place: (0, place[2])),
                pl.BlockSpec((3, TILE), lambda t, place: (0, 0)),
            ],
            out_specs=pl.BlockSpec((2 * TILE, width), lambda t, place: (0, t)),
        ),
        compiler_params=pltpu.CompilerParams(vmem_limit_bytes=16 << 20),
        cost_estimate=pl.CostEstimate(
            flops=32 * TILE * ALL_ROWS, bytes_accessed=TILE * ALL_ROWS * 4, transcendentals=0
        ),
        name="message_tables",
    )(place, steps, coords, near)


def message_kernel(tables_ref, filtered_ref, own_ref, other_ref, *, side):
    half = TILE // 2
    core = lax.axis_index("wave") % 2
    filtered = filtered_ref[...]
    for held, out_ref in ((core, own_ref), (1 - core, other_ref)):
        start = pl.multiple_of(held * half, half) + side * TILE
        message = jnp.dot(
            tables_ref[pl.ds(start, half), :], filtered, preferred_element_type=jnp.float32
        )
        out_ref[...] = message.astype(out_ref.dtype)


def message_halves(tables, filtered, side):
    half = TILE // 2
    return pl.pallas_call(
        functools.partial(message_kernel, side=side),
        out_shape=(
            jax.ShapeDtypeStruct((half, F), jnp.bfloat16 if side else jnp.float32),
            jax.ShapeDtypeStruct((half, F), jnp.bfloat16),
        ),
        in_specs=[pl.BlockSpec(memory_space=pltpu.VMEM)] * 2,
        out_specs=(pl.BlockSpec(memory_space=pltpu.VMEM),) * 2,
        compiler_params=pltpu.CompilerParams(vmem_limit_bytes=16 << 20),
        cost_estimate=pl.CostEstimate(
            flops=4 * half * ALL_ROWS * F, bytes_accessed=8 * half * ALL_ROWS, transcendentals=0
        ),
        name="message_far" if side else "message_near",
    )(tables, filtered)


def update_kernel(
    features_ref, own_ref, a_ref, b_ref, c_ref, gain_ref, w_in_ref, w_out_ref, out_ref
):
    gain, w_in, w_out = gain_ref[...], w_in_ref[...], w_out_ref[...]
    half = TILE // 2
    base = pl.multiple_of(lax.axis_index("wave") * half, half)
    chunk = half // 2
    for start in range(0, half, chunk):
        rows = pl.ds(start, chunk)
        message = own_ref[rows, :]
        for part_ref in (a_ref, b_ref, c_ref):
            message += part_ref[rows, :].astype(jnp.float32)
        features = features_ref[pl.ds(base + start, chunk), :].astype(jnp.float32)
        updated = features + message * (1.0 / math.sqrt(K))
        power = jnp.mean(updated * updated, axis=1, keepdims=True)
        normed = (updated / jnp.sqrt(power + 1e-06) * gain).astype(jnp.bfloat16)
        hidden = jnp.dot(normed, w_in, preferred_element_type=jnp.float32)
        hidden = (hidden / (1.0 + jnp.exp(-hidden))).astype(jnp.bfloat16)
        added = jnp.dot(hidden, w_out, preferred_element_type=jnp.float32)
        out_ref[rows, :] = (updated + added).astype(jnp.bfloat16)


def update(features, own, other, far, cross, gain, w_in, w_out):
    return pl.pallas_call(
        update_kernel,
        out_shape=jax.ShapeDtypeStruct((TILE // 2, F), jnp.bfloat16),
        in_specs=[pl.BlockSpec(memory_space=pltpu.VMEM)] * 8,
        out_specs=pl.BlockSpec(memory_space=pltpu.VMEM),
        compiler_params=pltpu.CompilerParams(vmem_limit_bytes=8 << 20),
        name="update",
    )(features, own, other, far, cross, gain, w_in, w_out)


def exchange(pieces, groups):
    return lax.all_to_all(
        pieces, AXES, split_axis=0, concat_axis=0, tiled=True, axis_index_groups=groups
    )


FIRST_STEPS = first_steps()
ALL_STEPS = all_steps()


def layer(features, coords, miller, filter_weights, norm_gain, w_in, w_out):
    factors = partial_factors(jnp.asarray(FIRST_STEPS), coords, features)
    factors, coords, miller = lax.optimization_barrier((factors, coords, miller))
    atom, wave = lax.axis_index("atom"), lax.axis_index("wave")
    core, high = wave % 2, wave // 2
    place = jnp.stack([wave, core, high, core * 2 + atom // 4 % 2]).astype(jnp.int32)
    arrived = exchange(factors, GROUPS_XY)
    weights = grid_weights(miller, filter_weights)
    weights += lax.ppermute(weights, AXES, OUTER_PAIRS)
    far_weights = lax.ppermute(weights, AXES, INNER_PAIRS)
    arrived, weights = lax.optimization_barrier((arrived, weights))
    sums = plane_sum(arrived)
    shares = exchange(sums, GROUPS_LO)
    weights += far_weights
    swapped = lax.ppermute(weights[POINTS:], AXES, SWAP)
    filtered = filter_column(shares, weights[:POINTS], swapped)
    filtered, coords = lax.optimization_barrier((filtered, coords))
    near = lax.dynamic_slice_in_dim(coords, high * TILE, TILE, 1)
    near = lax.ppermute(near, AXES, LINE_SAME)
    filtered = exchange(filtered, GROUPS_XY).reshape(ALL_ROWS, F)
    tables = message_tables(place, jnp.asarray(ALL_STEPS), coords, near)
    far, cross = message_halves(tables, filtered, 1)
    far = lax.ppermute(far, AXES, LINE_SAME)
    cross = lax.ppermute(cross, AXES, LINE_CROSS)
    own, other = message_halves(tables, filtered, 0)
    other = lax.ppermute(other, AXES, SWAP)
    gain = norm_gain.reshape(1, F)
    return update(features, own, other, far, cross, gain, w_in, w_out)


def solution(mesh):
    in_specs = (P("atom", None), P(None, "atom"), P(None, "wave"), P("wave", None), P(), P(), P())
    out_specs = P(("atom", "wave"), None)
    return jax.shard_map(layer, mesh=mesh, in_specs=in_specs, out_specs=out_specs, check_vma=False)
```

```python
import functools
import itertools
import math

import jax
import jax.numpy as jnp
import numpy as np
from jax import lax
from jax.experimental import pallas as pl
from jax.experimental.pallas import tpu as pltpu
from jax.sharding import PartitionSpec as P

K = 4096
KMAX = 8
SIDE = 2 * KMAX + 1
PLANES = 16
BLOCKS = 4
OWN = 20
BLOCK = 2 * OWN
COLUMN = BLOCKS * BLOCK
HALF = COLUMN // 2
ALL_ROWS = PLANES * HALF
MIDDLE = 8
POINTS = BLOCKS * OWN // 2
F = 256
HALVES = 256
TILE = 512
AXES = ("atom", "wave")
OUTER = (((0,), (0,)), ((), ()))


def device(y, z_lo, x, z_hi, core):
    return (((y * 4 + z_lo) * 4 + x) * 4 + z_hi) * 2 + core


FOUR = range(4)
TWO = range(2)
GROUPS_XY = [
    [device(y, l, x, h, c) for y in FOUR for x in FOUR] for l in FOUR for h in FOUR for c in TWO
]
GROUPS_LO = [
    [device(y, l, x, h, c) for l in FOUR] for y in FOUR for x in FOUR for h in FOUR for c in TWO
]
SWAP = [
    (device(y, l, x, h, c), device(y, l, x, h, 1 - c))
    for y, l, x, h, c in itertools.product(FOUR, FOUR, FOUR, FOUR, TWO)
]
OUTER_PAIRS = [
    (device(y, l, x, h, c), device(y, l, x, 3 - h, c))
    for y, l, x, h, c in itertools.product(FOUR, FOUR, FOUR, FOUR, TWO)
]
INNER_PAIRS = [
    (device(y, l, x, h, c), device(y, l, x, h ^ 1, c))
    for y, l, x, h, c in itertools.product(FOUR, FOUR, FOUR, FOUR, TWO)
]


LINE_SAME = [
    (device(y, l, x, h, c), device(y, l ^ 1, x, h, c))
    for y, l, x, h, c in itertools.product(FOUR, FOUR, FOUR, FOUR, TWO)
]
LINE_CROSS = [
    (device(y, l, x, h, c), device(y, l ^ 1, x, h, 1 - c))
    for y, l, x, h, c in itertools.product(FOUR, FOUR, FOUR, FOUR, TWO)
]


def row_line(core, block, spot):
    third = 2 * block + core + 1
    if spot < SIDE:
        return (spot - KMAX, 0, third), 1
    if spot == SIDE:
        return (4 * core + block + 1, 0, 0), 1
    if spot == SIDE + 1:
        return (0, KMAX, third), 0
    if (core, block) == (0, 0):
        return (0, MIDDLE, 0), 1
    if (core, block) == (0, 1):
        return (MIDDLE + 1, KMAX, 0), 0
    if (core, block) == (0, 2):
        return (KMAX, KMAX, MIDDLE + 1), 2
    return None


def column_of(vector, part):
    steps = np.zeros(8, np.float32)
    steps[0:3] = vector
    steps[3:6] = vector
    steps[6] = -0.25 * part
    return steps


def spot_of(row):
    if row < 2 * SIDE:
        return row % SIDE, row // SIDE
    extra = OWN - SIDE
    return SIDE + (row - 2 * SIDE) % extra, (row - 2 * SIDE) // extra


def row_steps(core, block, row, peer):
    spot, part = spot_of(row)
    line = row_line(core, block, spot)
    if line is None:
        return column_of((0, 0, 0), 1)
    vector = list(line[0])
    vector[line[1]] += peer - MIDDLE
    return column_of(vector, part)


def stride_steps(core, block, row):
    line = row_line(core, block, spot_of(row)[0])
    vector = [0, 0, 0]
    vector[1 if line is None else line[1]] = 1
    return column_of(vector, 0)


MAIN = 32
MIXED = range(MAIN, BLOCK)
AT = [0, 2 * BLOCK, 4 * BLOCK, 4 * BLOCK + 16]
STRIDES = 4 * BLOCK + 32
THIRD = STRIDES + 8 * BLOCKS
FIRST = THIRD + 8


def first_steps():
    out = np.zeros((2, 8, FIRST), np.float32)
    for core in range(2):
        columns = []
        for block in range(BLOCKS):
            rows = range(BLOCK) if block < 2 else MIXED
            columns += [row_steps(core, block, row, MIDDLE) for row in rows]
            columns += [row_steps(core, block, row, MIDDLE + 1) for row in rows]
        for block in range(BLOCKS):
            columns += [stride_steps(core, block, row) for row in MIXED]
        columns += [column_of((0, 0, 2), 0)] * 8
        out[core] = np.stack(columns, axis=1)
    return out


def all_steps():
    out = []
    for core, part in itertools.product(TWO, TWO):
        rows = itertools.product(range(PLANES), (2 * part, 2 * part + 1), range(BLOCK))
        out.append(np.stack([row_steps(core, b, r, q) for q, b, r in rows], axis=1))
    return np.stack(out)


def split_coords(coords):
    high = (coords >> 8).astype(jnp.float32) * (1.0 / 256.0)
    low = (coords & 255).astype(jnp.float32) * (1.0 / 65536.0)
    ones = jnp.ones((2, coords.shape[1]), jnp.float32)
    return jnp.concatenate([high, low, ones], axis=0).astype(jnp.bfloat16)


def cosine_coefficients():
    nodes = 0.125 + 0.125 * np.cos(np.pi * (np.arange(400) + 0.5) / 400)
    fit = np.polynomial.chebyshev.Chebyshev.fit(
        nodes, np.cos(2 * np.pi * np.sqrt(nodes)), 5, domain=[0, 0.25]
    )
    return [float(c) for c in fit.convert(kind=np.polynomial.Polynomial).coef]


COSINE = cosine_coefficients()


def cosine_of_turns(turns):
    left = turns - jnp.round(turns)
    square = left * left
    total = jnp.full_like(square, COSINE[-1])
    for c in COSINE[-2::-1]:
        total = total * square + c
    return total


def factors_kernel(
    steps_ref, coords_ref, features_ref, out_ref, features, first, tables, made, copied, sent
):
    copy = pltpu.make_async_copy(features_ref, features, copied)
    copy.start()
    core = lax.axis_index("wave") % 2
    steps = steps_ref[core].astype(jnp.bfloat16)
    atoms = coords_ref.shape[1]
    for start in range(0, atoms, TILE):
        parts = split_coords(coords_ref[:, start : start + TILE])
        turns = lax.dot_general(steps, parts, OUTER, preferred_element_type=jnp.float32)
        first[:, start : start + TILE] = cosine_of_turns(turns)
    mains, sends = {}, []
    for block in range(BLOCKS):
        for start in range(0, atoms, HALVES):
            lanes = pl.ds(start, HALVES)
            if block < 2:
                at = first[AT[block] : AT[block] + BLOCK, lanes]
                after = first[AT[block] + BLOCK : AT[block] + 2 * BLOCK, lanes]
            else:
                third = 2.0 * first[THIRD : THIRD + 1, lanes]
                main = [
                    third * near - far
                    for near, far in zip(mains[block - 1, start], mains[block - 2, start])
                ]
                mixed = [first[AT[block] + 8 * p : AT[block] + 8 * p + 8, lanes] for p in TWO]
                at, after = (jnp.concatenate([main[p], mixed[p]], axis=0) for p in TWO)
            mains[block, start] = at[:MAIN], after[:MAIN]
            mixed = 2.0 * first[STRIDES + 8 * block : STRIDES + 8 * block + 8, lanes]
            common = jnp.broadcast_to(mixed[0:1, :], (MAIN, HALVES))
            stride = jnp.concatenate([common, mixed], axis=0)
            held = {MIDDLE: at, MIDDLE + 1: after}
            for peer in range(MIDDLE, PLANES, 2):
                for later in (peer, peer + 1):
                    if later not in held:
                        held[later] = stride * held[later - 1] - held[later - 2]
                pair = jnp.concatenate([held[peer], held[peer + 1]], axis=0)
                tables[block, peer * BLOCK : (peer + 2) * BLOCK, lanes] = pair.astype(jnp.bfloat16)
            for peer in range(MIDDLE - 2, -1, -2):
                for earlier in (peer + 1, peer):
                    held[earlier] = stride * held[earlier + 1] - held[earlier + 2]
                pair = jnp.concatenate([held[peer], held[peer + 1]], axis=0)
                tables[block, peer * BLOCK : (peer + 2) * BLOCK, lanes] = pair.astype(jnp.bfloat16)
        if block == 0:
            copy.wait()
        summed = jnp.dot(tables[block], features[...], preferred_element_type=jnp.float32)
        for peer in range(PLANES):
            piece = summed[peer * BLOCK : (peer + 1) * BLOCK, :].astype(jnp.bfloat16)
            made[block, peer] = piece
        for group in range(4):
            sends.append(
                pltpu.make_async_copy(
                    made.at[block, pl.ds(4 * group, 4)],
                    out_ref.at[pl.ds(4 * group, 4), pl.ds(block * BLOCK, BLOCK), :],
                    sent.at[block, group],
                )
            )
            sends[-1].start()
    for send in sends:
        send.wait()


def partial_factors(steps, coords, features):
    atoms = features.shape[0]
    return pl.pallas_call(
        factors_kernel,
        out_shape=jax.ShapeDtypeStruct((PLANES, COLUMN, F), jnp.bfloat16),
        in_specs=[
            pl.BlockSpec(memory_space=pltpu.VMEM),
            pl.BlockSpec(memory_space=pltpu.VMEM),
            pl.BlockSpec(memory_space=pl.ANY),
        ],
        out_specs=pl.BlockSpec(memory_space=pl.ANY),
        scratch_shapes=[
            pltpu.VMEM((atoms, F), jnp.bfloat16),
            pltpu.VMEM((FIRST, atoms), jnp.float32),
            pltpu.VMEM((BLOCKS, PLANES * BLOCK, atoms), jnp.bfloat16),
            pltpu.VMEM((BLOCKS, PLANES, BLOCK, F), jnp.bfloat16),
            pltpu.SemaphoreType.DMA,
            pltpu.SemaphoreType.DMA((BLOCKS, 4)),
        ],
        cost_estimate=pl.CostEstimate(
            flops=2 * PLANES * COLUMN * atoms * F, bytes_accessed=atoms * F * 2, transcendentals=0
        ),
        name="factors",
    )(steps, coords, features)


def grid_spots(m0, m1, m2):
    flip = (m2 < 0) | ((m2 == 0) & ((m0 < 0) | ((m0 == 0) & (m1 < 0))))
    m0, m1, m2 = (jnp.where(flip, -m, m) for m in (m0, m1, m2))
    zero, last = m2 == 0, m1 == KMAX
    corner = last & (m0 == KMAX) & (m2 > 0)
    edge = zero & last & (m0 > 0)
    axis = zero & (m0 == 0)
    sheet = zero & (m0 > 0) & (m1 < KMAX)
    rim = last & (m0 < KMAX) & (m2 > 0)
    core = jnp.where(sheet, (m0 - 1) >> 2, (m2 - 1) & 1)
    block = jnp.where(sheet, (m0 - 1) & 3, (m2 - 1) >> 1)
    block = jnp.where(corner, 2, jnp.where(edge, 1, jnp.where(axis, 0, block)))
    core = jnp.where(corner | edge | axis, 0, core)
    peer = jnp.where(rim, m0 + KMAX, m1 + KMAX)
    peer = jnp.where(corner, m2 - 1, jnp.where(edge, m0 - 1, jnp.where(axis, m1, peer)))
    spot = jnp.where(sheet, SIDE, jnp.where(rim, SIDE + 1, m0 + KMAX))
    spot = jnp.where(corner | edge | axis, SIDE + 2, spot)
    return ((core * PLANES + peer) * BLOCKS + block) * OWN + spot


def weights_kernel(miller_ref, weights_ref, out_ref):
    core, atom = lax.axis_index("wave") % 2, lax.axis_index("atom")
    plane, part = atom // 16 * 4 + atom % 4, atom // 4 % 2
    spots = grid_spots(miller_ref[0:1, :], miller_ref[1:2, :], miller_ref[2:3, :])
    row = lax.broadcasted_iota(jnp.int32, (POINTS, miller_ref.shape[1]), 0)
    weights = weights_ref[...]
    upper = weights.astype(jnp.bfloat16)
    lower = (weights - upper.astype(jnp.float32)).astype(jnp.bfloat16)
    for turn, held in enumerate((core, 1 - core)):
        wanted = row + ((held * PLANES + plane) * 2 + part) * POINTS
        match = jnp.where(wanted == spots, 1.0, 0.0).astype(jnp.bfloat16)
        summed = jnp.dot(match, upper, preferred_element_type=jnp.float32)
        summed += jnp.dot(match, lower, preferred_element_type=jnp.float32)
        out_ref[turn * POINTS : (turn + 1) * POINTS, :] = summed.astype(jnp.bfloat16)


def grid_weights(miller, weights):
    return pl.pallas_call(
        weights_kernel,
        out_shape=jax.ShapeDtypeStruct((2 * POINTS, F), jnp.bfloat16),
        in_specs=[pl.BlockSpec(memory_space=pltpu.VMEM)] * 2,
        out_specs=pl.BlockSpec(memory_space=pltpu.VMEM),
        compiler_params=pltpu.CompilerParams(vmem_limit_bytes=8 << 20),
        cost_estimate=pl.CostEstimate(
            flops=8 * POINTS * 512 * F, bytes_accessed=512 * F * 4, transcendentals=0
        ),
        name="grid_weights",
    )(miller, weights)


def plane_sum_kernel(arrived_ref, out_ref):
    for part in TWO:
        rows = pl.ds(part * HALF, HALF)
        total = arrived_ref[0, rows, :].astype(jnp.float32)
        for peer in range(1, PLANES):
            total += arrived_ref[peer, rows, :].astype(jnp.float32)
        sent = total.astype(jnp.bfloat16)
        for peer in (part, part + 2):
            out_ref[peer] = sent


def plane_sum(arrived):
    return pl.pallas_call(
        plane_sum_kernel,
        out_shape=jax.ShapeDtypeStruct((4, HALF, F), jnp.bfloat16),
        in_specs=[pl.BlockSpec(memory_space=pltpu.VMEM)],
        out_specs=pl.BlockSpec(memory_space=pltpu.VMEM),
        compiler_params=pltpu.CompilerParams(vmem_limit_bytes=8 << 20),
        name="plane_sum",
    )(arrived)


def filter_kernel(arrived_ref, near_ref, far_ref, out_ref, total, filtered):
    total[...] = jnp.sum(arrived_ref[...].astype(jnp.float32), axis=0)
    weights = near_ref[...].astype(jnp.float32) + far_ref[...].astype(jnp.float32)
    extra = OWN - SIDE
    for block in range(BLOCKS // 2):
        for row, spot, count in ((0, 0, SIDE), (2 * SIDE, SIDE, extra)):
            start, weight = block * BLOCK + row, block * OWN + spot
            cosines, sines = total[start : start + count, :], total[start + count : start + 2 * count, :]
            power = jnp.sum(cosines * cosines + sines * sines, axis=1, keepdims=True) * (0.5 / F)
            scaled = weights[weight : weight + count] * (1.0 / jnp.sqrt(power + 1e-05))
            filtered[start : start + count, :] = cosines * scaled
            filtered[start + count : start + 2 * count, :] = sines * scaled
    column = filtered[...].astype(jnp.bfloat16)
    for peer in range(PLANES):
        out_ref[peer] = column


def filter_column(arrived, near, far):
    return pl.pallas_call(
        filter_kernel,
        out_shape=jax.ShapeDtypeStruct((PLANES, HALF, F), jnp.bfloat16),
        in_specs=[pl.BlockSpec(memory_space=pltpu.VMEM)] * 3,
        out_specs=pl.BlockSpec(memory_space=pltpu.VMEM),
        scratch_shapes=[pltpu.VMEM((HALF, F), jnp.float32)] * 2,
        compiler_params=pltpu.CompilerParams(vmem_limit_bytes=8 << 20),
        name="filter_column",
    )(arrived, near, far)


def tables_kernel(place_ref, steps_ref, own_ref, near_ref, out_ref):
    steps = steps_ref[0].astype(jnp.bfloat16)
    block = 128
    for side, coords_ref in enumerate((own_ref, near_ref)):
        parts = split_coords(coords_ref[...])
        for start in range(0, TILE, block):
            turns = lax.dot_general(
                parts[:, start : start + block], steps, OUTER, preferred_element_type=jnp.float32
            )
            rows = side * TILE + start
            out_ref[rows : rows + block, :] = cosine_of_turns(turns).astype(jnp.bfloat16)


def message_tables(place, steps, coords, near):
    width = 256
    return pl.pallas_call(
        tables_kernel,
        out_shape=jax.ShapeDtypeStruct((2 * TILE, ALL_ROWS), jnp.bfloat16),
        grid_spec=pltpu.PrefetchScalarGridSpec(
            num_scalar_prefetch=1,
            grid=(ALL_ROWS // width,),
            in_specs=[
                pl.BlockSpec((1, 8, width), lambda t, place: (place[3], 0, t)),
                pl.BlockSpec((3, TILE), lambda t, place: (0, place[2])),
                pl.BlockSpec((3, TILE), lambda t, place: (0, 0)),
            ],
            out_specs=pl.BlockSpec((2 * TILE, width), lambda t, place: (0, t)),
        ),
        compiler_params=pltpu.CompilerParams(vmem_limit_bytes=16 << 20),
        cost_estimate=pl.CostEstimate(
            flops=32 * TILE * ALL_ROWS, bytes_accessed=TILE * ALL_ROWS * 4, transcendentals=0
        ),
        name="message_tables",
    )(place, steps, coords, near)


def message_kernel(tables_ref, filtered_ref, own_ref, other_ref, *, side):
    half = TILE // 2
    core = lax.axis_index("wave") % 2
    filtered = filtered_ref[...]
    for held, out_ref in ((core, own_ref), (1 - core, other_ref)):
        start = pl.multiple_of(held * half, half) + side * TILE
        message = jnp.dot(
            tables_ref[pl.ds(start, half), :], filtered, preferred_element_type=jnp.float32
        )
        out_ref[...] = message.astype(out_ref.dtype)


def message_halves(tables, filtered, side):
    half = TILE // 2
    return pl.pallas_call(
        functools.partial(message_kernel, side=side),
        out_shape=(
            jax.ShapeDtypeStruct((half, F), jnp.bfloat16 if side else jnp.float32),
            jax.ShapeDtypeStruct((half, F), jnp.bfloat16),
        ),
        in_specs=[pl.BlockSpec(memory_space=pltpu.VMEM)] * 2,
        out_specs=(pl.BlockSpec(memory_space=pltpu.VMEM),) * 2,
        compiler_params=pltpu.CompilerParams(vmem_limit_bytes=16 << 20),
        cost_estimate=pl.CostEstimate(
            flops=4 * half * ALL_ROWS * F, bytes_accessed=8 * half * ALL_ROWS, transcendentals=0
        ),
        name="message_far" if side else "message_near",
    )(tables, filtered)


def update_kernel(
    features_ref, own_ref, a_ref, b_ref, c_ref, gain_ref, w_in_ref, w_out_ref, out_ref
):
    gain, w_in, w_out = gain_ref[...], w_in_ref[...], w_out_ref[...]
    half = TILE // 2
    base = pl.multiple_of(lax.axis_index("wave") * half, half)
    chunk = half // 2
    for start in range(0, half, chunk):
        rows = pl.ds(start, chunk)
        message = own_ref[rows, :]
        for part_ref in (a_ref, b_ref, c_ref):
            message += part_ref[rows, :].astype(jnp.float32)
        features = features_ref[pl.ds(base + start, chunk), :].astype(jnp.float32)
        updated = features + message * (1.0 / math.sqrt(K))
        power = jnp.mean(updated * updated, axis=1, keepdims=True)
        normed = (updated / jnp.sqrt(power + 1e-06) * gain).astype(jnp.bfloat16)
        hidden = jnp.dot(normed, w_in, preferred_element_type=jnp.float32)
        hidden = (hidden / (1.0 + jnp.exp(-hidden))).astype(jnp.bfloat16)
        added = jnp.dot(hidden, w_out, preferred_element_type=jnp.float32)
        out_ref[rows, :] = (updated + added).astype(jnp.bfloat16)


def update(features, own, other, far, cross, gain, w_in, w_out):
    return pl.pallas_call(
        update_kernel,
        out_shape=jax.ShapeDtypeStruct((TILE // 2, F), jnp.bfloat16),
        in_specs=[pl.BlockSpec(memory_space=pltpu.VMEM)] * 8,
        out_specs=pl.BlockSpec(memory_space=pltpu.VMEM),
        compiler_params=pltpu.CompilerParams(vmem_limit_bytes=8 << 20),
        name="update",
    )(features, own, other, far, cross, gain, w_in, w_out)


def exchange(pieces, groups):
    return lax.all_to_all(
        pieces, AXES, split_axis=0, concat_axis=0, tiled=True, axis_index_groups=groups
    )


FIRST_STEPS = first_steps()
ALL_STEPS = all_steps()


def layer(features, coords, miller, filter_weights, norm_gain, w_in, w_out):
    factors = partial_factors(jnp.asarray(FIRST_STEPS), coords, features)
    factors, coords, miller = lax.optimization_barrier((factors, coords, miller))
    atom, wave = lax.axis_index("atom"), lax.axis_index("wave")
    core, high = wave % 2, wave // 2
    place = jnp.stack([wave, core, high, core * 2 + atom // 4 % 2]).astype(jnp.int32)
    arrived = exchange(factors, GROUPS_XY)
    weights = grid_weights(miller, filter_weights)
    weights += lax.ppermute(weights, AXES, OUTER_PAIRS)
    far_weights = lax.ppermute(weights, AXES, INNER_PAIRS)
    arrived, weights = lax.optimization_barrier((arrived, weights))
    sums = plane_sum(arrived)
    shares = exchange(sums, GROUPS_LO)
    weights += far_weights
    swapped = lax.ppermute(weights[POINTS:], AXES, SWAP)
    filtered = filter_column(shares, weights[:POINTS], swapped)
    filtered, coords = lax.optimization_barrier((filtered, coords))
    near = lax.dynamic_slice_in_dim(coords, high * TILE, TILE, 1)
    near = lax.ppermute(near, AXES, LINE_SAME)
    filtered = exchange(filtered, GROUPS_XY).reshape(ALL_ROWS, F)
    tables = message_tables(place, jnp.asarray(ALL_STEPS), coords, near)
    far, cross = message_halves(tables, filtered, 1)
    far = lax.ppermute(far, AXES, LINE_SAME)
    cross = lax.ppermute(cross, AXES, LINE_CROSS)
    own, other = message_halves(tables, filtered, 0)
    other = lax.ppermute(other, AXES, SWAP)
    gain = norm_gain.reshape(1, F)
    return update(features, own, other, far, cross, gain, w_in, w_out)


def solution(mesh):
    in_specs = (P("atom", None), P(None, "atom"), P(None, "wave"), P("wave", None), P(), P(), P())
    out_specs = P(("atom", "wave"), None)
    return jax.shard_map(layer, mesh=mesh, in_specs=in_specs, out_specs=out_specs, check_vma=False)
```

```python
import itertools
import math

import jax
import jax.numpy as jnp
import numpy as np
from jax import lax
from jax.experimental import pallas as pl
from jax.experimental.pallas import tpu as pltpu
from jax.sharding import PartitionSpec as P

K = 4096
KMAX = 8
SIDE = 2 * KMAX + 1
PLANES = 16
BLOCKS = 4
OWN = 20
BLOCK = 2 * OWN
COLUMN = BLOCKS * BLOCK
HALF = COLUMN // 2
ALL_ROWS = PLANES * HALF
MIDDLE = 8
POINTS = BLOCKS * OWN // 2
F = 256
HALVES = 256
TILE = 512
AXES = ("atom", "wave")
OUTER = (((0,), (0,)), ((), ()))


def device(y, z_lo, x, z_hi, core):
    return (((y * 4 + z_lo) * 4 + x) * 4 + z_hi) * 2 + core


FOUR = range(4)
TWO = range(2)
GROUPS_XY = [
    [device(y, l, x, h, c) for y in FOUR for x in FOUR] for l in FOUR for h in FOUR for c in TWO
]
GROUPS_LO = [
    [device(y, l, x, h, c) for l in FOUR] for y in FOUR for x in FOUR for h in FOUR for c in TWO
]
SWAP = [
    (device(y, l, x, h, c), device(y, l, x, h, 1 - c))
    for y, l, x, h, c in itertools.product(FOUR, FOUR, FOUR, FOUR, TWO)
]
OUTER_PAIRS = [
    (device(y, l, x, h, c), device(y, l, x, 3 - h, c))
    for y, l, x, h, c in itertools.product(FOUR, FOUR, FOUR, FOUR, TWO)
]
INNER_PAIRS = [
    (device(y, l, x, h, c), device(y, l, x, h ^ 1, c))
    for y, l, x, h, c in itertools.product(FOUR, FOUR, FOUR, FOUR, TWO)
]


LINE_SAME = [
    (device(y, l, x, h, c), device(y, l ^ 1, x, h, c))
    for y, l, x, h, c in itertools.product(FOUR, FOUR, FOUR, FOUR, TWO)
]
LINE_CROSS = [
    (device(y, l, x, h, c), device(y, l ^ 1, x, h, 1 - c))
    for y, l, x, h, c in itertools.product(FOUR, FOUR, FOUR, FOUR, TWO)
]


def row_line(core, block, spot):
    third = 2 * block + core + 1
    if spot < SIDE:
        return (spot - KMAX, 0, third), 1
    if spot == SIDE:
        return (4 * core + block + 1, 0, 0), 1
    if spot == SIDE + 1:
        return (0, KMAX, third), 0
    if (core, block) == (0, 0):
        return (0, MIDDLE, 0), 1
    if (core, block) == (0, 1):
        return (MIDDLE + 1, KMAX, 0), 0
    if (core, block) == (0, 2):
        return (KMAX, KMAX, MIDDLE + 1), 2
    return None


def column_of(vector, part):
    steps = np.zeros(8, np.float32)
    steps[0:3] = vector
    steps[3:6] = vector
    steps[6] = -0.25 * part
    return steps


def spot_of(row):
    if row < 2 * SIDE:
        return row % SIDE, row // SIDE
    extra = OWN - SIDE
    return SIDE + (row - 2 * SIDE) % extra, (row - 2 * SIDE) // extra


def row_steps(core, block, row, peer):
    spot, part = spot_of(row)
    line = row_line(core, block, spot)
    if line is None:
        return column_of((0, 0, 0), 1)
    vector = list(line[0])
    vector[line[1]] += peer - MIDDLE
    return column_of(vector, part)


def stride_steps(core, block, row):
    line = row_line(core, block, spot_of(row)[0])
    vector = [0, 0, 0]
    vector[1 if line is None else line[1]] = 1
    return column_of(vector, 0)


MAIN = 32
MIXED = range(MAIN, BLOCK)
AT = [0, 2 * BLOCK, 4 * BLOCK, 4 * BLOCK + 16]
STRIDES = 4 * BLOCK + 32
THIRD = STRIDES + 8 * BLOCKS
FIRST = THIRD + 8


def first_steps():
    out = np.zeros((2, 8, FIRST), np.float32)
    for core in range(2):
        columns = []
        for block in range(BLOCKS):
            rows = range(BLOCK) if block < 2 else MIXED
            columns += [row_steps(core, block, row, MIDDLE) for row in rows]
            columns += [row_steps(core, block, row, MIDDLE + 1) for row in rows]
        for block in range(BLOCKS):
            columns += [stride_steps(core, block, row) for row in MIXED]
        columns += [column_of((0, 0, 2), 0)] * 8
        out[core] = np.stack(columns, axis=1)
    return out


def all_steps():
    out = []
    for core, part in itertools.product(TWO, TWO):
        rows = itertools.product(range(PLANES), (2 * part, 2 * part + 1), range(BLOCK))
        out.append(np.stack([row_steps(core, b, r, q) for q, b, r in rows], axis=1))
    return np.stack(out)


def split_coords(coords):
    high = (coords >> 8).astype(jnp.float32) * (1.0 / 256.0)
    low = (coords & 255).astype(jnp.float32) * (1.0 / 65536.0)
    ones = jnp.ones((2, coords.shape[1]), jnp.float32)
    return jnp.concatenate([high, low, ones], axis=0).astype(jnp.bfloat16)


def cosine_coefficients():
    nodes = 0.125 + 0.125 * np.cos(np.pi * (np.arange(400) + 0.5) / 400)
    fit = np.polynomial.chebyshev.Chebyshev.fit(
        nodes, np.cos(2 * np.pi * np.sqrt(nodes)), 5, domain=[0, 0.25]
    )
    return [float(c) for c in fit.convert(kind=np.polynomial.Polynomial).coef]


COSINE = cosine_coefficients()


def cosine_of_turns(turns):
    left = turns - jnp.round(turns)
    square = left * left
    total = jnp.full_like(square, COSINE[-1])
    for c in COSINE[-2::-1]:
        total = total * square + c
    return total


def factors_kernel(
    steps_ref, coords_ref, features_ref, out_ref, features, first, tables, made, copied, sent
):
    copy = pltpu.make_async_copy(features_ref, features, copied)
    copy.start()
    core = lax.axis_index("wave") % 2
    steps = steps_ref[core].astype(jnp.bfloat16)
    atoms = coords_ref.shape[1]
    for start in range(0, atoms, TILE):
        parts = split_coords(coords_ref[:, start : start + TILE])
        turns = lax.dot_general(steps, parts, OUTER, preferred_element_type=jnp.float32)
        first[:, start : start + TILE] = cosine_of_turns(turns)
    mains, sends = {}, []
    for block in range(BLOCKS):
        for start in range(0, atoms, HALVES):
            lanes = pl.ds(start, HALVES)
            if block < 2:
                at = first[AT[block] : AT[block] + BLOCK, lanes]
                after = first[AT[block] + BLOCK : AT[block] + 2 * BLOCK, lanes]
            else:
                third = 2.0 * first[THIRD : THIRD + 1, lanes]
                main = [
                    third * near - far
                    for near, far in zip(mains[block - 1, start], mains[block - 2, start])
                ]
                mixed = [first[AT[block] + 8 * p : AT[block] + 8 * p + 8, lanes] for p in TWO]
                at, after = (jnp.concatenate([main[p], mixed[p]], axis=0) for p in TWO)
            mains[block, start] = at[:MAIN], after[:MAIN]
            mixed = 2.0 * first[STRIDES + 8 * block : STRIDES + 8 * block + 8, lanes]
            common = jnp.broadcast_to(mixed[0:1, :], (MAIN, HALVES))
            stride = jnp.concatenate([common, mixed], axis=0)
            held = {MIDDLE: at, MIDDLE + 1: after}
            for peer in range(MIDDLE, PLANES, 2):
                for later in (peer, peer + 1):
                    if later not in held:
                        held[later] = stride * held[later - 1] - held[later - 2]
                pair = jnp.concatenate([held[peer], held[peer + 1]], axis=0)
                tables[block, peer * BLOCK : (peer + 2) * BLOCK, lanes] = pair.astype(jnp.bfloat16)
            for peer in range(MIDDLE - 2, -1, -2):
                for earlier in (peer + 1, peer):
                    held[earlier] = stride * held[earlier + 1] - held[earlier + 2]
                pair = jnp.concatenate([held[peer], held[peer + 1]], axis=0)
                tables[block, peer * BLOCK : (peer + 2) * BLOCK, lanes] = pair.astype(jnp.bfloat16)
        if block == 0:
            copy.wait()
        summed = jnp.dot(tables[block], features[...], preferred_element_type=jnp.float32)
        for peer in range(PLANES):
            piece = summed[peer * BLOCK : (peer + 1) * BLOCK, :].astype(jnp.bfloat16)
            made[block, peer] = piece
        for group in range(4):
            sends.append(
                pltpu.make_async_copy(
                    made.at[block, pl.ds(4 * group, 4)],
                    out_ref.at[pl.ds(4 * group, 4), pl.ds(block * BLOCK, BLOCK), :],
                    sent.at[block, group],
                )
            )
            sends[-1].start()
    for send in sends:
        send.wait()


def partial_factors(steps, coords, features):
    atoms = features.shape[0]
    return pl.pallas_call(
        factors_kernel,
        out_shape=jax.ShapeDtypeStruct((PLANES, COLUMN, F), jnp.bfloat16),
        in_specs=[
            pl.BlockSpec(memory_space=pltpu.VMEM),
            pl.BlockSpec(memory_space=pltpu.VMEM),
            pl.BlockSpec(memory_space=pl.ANY),
        ],
        out_specs=pl.BlockSpec(memory_space=pl.ANY),
        scratch_shapes=[
            pltpu.VMEM((atoms, F), jnp.bfloat16),
            pltpu.VMEM((FIRST, atoms), jnp.float32),
            pltpu.VMEM((BLOCKS, PLANES * BLOCK, atoms), jnp.bfloat16),
            pltpu.VMEM((BLOCKS, PLANES, BLOCK, F), jnp.bfloat16),
            pltpu.SemaphoreType.DMA,
            pltpu.SemaphoreType.DMA((BLOCKS, 4)),
        ],
        cost_estimate=pl.CostEstimate(
            flops=2 * PLANES * COLUMN * atoms * F, bytes_accessed=atoms * F * 2, transcendentals=0
        ),
        name="factors",
    )(steps, coords, features)


def grid_spots(m0, m1, m2):
    flip = (m2 < 0) | ((m2 == 0) & ((m0 < 0) | ((m0 == 0) & (m1 < 0))))
    m0, m1, m2 = (jnp.where(flip, -m, m) for m in (m0, m1, m2))
    zero, last = m2 == 0, m1 == KMAX
    corner = last & (m0 == KMAX) & (m2 > 0)
    edge = zero & last & (m0 > 0)
    axis = zero & (m0 == 0)
    sheet = zero & (m0 > 0) & (m1 < KMAX)
    rim = last & (m0 < KMAX) & (m2 > 0)
    core = jnp.where(sheet, (m0 - 1) >> 2, (m2 - 1) & 1)
    block = jnp.where(sheet, (m0 - 1) & 3, (m2 - 1) >> 1)
    block = jnp.where(corner, 2, jnp.where(edge, 1, jnp.where(axis, 0, block)))
    core = jnp.where(corner | edge | axis, 0, core)
    peer = jnp.where(rim, m0 + KMAX, m1 + KMAX)
    peer = jnp.where(corner, m2 - 1, jnp.where(edge, m0 - 1, jnp.where(axis, m1, peer)))
    spot = jnp.where(sheet, SIDE, jnp.where(rim, SIDE + 1, m0 + KMAX))
    spot = jnp.where(corner | edge | axis, SIDE + 2, spot)
    return ((core * PLANES + peer) * BLOCKS + block) * OWN + spot


def weights_kernel(miller_ref, weights_ref, out_ref):
    core, atom = lax.axis_index("wave") % 2, lax.axis_index("atom")
    plane, part = atom // 16 * 4 + atom % 4, atom // 4 % 2
    spots = grid_spots(miller_ref[0:1, :], miller_ref[1:2, :], miller_ref[2:3, :])
    row = lax.broadcasted_iota(jnp.int32, (POINTS, miller_ref.shape[1]), 0)
    weights = weights_ref[...]
    upper = weights.astype(jnp.bfloat16)
    lower = (weights - upper.astype(jnp.float32)).astype(jnp.bfloat16)
    for turn, held in enumerate((core, 1 - core)):
        wanted = row + ((held * PLANES + plane) * 2 + part) * POINTS
        match = jnp.where(wanted == spots, 1.0, 0.0).astype(jnp.bfloat16)
        summed = jnp.dot(match, upper, preferred_element_type=jnp.float32)
        summed += jnp.dot(match, lower, preferred_element_type=jnp.float32)
        out_ref[turn * POINTS : (turn + 1) * POINTS, :] = summed.astype(jnp.bfloat16)


def grid_weights(miller, weights):
    return pl.pallas_call(
        weights_kernel,
        out_shape=jax.ShapeDtypeStruct((2 * POINTS, F), jnp.bfloat16),
        in_specs=[pl.BlockSpec(memory_space=pltpu.VMEM)] * 2,
        out_specs=pl.BlockSpec(memory_space=pltpu.VMEM),
        compiler_params=pltpu.CompilerParams(vmem_limit_bytes=8 << 20),
        cost_estimate=pl.CostEstimate(
            flops=8 * POINTS * 512 * F, bytes_accessed=512 * F * 4, transcendentals=0
        ),
        name="grid_weights",
    )(miller, weights)


def plane_sum_kernel(arrived_ref, out_ref):
    for part in TWO:
        rows = pl.ds(part * HALF, HALF)
        total = arrived_ref[0, rows, :].astype(jnp.float32)
        for peer in range(1, PLANES):
            total += arrived_ref[peer, rows, :].astype(jnp.float32)
        sent = total.astype(jnp.bfloat16)
        for peer in (part, part + 2):
            out_ref[peer] = sent


def plane_sum(arrived):
    return pl.pallas_call(
        plane_sum_kernel,
        out_shape=jax.ShapeDtypeStruct((4, HALF, F), jnp.bfloat16),
        in_specs=[pl.BlockSpec(memory_space=pltpu.VMEM)],
        out_specs=pl.BlockSpec(memory_space=pltpu.VMEM),
        compiler_params=pltpu.CompilerParams(vmem_limit_bytes=8 << 20),
        name="plane_sum",
    )(arrived)


def filter_kernel(arrived_ref, near_ref, far_ref, out_ref, total, filtered):
    total[...] = jnp.sum(arrived_ref[...].astype(jnp.float32), axis=0)
    weights = near_ref[...].astype(jnp.float32) + far_ref[...].astype(jnp.float32)
    extra = OWN - SIDE
    for block in range(BLOCKS // 2):
        for row, spot, count in ((0, 0, SIDE), (2 * SIDE, SIDE, extra)):
            start, weight = block * BLOCK + row, block * OWN + spot
            cosines, sines = total[start : start + count, :], total[start + count : start + 2 * count, :]
            power = jnp.sum(cosines * cosines + sines * sines, axis=1, keepdims=True) * (0.5 / F)
            scaled = weights[weight : weight + count] * (1.0 / jnp.sqrt(power + 1e-05))
            filtered[start : start + count, :] = cosines * scaled
            filtered[start + count : start + 2 * count, :] = sines * scaled
    column = filtered[...].astype(jnp.bfloat16)
    for peer in range(PLANES):
        out_ref[peer] = column


def filter_column(arrived, near, far):
    return pl.pallas_call(
        filter_kernel,
        out_shape=jax.ShapeDtypeStruct((PLANES, HALF, F), jnp.bfloat16),
        in_specs=[pl.BlockSpec(memory_space=pltpu.VMEM)] * 3,
        out_specs=pl.BlockSpec(memory_space=pltpu.VMEM),
        scratch_shapes=[pltpu.VMEM((HALF, F), jnp.float32)] * 2,
        compiler_params=pltpu.CompilerParams(vmem_limit_bytes=8 << 20),
        name="filter_column",
    )(arrived, near, far)


def tables_kernel(place_ref, steps_ref, coords_ref, out_ref):
    steps = steps_ref[0].astype(jnp.bfloat16)
    parts = split_coords(coords_ref[...])
    block = 128
    for start in range(0, TILE, block):
        turns = lax.dot_general(
            parts[:, start : start + block], steps, OUTER, preferred_element_type=jnp.float32
        )
        out_ref[start : start + block, :] = cosine_of_turns(turns).astype(jnp.bfloat16)


def message_tables(place, steps, coords):
    width = 256
    return pl.pallas_call(
        tables_kernel,
        out_shape=jax.ShapeDtypeStruct((TILE, ALL_ROWS), jnp.bfloat16),
        grid_spec=pltpu.PrefetchScalarGridSpec(
            num_scalar_prefetch=1,
            grid=(ALL_ROWS // width,),
            in_specs=[
                pl.BlockSpec((1, 8, width), lambda t, place: (place[0], 0, t)),
                pl.BlockSpec((3, TILE), lambda t, place: (0, 0)),
            ],
            out_specs=pl.BlockSpec((TILE, width), lambda t, place: (0, t)),
        ),
        compiler_params=pltpu.CompilerParams(vmem_limit_bytes=16 << 20),
        cost_estimate=pl.CostEstimate(
            flops=600 * TILE * ALL_ROWS, bytes_accessed=TILE * ALL_ROWS * 2, transcendentals=0
        ),
    )(place, steps, coords)


def message_kernel(tables_ref, filtered_ref, own_ref, other_ref):
    half = TILE // 2
    core = lax.axis_index("wave") % 2
    filtered = filtered_ref[...]
    for held, out_ref in ((core, own_ref), (1 - core, other_ref)):
        start = pl.multiple_of(held * half, half)
        message = jnp.dot(
            tables_ref[pl.ds(start, half), :], filtered, preferred_element_type=jnp.float32
        )
        out_ref[...] = message.astype(out_ref.dtype)


def message_halves(tables, filtered, side):
    half = TILE // 2
    return pl.pallas_call(
        message_kernel,
        out_shape=(
            jax.ShapeDtypeStruct((half, F), jnp.bfloat16 if side else jnp.float32),
            jax.ShapeDtypeStruct((half, F), jnp.bfloat16),
        ),
        in_specs=[pl.BlockSpec(memory_space=pltpu.VMEM)] * 2,
        out_specs=(pl.BlockSpec(memory_space=pltpu.VMEM),) * 2,
        compiler_params=pltpu.CompilerParams(vmem_limit_bytes=16 << 20),
        cost_estimate=pl.CostEstimate(
            flops=4 * half * ALL_ROWS * F, bytes_accessed=8 * half * ALL_ROWS, transcendentals=0
        ),
        name="message_far" if side else "message_near",
    )(tables, filtered)


def update_kernel(
    features_ref, own_ref, a_ref, b_ref, c_ref, gain_ref, w_in_ref, w_out_ref, out_ref
):
    gain, w_in, w_out = gain_ref[...], w_in_ref[...], w_out_ref[...]
    half = TILE // 2
    base = pl.multiple_of(lax.axis_index("wave") * half, half)
    chunk = half // 2
    for start in range(0, half, chunk):
        rows = pl.ds(start, chunk)
        message = own_ref[rows, :]
        for part_ref in (a_ref, b_ref, c_ref):
            message += part_ref[rows, :].astype(jnp.float32)
        features = features_ref[pl.ds(base + start, chunk), :].astype(jnp.float32)
        updated = features + message * (1.0 / math.sqrt(K))
        power = jnp.mean(updated * updated, axis=1, keepdims=True)
        normed = (updated / jnp.sqrt(power + 1e-06) * gain).astype(jnp.bfloat16)
        hidden = jnp.dot(normed, w_in, preferred_element_type=jnp.float32)
        hidden = (hidden / (1.0 + jnp.exp(-hidden))).astype(jnp.bfloat16)
        added = jnp.dot(hidden, w_out, preferred_element_type=jnp.float32)
        out_ref[rows, :] = (updated + added).astype(jnp.bfloat16)


def update(features, own, other, far, cross, gain, w_in, w_out):
    return pl.pallas_call(
        update_kernel,
        out_shape=jax.ShapeDtypeStruct((TILE // 2, F), jnp.bfloat16),
        in_specs=[pl.BlockSpec(memory_space=pltpu.VMEM)] * 8,
        out_specs=pl.BlockSpec(memory_space=pltpu.VMEM),
        compiler_params=pltpu.CompilerParams(vmem_limit_bytes=8 << 20),
        name="update",
    )(features, own, other, far, cross, gain, w_in, w_out)


def exchange(pieces, groups):
    return lax.all_to_all(
        pieces, AXES, split_axis=0, concat_axis=0, tiled=True, axis_index_groups=groups
    )


FIRST_STEPS = first_steps()
ALL_STEPS = all_steps()


def layer(features, coords, miller, filter_weights, norm_gain, w_in, w_out):
    factors = partial_factors(jnp.asarray(FIRST_STEPS), coords, features)
    factors, coords, miller = lax.optimization_barrier((factors, coords, miller))
    atom, wave = lax.axis_index("atom"), lax.axis_index("wave")
    core, high = wave % 2, wave // 2
    place = jnp.reshape(core * 2 + atom // 4 % 2, (1,)).astype(jnp.int32)
    arrived = exchange(factors, GROUPS_XY)
    weights = grid_weights(miller, filter_weights)
    weights += lax.ppermute(weights, AXES, OUTER_PAIRS)
    far_weights = lax.ppermute(weights, AXES, INNER_PAIRS)
    arrived, weights = lax.optimization_barrier((arrived, weights))
    sums = plane_sum(arrived)
    shares = exchange(sums, GROUPS_LO)
    weights += far_weights
    swapped = lax.ppermute(weights[POINTS:], AXES, SWAP)
    filtered = filter_column(shares, weights[:POINTS], swapped)
    filtered, coords = lax.optimization_barrier((filtered, coords))
    mine = lax.dynamic_slice_in_dim(coords, high * TILE, TILE, 1)
    near = lax.ppermute(mine, AXES, LINE_SAME)
    filtered = exchange(filtered, GROUPS_XY).reshape(ALL_ROWS, F)
    steps = jnp.asarray(ALL_STEPS)
    own_tables = message_tables(place, steps, mine)
    near_tables = message_tables(place, steps, near)
    far, cross = message_halves(near_tables, filtered, 1)
    far = lax.ppermute(far, AXES, LINE_SAME)
    cross = lax.ppermute(cross, AXES, LINE_CROSS)
    own, other = message_halves(own_tables, filtered, 0)
    other = lax.ppermute(other, AXES, SWAP)
    gain = norm_gain.reshape(1, F)
    return update(features, own, other, far, cross, gain, w_in, w_out)


def solution(mesh):
    in_specs = (P("atom", None), P(None, "atom"), P(None, "wave"), P("wave", None), P(), P(), P())
    out_specs = P(("atom", "wave"), None)
    return jax.shard_map(layer, mesh=mesh, in_specs=in_specs, out_specs=out_specs, check_vma=False)
```
